128 devices in a mesh: dp: 16 (over x, y), expert: 8 (over z, core).
Axes of the slice: x: 4, y: 4, z: 4, core: 2. Of those that a mesh axis runs over, the one named last changes fastest.
Arguments:
- tokens: bfloat16 [32768, 1024], P(('dp', 'expert')), may hold values from -6 to 6
- cotangent: bfloat16 [32768, 1024], P(('dp', 'expert')), may hold values from -6 to 6
- segments: int32 [16, 2048], P('dp', 'expert'), may hold values from 0 to 15, never falling along the last dimension, each value on 1 to 1024 neighbouring positions
- routes: int32 [16, 2048], P('dp', 'expert'), may hold values from 0 to 7, as said below
- attngain: bfloat16 [1024], replicated, may hold values from 0.5 to 1.5
- attnshift: bfloat16 [1024], replicated, may hold values from -0.59765625 to 0.59765625
- querymat: bfloat16 [1024, 1024], replicated, may hold values from -0.25 to 0.25
- querybias: bfloat16 [1024], replicated, may hold values from -0.59765625 to 0.59765625
- keymat: bfloat16 [1024, 1024], replicated, may hold values from -0.25 to 0.25
- valuemat: bfloat16 [1024, 1024], replicated, may hold values from -0.1875 to 0.1875
- valuebias: bfloat16 [1024], replicated, may hold values from -0.59765625 to 0.59765625
- outmat: bfloat16 [1024, 1024], replicated, may hold values from -0.75 to 0.75
- outbias: bfloat16 [1024], replicated, may hold values from -0.59765625 to 0.59765625
- frontgain: bfloat16 [8, 1024], P('expert', 'dp'), may hold values from 0.5 to 1.5
- frontshift: bfloat16 [8, 1024], P('expert', 'dp'), may hold values from -0.59765625 to 0.59765625
- frontexpand: bfloat16 [8, 1024, 4096], P('expert', None, 'dp'), may hold values from -0.1875 to 0.1875
- frontlift: bfloat16 [8, 4096], P('expert', 'dp'), may hold values from -0.59765625 to 0.59765625
- frontreduce: bfloat16 [8, 4096, 1024], P('expert', 'dp'), may hold values from -0.125 to 0.125
- frontoffset: bfloat16 [8, 1024], P('expert', 'dp'), may hold values from -0.59765625 to 0.59765625
- backgain: bfloat16 [8, 1024], P('expert', 'dp'), may hold values from 0.5 to 1.5
- backshift: bfloat16 [8, 1024], P('expert', 'dp'), may hold values from -0.59765625 to 0.59765625
- backexpand: bfloat16 [8, 1024, 4096], P('expert', None, 'dp'), may hold values from -0.1875 to 0.1875
- backlift: bfloat16 [8, 4096], P('expert', 'dp'), may hold values from -0.59765625 to 0.59765625
- backreduce: bfloat16 [8, 4096, 1024], P('expert', 'dp'), may hold values from -0.125 to 0.125
- backoffset: bfloat16 [8, 1024], P('expert', 'dp'), may hold values from -0.59765625 to 0.59765625
- centroid: bfloat16 [8, 1024], P('expert', 'dp'), may hold values from -0.125 to 0.125
Outputs:
- result: bfloat16 [32768, 1024], P(('dp', 'expert'))
- tokens_grad: float32 [32768, 1024], P(('dp', 'expert'))
- attngain_grad: float32 [1024], replicated
- attnshift_grad: float32 [1024], replicated
- querymat_grad: float32 [1024, 1024], replicated
- querybias_grad: float32 [1024], replicated
- keymat_grad: float32 [1024, 1024], replicated
- valuemat_grad: float32 [1024, 1024], replicated
- valuebias_grad: float32 [1024], replicated
- outmat_grad: float32 [1024, 1024], replicated
- outbias_grad: float32 [1024], replicated
- frontgain_grad: float32 [8, 1024], P('expert', 'dp')
- frontshift_grad: float32 [8, 1024], P('expert', 'dp')
- frontexpand_grad: float32 [8, 1024, 4096], P('expert', None, 'dp')
- frontlift_grad: float32 [8, 4096], P('expert', 'dp')
- frontreduce_grad: float32 [8, 4096, 1024], P('expert', 'dp')
- frontoffset_grad: float32 [8, 1024], P('expert', 'dp')
- backgain_grad: float32 [8, 1024], P('expert', 'dp')
- backshift_grad: float32 [8, 1024], P('expert', 'dp')
- backexpand_grad: float32 [8, 1024, 4096], P('expert', None, 'dp')
- backlift_grad: float32 [8, 4096], P('expert', 'dp')
- backreduce_grad: float32 [8, 4096, 1024], P('expert', 'dp')
- backoffset_grad: float32 [8, 1024], P('expert', 'dp')
- centroid_grad: float32 [8, 1024], P('expert', 'dp')
The draws below stay inside these ranges and needn't reach their ends.
Inputs may be any that keep to these rules, and one draw needn't show every extreme that they name: `routes`: every expert gets exactly 256 tokens of each sequence. Among the 256 tokens of one device (tokens d * 256 to (d + 1) * 256 - 1 of a sequence), one expert gets exactly 48, one other gets 2 * 32 - 48, and each remaining expert 256 // 8; which experts and which tokens vary.
All inputs are finite; a program needn't handle non-finite values.
Results may differ from the reference program's by a relative error of at most 0.018.
Values may be sent and summed in bfloat16 or wider, within the bound.
No kernel may reach another device: no remote copies, remote signals or barrier semaphores. Data moves between devices by JAX's collectives and lax.ppermute only.
A program may use at most 256 MiB of HBM per device.

```python
import math
import jax
import jax.numpy as jnp
import numpy as np
from jax import lax

D = 1024
HEADS = 16
HEAD_DIM = 64
FF = 4096
TOK_DEV = 256
EXPERTS = 8
SEQS = 16
LENGTH = 2048
TOKENS = 32768


def draw_routes(key, part):
    base_count = TOK_DEV // EXPERTS
    extra_count = TOK_DEV // (2 * EXPERTS)

    def one_group(group_key):
        leading = jax.random.permutation(jax.random.fold_in(group_key, 1), EXPERTS)
        following = jnp.roll(leading, -1)
        expert_ids = jnp.arange(EXPERTS)
        counts = base_count + extra_count * (expert_ids[None, :] == leading[:, None]).astype(jnp.int32) - extra_count * (expert_ids[None, :] == following[:, None]).astype(jnp.int32)
        bounds = jnp.cumsum(counts, axis=1)
        slot_ids = jnp.arange(TOK_DEV)
        labels = jnp.sum((bounds[:, None, :] <= slot_ids[None, :, None]).astype(jnp.int32), -1)
        device_keys = jax.random.split(jax.random.fold_in(group_key, 2), EXPERTS)
        shuffled = jax.vmap(lambda dev_key, label_row: label_row[jax.random.permutation(dev_key, TOK_DEV)])(device_keys, labels)
        return shuffled.reshape(LENGTH)
    group_keys = jax.random.split(jax.random.fold_in(key, 7), SEQS)
    return jax.vmap(one_group)(group_keys).astype(jnp.int32)


def steps_of(rng, dims, shards, smallest, high):
    level = 1.0
    for axis_at, shards_of in shards:
        heights = jax.random.uniform(jax.random.fold_in(jax.random.fold_in(rng, 6), axis_at), (shards_of,), jnp.float32, smallest / len(shards), high / len(shards))
        level = level * jnp.repeat(jnp.exp(heights), dims[axis_at] // shards_of).reshape((-1,) + (1,) * (len(dims) - 1 - axis_at))
    return level


def profile(count, total, limit, skew):
    weights = [(1 << 20) // math.isqrt(standing ** skew) + 1 for standing in range(2, count + 1)]
    spare, holding = total - limit - (count - 1), [1] * (count - 1)
    while spare > 0:
        candidates = [i for i in range(count - 1) if holding[i] < limit]
        mass, remaining = sum([weights[i] for i in candidates]), spare
        for i in candidates:
            extra = min(limit - holding[i], max(1, remaining * weights[i] // mass), spare)
            holding[i] = holding[i] + extra
            spare = spare - extra
    return np.array([limit] + holding)


def ragged(own_key, count, total, limit, slope):
    if count == 2:
        one = jax.random.randint(own_key, (), max(1, total - limit), min(limit, total - 1) + 1)
        return jnp.stack([one, total - one])
    tallies = jnp.asarray(profile(count, total, limit, slope), jnp.int32)
    pairs = (count - 1) // 2
    source_of, sink = tallies[1:1 + 2 * pairs:2], tallies[2:2 + 2 * pairs:2]
    slack = jnp.minimum(source_of - 1, limit - sink)
    moved = jax.random.randint(jax.random.fold_in(own_key, 1), (pairs,), 0, 1 << 20) % (slack + 1)
    tallies = tallies.at[1:1 + 2 * pairs:2].set(source_of - moved).at[2:2 + 2 * pairs:2].set(sink + moved)
    return tallies[jax.random.permutation(jax.random.fold_in(own_key, 2), count)]


def normal_values(key, extent, scale, bound, shards=(), dtype=jnp.bfloat16):
    factor_of = steps_of(key, extent, shards, -0.22, 0.18) if shards else 1.0
    drawn = jax.random.normal(key, extent, jnp.float32) * scale * factor_of
    return jnp.minimum(jnp.maximum(drawn, -bound), bound).astype(dtype)


def setup_inputs(seed: int = 0) -> dict:
    key_of = jax.random.split(jax.random.key(seed), 27)
    return {
        "tokens": normal_values(key_of[0], (TOKENS, D), 1.0, 6.0, ((0, 128),)),
        "cotangent": normal_values(key_of[1], (TOKENS, D), 1.0, 6.0, ((0, 128),)),
        "segments": jax.vmap(lambda own: jnp.searchsorted(jnp.cumsum(ragged(own, 16, LENGTH, LENGTH // 2, 2)), jnp.arange(LENGTH), side="right"))(jax.random.split(key_of[2], SEQS)).reshape((SEQS, LENGTH)).astype(jnp.int32),
        "routes": draw_routes(jax.random.fold_in(key_of[26], 71), 0),
        "attngain": jnp.clip(1.0 + 0.1 * jax.random.normal(key_of[4], (D,), jnp.float32), 0.5, 1.5).astype(jnp.bfloat16),
        "attnshift": normal_values(key_of[5], (D,), 0.1, 0.59765625),
        "querymat": normal_values(key_of[6], (D, D), (D // 2) ** -0.5, 0.25),
        "querybias": normal_values(key_of[7], (D,), 0.1, 0.59765625),
        "keymat": normal_values(key_of[8], (D, D), (D // 2) ** -0.5, 0.25),
        "valuemat": normal_values(key_of[9], (D, D), D ** -0.5, 0.1875),
        "valuebias": normal_values(key_of[10], (D,), 0.1, 0.59765625),
        "outmat": normal_values(key_of[11], (D, D), (D // 16) ** -0.5, 0.75),
        "outbias": normal_values(key_of[12], (D,), 0.1, 0.59765625),
        "frontgain": jnp.clip(1.0 + 0.1 * jax.random.normal(key_of[13], (EXPERTS, D), jnp.float32), 0.5, 1.5).astype(jnp.bfloat16),
        "frontshift": normal_values(key_of[14], (EXPERTS, D), 0.1, 0.59765625, ((0, 8), (1, 16))),
        "frontexpand": normal_values(key_of[15], (EXPERTS, D, FF), D ** -0.5, 0.1875, ((0, 8), (2, 16))),
        "frontlift": normal_values(key_of[16], (EXPERTS, FF), 0.1, 0.59765625, ((0, 8), (1, 16))),
        "frontreduce": normal_values(key_of[17], (EXPERTS, FF, D), (FF // 2) ** -0.5, 0.125, ((0, 8), (1, 16))),
        "frontoffset": normal_values(key_of[18], (EXPERTS, D), 0.1, 0.59765625, ((0, 8), (1, 16))),
        "backgain": jnp.clip(1.0 + 0.1 * jax.random.normal(key_of[19], (EXPERTS, D), jnp.float32), 0.5, 1.5).astype(jnp.bfloat16),
        "backshift": normal_values(key_of[20], (EXPERTS, D), 0.1, 0.59765625, ((0, 8), (1, 16))),
        "backexpand": normal_values(key_of[21], (EXPERTS, D, FF), D ** -0.5, 0.1875, ((0, 8), (2, 16))),
        "backlift": normal_values(key_of[22], (EXPERTS, FF), 0.1, 0.59765625, ((0, 8), (1, 16))),
        "backreduce": normal_values(key_of[23], (EXPERTS, FF, D), (FF // 2) ** -0.5, 0.125, ((0, 8), (1, 16))),
        "backoffset": normal_values(key_of[24], (EXPERTS, D), 0.1, 0.59765625, ((0, 8), (1, 16))),
        "centroid": normal_values(key_of[25], (EXPERTS, D), (2 * D) ** -0.5, 0.125, ((0, 8), (1, 16))),
    }


@jax.custom_vjp
def low(v):
    return lax.optimization_barrier(v.astype(jnp.bfloat16)).astype(jnp.float32)

@jax.custom_vjp
def low_back(v):
    return v

def low_keep(v):
    return (low(v), None)

def low_pass(kept, grad):
    return (grad,)

def back_keep(v):
    return (v, None)

def back_low(kept, grad):
    return (low(grad),)
low.defvjp(low_keep, low_pass)
low_back.defvjp(back_keep, back_low)
epsilon = 1e-05
highest = lax.Precision.HIGHEST

def norm_rows(stream, gain_vec, shift_vec):
    center = stream - lax.optimization_barrier(jnp.mean(stream, -1, keepdims=True))
    variance = lax.optimization_barrier(jnp.mean(center * center, -1, keepdims=True))
    return center * lax.rsqrt(variance + epsilon) * gain_vec + shift_vec

def attend_sequence(stream, seg_row, params):
    gain_vec, shift_vec, query_w, query_b, key_w, value_w, value_b, out_w, out_b = params
    normed = low(norm_rows(stream, gain_vec, shift_vec))
    queries = low(low_back(jnp.dot(normed, query_w, precision=highest) + query_b))
    keys_all = low(low_back(jnp.dot(normed, key_w, precision=highest)))
    values_all = low(low_back(jnp.dot(normed, value_w, precision=highest) + value_b))
    query_h = queries.reshape(LENGTH, HEADS, HEAD_DIM)
    key_h = keys_all.reshape(LENGTH, HEADS, HEAD_DIM)
    value_h = values_all.reshape(LENGTH, HEADS, HEAD_DIM)
    scale = HEAD_DIM ** (-0.5)
    scores = low_back(jnp.einsum('qhd,khd->hqk', query_h, key_h, precision=highest) * scale)
    position = jnp.arange(LENGTH)
    allowed = (position[None, :] <= position[:, None]) & (seg_row[None, :] == seg_row[:, None])
    masked = jnp.where(allowed[None], scores, -jnp.inf)
    maximum = lax.optimization_barrier(jnp.max(masked, -1, keepdims=True))
    expo = jnp.exp(masked - maximum)
    probs = expo / lax.optimization_barrier(jnp.sum(expo, -1, keepdims=True))
    context = jnp.einsum('hqk,khd->qhd', low(probs), value_h, precision=highest).reshape(LENGTH, D)
    context = low(low_back(context))
    return stream + low_back(jnp.dot(context, out_w, precision=highest) + out_b)

def sublayer(stream, gain_vec, shift_vec, expand, lift, shrink, offset):
    normed = low(norm_rows(stream, gain_vec, shift_vec))
    hidden_pre = low_back(jnp.dot(normed, expand, precision=highest) + lift)
    active = low(jax.nn.gelu(hidden_pre, approximate=False))
    return low_back(jnp.dot(active, shrink, precision=highest) + offset)

def expert_rows(row_data, params):
    fgain, fshift, fexpand, flift, fshrink, foffset, bgain, bshift, bexpand, blift, bshrink, boffset, centre = params
    front_out = sublayer(row_data, fgain, fshift, fexpand, flift, fshrink, foffset)
    middle = row_data + front_out
    back_out = sublayer(middle, bgain, bshift, bexpand, blift, bshrink, boffset)
    gate = jax.nn.sigmoid(lax.optimization_barrier(jnp.sum(row_data * centre, -1, keepdims=True)))
    return low(gate * (front_out + back_out))

def reference(tokens, cotangent, segments, routes, attngain, attnshift, querymat, querybias, keymat, valuemat, valuebias, outmat, outbias, frontgain, frontshift, frontexpand, frontlift, frontreduce, frontoffset, backgain, backshift, backexpand, backlift, backreduce, backoffset, centroid):
    wide = jnp.float32
    attn_args = tuple((entry.astype(wide) for entry in (attngain, attnshift, querymat, querybias, keymat, valuemat, valuebias, outmat, outbias)))
    expert_args = tuple((entry.astype(wide) for entry in (frontgain, frontshift, frontexpand, frontlift, frontreduce, frontoffset, backgain, backshift, backexpand, backlift, backreduce, backoffset, centroid)))
    ordering = jnp.argsort(routes.reshape(-1), stable=True).astype(jnp.int32)
    attend = jax.checkpoint(attend_sequence)
    expert_fn = jax.checkpoint(expert_rows)

    def forward(inputs, attn_params, expert_params):
        streams = inputs.reshape(SEQS, LENGTH, D)

        def scan_step(carry, couple):
            return (carry, attend(couple[0], couple[1], attn_params))
        _, hidden = lax.scan(scan_step, jnp.zeros((), jnp.float32), (streams, segments))
        hidden = hidden.reshape(TOKENS, D)
        sent = low(low_back(hidden))
        grouped = sent[ordering].reshape(EXPERTS, SEQS * TOK_DEV, D)
        outputs = lax.map(lambda couple: expert_fn(couple[0], couple[1]), (grouped, expert_params))
        delta = jnp.zeros((TOKENS, D), jnp.float32).at[ordering].set(outputs.reshape(TOKENS, D))
        return hidden + delta
    output, pullback = jax.vjp(forward, tokens.astype(wide), attn_args, expert_args)
    tokens_grad, attn_grads, expert_grads = pullback(cotangent.astype(wide))
    return (output.astype(jnp.bfloat16), tokens_grad, attn_grads[0], attn_grads[1], attn_grads[2], attn_grads[3], attn_grads[4], attn_grads[5], attn_grads[6], attn_grads[7], attn_grads[8], expert_grads[0], expert_grads[1], expert_grads[2], expert_grads[3], expert_grads[4], expert_grads[5], expert_grads[6], expert_grads[7], expert_grads[8], expert_grads[9], expert_grads[10], expert_grads[11], expert_grads[12])
```

```python
import jax
import jax.numpy as jnp
from jax import lax
from jax.experimental import pallas as pl
from jax.experimental.pallas import tpu as pltpu
from jax.sharding import Mesh, PartitionSpec as P

HEADS = 16
HEAD_DIM = 64
EPSILON = 1e-05
MASKED = -1e30

GROUP = ("z", "c")
DATA = ("x", "y")
EVERY = ("x", "y", "z", "c")

wide = jnp.float32
narrow = jnp.bfloat16


def matmul(left, right):
    return jnp.dot(left, right, preferred_element_type=wide)


def matmul_left(left, right):
    return lax.dot_general(left, right, (((0,), (0,)), ((), ())), preferred_element_type=wide)


def matmul_right(left, right):
    return lax.dot_general(left, right, (((1,), (1,)), ((), ())), preferred_element_type=wide)


def norm_parts(stream):
    center = stream - jnp.mean(stream, -1, keepdims=True)
    inverse = lax.rsqrt(jnp.mean(center * center, -1, keepdims=True) + EPSILON)
    return center * inverse, inverse


def norm_back(scaled, xhat, inverse):
    return (
        scaled
        - jnp.mean(scaled, -1, keepdims=True)
        - xhat * jnp.mean(scaled * xhat, -1, keepdims=True)
    ) * inverse


def gelu_pair(value):
    cdf = 0.5 + 0.5 * lax.erf(value * (0.5**0.5))
    pdf = jnp.exp(-0.5 * value * value) * 0.3989422804014327
    return value * cdf, cdf + value * pdf


def shift_by(value, axis, step):
    return lax.ppermute(value, axis, [(i, (i + step) % 4) for i in range(4)])


def share_rows(rows, axis):
    return jnp.concatenate(
        [rows, shift_by(rows, axis, 1), shift_by(rows, axis, 3), shift_by(rows, axis, 2)], 0
    )


def sum_rows(partial, axis):
    own, back, ahead, away = jnp.split(partial.astype(narrow), 4, 0)
    got = (shift_by(back, axis, 3), shift_by(ahead, axis, 1), shift_by(away, axis, 2))
    return own.astype(wide) + sum(part.astype(wide) for part in got)


def exchange(blocks, axes):
    return lax.all_to_all(blocks, axes, 0, 0, tiled=True)


def to_everyone(block, axes, count):
    return exchange(jnp.broadcast_to(block[None], (count,) + block.shape), axes)


def head_rows(matrix, head):
    rows = lax.broadcasted_iota(jnp.int32, matrix.shape, 0) // HEAD_DIM
    return jnp.where(rows == head, matrix, jnp.zeros_like(matrix))


def head_lanes(matrix, head):
    lanes = lax.broadcasted_iota(jnp.int32, matrix.shape, 1) // HEAD_DIM
    return jnp.where(lanes == head, matrix, jnp.zeros_like(matrix))


def turn(matrix):
    return jnp.transpose(matrix.astype(wide), (1, 0)).astype(matrix.dtype)


def mask_of(segcol_ref, segrow_ref, i, j, diagonal):
    same = segcol_ref[j] == segrow_ref[i]
    if diagonal:
        size = same.shape
        same = same & (
            lax.broadcasted_iota(jnp.int32, size, 0) <= lax.broadcasted_iota(jnp.int32, size, 1)
        )
    return same


def attend_kernel(low_ref, qkv_ref, segcol_ref, segrow_ref, ctx_ref, full_ref, lse_ref, vals_ref):
    blocks, size, _ = qkv_ref.shape
    for j in range(blocks):
        turned = turn(qkv_ref[j, :, 256:384])
        for head in range(2):
            vals_ref[j, head, 0:64, :] = turned[head * 64 : head * 64 + 64]
            vals_ref[j, head, 64:80, :] = jnp.ones((16, size), narrow)
    for i in range(blocks):
        query = turn((qkv_ref[i, :, 0:128].astype(wide) * HEAD_DIM**-0.5).astype(narrow))
        queries = [head_rows(query, head) for head in range(2)]

        def step(j, carry, diagonal):
            keys = qkv_ref[j, :, 128:256]
            mask = mask_of(segcol_ref, segrow_ref, i, j, diagonal)
            out = []
            for head in range(2):
                scores = jnp.where(mask, matmul(keys, queries[head]), MASKED)
                top = jnp.max(scores, 0, keepdims=True)
                if carry is not None:
                    top = jnp.maximum(top, carry[2 * head])
                probs = jnp.exp(scores - top).astype(narrow)
                total = matmul(vals_ref[j, head], probs)
                if carry is not None:
                    total = total + carry[2 * head + 1] * jnp.exp(carry[2 * head] - top)
                out += [top, total]
            return tuple(out)

        carry = step(i, None, True)
        if i > 0:
            carry = lax.fori_loop(low_ref[i], i, lambda j, c: step(j, c, False), carry)
        parts = []
        for head in range(2):
            top, total = carry[2 * head], carry[2 * head + 1]
            parts.append(total[0:64] / total[64:65])
            lse_ref[i, head : head + 1, :] = top + jnp.log(total[64:65])
        full = jnp.concatenate(parts, 0)
        full_ref[i] = full
        ctx_ref[i] = jnp.transpose(full, (1, 0)).astype(narrow)


def attend(low, qkv, segcol, segrow):
    blocks, size, _ = qkv.shape
    vmem = pl.BlockSpec(memory_space=pltpu.VMEM)
    return pl.pallas_call(
        attend_kernel,
        out_shape=(
            jax.ShapeDtypeStruct((blocks, size, 128), narrow),
            jax.ShapeDtypeStruct((blocks, 128, size), wide),
            jax.ShapeDtypeStruct((blocks, 8, size), wide),
        ),
        in_specs=[pl.BlockSpec(memory_space=pltpu.SMEM), vmem, vmem, vmem],
        out_specs=(vmem, vmem, vmem),
        scratch_shapes=[pltpu.VMEM((blocks, 2, 80, size), narrow)],
        compiler_params=pltpu.CompilerParams(vmem_limit_bytes=40 << 20),
        name="attend",
    )(low, qkv, segcol, segrow)


def attend_back_kernel(
    low_ref, qkv_ref, grad_ref, full_ref, lse_ref, segcol_ref, segrow_ref,
    out_ref, keys_ref, dk_ref, dv_ref,
):
    blocks, size, _ = qkv_ref.shape
    for j in range(blocks):
        keys_ref[j] = turn(qkv_ref[j, :, 128:256])
    dk_ref[...] = jnp.zeros_like(dk_ref)
    dv_ref[...] = jnp.zeros_like(dv_ref)
    for i in range(blocks):
        query = (qkv_ref[i, :, 0:128].astype(wide) * HEAD_DIM**-0.5).astype(narrow)
        query_t = turn(query)
        grad = grad_ref[i]
        grad_t = turn(grad)
        inner = grad_t.astype(wide) * full_ref[i]
        queries_t = [head_rows(query_t, head) for head in range(2)]
        grads_t = [head_rows(grad_t, head) for head in range(2)]
        inners = [
            jnp.sum(inner[head * 64 : head * 64 + 64], 0, keepdims=True) for head in range(2)
        ]
        lses = [lse_ref[i, head : head + 1, :] for head in range(2)]
        query_pair = jnp.concatenate([head_lanes(query, head) for head in range(2)], 0)
        grad_pair = jnp.concatenate([head_lanes(grad, head) for head in range(2)], 0)

        def step(j, carry, diagonal):
            keys = qkv_ref[j, :, 128:256]
            vals = qkv_ref[j, :, 256:384]
            mask = mask_of(segcol_ref, segrow_ref, i, j, diagonal)
            lows, score_lows, out = [], [], []
            for head in range(2):
                scores = matmul(keys, queries_t[head])
                probs = jnp.where(mask, jnp.exp(scores - lses[head]), 0.0)
                prob_grad = matmul(vals, grads_t[head])
                score_low = (probs * (prob_grad - inners[head])).astype(narrow)
                lows.append(probs.astype(narrow))
                score_lows.append(score_low)
                part = matmul(keys_ref[j, head * 64 : head * 64 + 64, :], score_low)
                out.append(part if carry is None else carry[head] + part)
            dv_ref[j] += matmul(jnp.concatenate(lows, 1), grad_pair)
            dk_ref[j] += matmul(jnp.concatenate(score_lows, 1), query_pair)
            return tuple(out)

        carry = step(i, None, True)
        if i > 0:
            carry = lax.fori_loop(low_ref[i], i, lambda j, c: step(j, c, False), carry)
        dq = jnp.concatenate(carry, 0) * HEAD_DIM**-0.5
        out_ref[i, :, 0:128] = jnp.transpose(dq, (1, 0)).astype(narrow)
    for j in range(blocks):
        out_ref[j, :, 128:256] = dk_ref[j].astype(narrow)
        out_ref[j, :, 256:384] = dv_ref[j].astype(narrow)


def attend_back(low, qkv, grad, full, lse, segcol, segrow):
    blocks, size, _ = qkv.shape
    vmem = pl.BlockSpec(memory_space=pltpu.VMEM)
    return pl.pallas_call(
        attend_back_kernel,
        out_shape=jax.ShapeDtypeStruct((blocks, size, 384), narrow),
        in_specs=[pl.BlockSpec(memory_space=pltpu.SMEM)] + [vmem] * 6,
        out_specs=vmem,
        scratch_shapes=[
            pltpu.VMEM((blocks, 128, size), narrow),
            pltpu.VMEM((blocks, size, 128), wide),
            pltpu.VMEM((blocks, size, 128), wide),
        ],
        compiler_params=pltpu.CompilerParams(vmem_limit_bytes=40 << 20),
        name="attend_back",
    )(low, qkv, grad, full, lse, segcol, segrow)


def per_device(
    tokens, cotangent, segments, routes,
    attngain, attnshift, querymat, querybias, keymat, valuemat, valuebias, outmat, outbias,
    frontgain, frontshift, frontexpand, frontlift, frontreduce, frontoffset,
    backgain, backshift, backexpand, backlift, backreduce, backoffset, centroid,
):
    rows, width = tokens.shape
    experts = 8
    capacity = rows // experts + rows // (2 * experts)
    slots = experts * capacity
    mine = lax.axis_index(GROUP)
    x_at, y_at = lax.axis_index("x"), lax.axis_index("y")

    plans = to_everyone(jnp.concatenate([segments, routes], 0), GROUP, experts)
    seg_all, route_all = plans[:, 0], plans[:, 1]
    small_own = jnp.concatenate(
        [
            frontgain[0], frontshift[0], frontoffset[0], backgain[0], backshift[0], backoffset[0],
            centroid[0], frontlift[0], backlift[0], jnp.zeros((64,), narrow),
        ]
    )
    small = to_everyone(small_own.reshape(8, 128), DATA, 16).reshape(16, 1024).astype(wide)
    front_gain, front_shift, front_offset, back_gain, back_shift, back_offset, centre = (
        small[:, i * 64 : i * 64 + 64].reshape(1, width) for i in range(7)
    )
    lifts = small[:, 448:960].reshape(4, 4, 512)
    front_lift = lax.dynamic_index_in_dim(lifts, y_at, 1, False)[:, :256].reshape(1, 1024)
    back_lift = lax.dynamic_index_in_dim(lifts, x_at, 0, False)[:, 256:].reshape(1, 1024)

    front_expand = lax.all_gather(frontexpand[0], "x", axis=0)
    front_shrink = lax.all_gather(frontreduce[0], "x", axis=0, tiled=True)
    back_expand = lax.all_gather(backexpand[0], "y", axis=0)
    back_shrink = lax.all_gather(backreduce[0], "y", axis=0, tiled=True)
    front_expand = jnp.transpose(front_expand, (1, 0, 2)).reshape(width, 1024)
    back_expand = jnp.transpose(back_expand, (1, 0, 2)).reshape(width, 1024)

    route = routes[0]
    picks = (route[:, None] == jnp.arange(experts)[None, :]).astype(narrow)
    lower = (jnp.arange(rows)[:, None] > jnp.arange(rows)[None, :]).astype(narrow)
    rank = jnp.sum(matmul(lower, picks) * picks.astype(wide), 1).astype(jnp.int32)
    send_index = route * capacity + rank
    sender = (jnp.arange(slots)[:, None] == send_index[None, :]).astype(narrow)
    counts = jnp.sum((route_all == mine).astype(jnp.int32), 1)
    ahead = jnp.arange(experts)[:, None] > jnp.arange(experts)[None, :]
    starts = jnp.sum(jnp.where(ahead, counts[None, :], 0), 1)
    place = jnp.arange(capacity)[None, :]
    spots = jnp.where(place < counts[:, None], starts[:, None] + place, -1).reshape(-1)
    taker = (jnp.arange(rows)[:, None] == spots[None, :]).astype(narrow)

    def to_experts(row_data):
        packed = matmul(sender, row_data).astype(narrow).reshape(experts, capacity, width)
        return matmul(taker, exchange(packed, GROUP).reshape(slots, width))

    def to_tokens(row_data):
        packed = matmul_left(taker, row_data).astype(narrow).reshape(experts, capacity, width)
        return matmul_left(sender, exchange(packed, GROUP).reshape(slots, width))

    ct_rows = to_experts(cotangent)

    inputs = tokens.astype(wide)
    attn_gain = attngain.astype(wide)
    attn_xhat, attn_inverse = norm_parts(inputs)
    attn_normed = (attn_xhat * attn_gain + attnshift.astype(wide)).astype(narrow)
    query = (matmul(attn_normed, querymat) + querybias.astype(wide)).astype(narrow)
    key = matmul(attn_normed, keymat).astype(narrow)
    value = (matmul(attn_normed, valuemat) + valuebias.astype(wide)).astype(narrow)
    split = jnp.stack([part.reshape(rows, experts, 128) for part in (query, key, value)], 2)
    qkv = exchange(jnp.transpose(split, (1, 0, 2, 3)).reshape(experts, rows, 384), GROUP)
    normed_all = lax.all_gather(attn_normed, GROUP, axis=0, tiled=True)
    segcol, segrow = seg_all[:, :, None], seg_all[:, None, :]
    low = jnp.sum((seg_all[None, :, -1] < seg_all[:, None, 0]).astype(jnp.int32), 1)
    ctx, full, lse = attend(low, qkv, segcol, segrow)
    context = jnp.transpose(exchange(ctx, GROUP), (1, 0, 2)).reshape(rows, width)
    hidden = inputs + matmul(context, outmat) + outbias.astype(wide)

    stream = to_experts(hidden.astype(narrow))
    gate = jax.nn.sigmoid(jnp.sum(stream * centre, -1, keepdims=True))
    gated = gate * ct_rows
    back_branch = gated.astype(narrow)
    back_branches = share_rows(back_branch, "x")
    front_xhat, front_inverse = norm_parts(stream)
    front_normed = (front_xhat * front_gain + front_shift).astype(narrow)
    front_rows = share_rows(front_normed, "y")
    front_act, front_slope = gelu_pair(matmul(front_rows, front_expand) + front_lift)
    front_act = front_act.astype(narrow)
    front_out = sum_rows(matmul(front_act, front_shrink), "y") + front_offset
    middle = stream + front_out
    back_xhat, back_inverse = norm_parts(middle)
    back_normed = (back_xhat * back_gain + back_shift).astype(narrow)
    back_rows = share_rows(back_normed, "x")
    back_act, back_slope = gelu_pair(matmul(back_rows, back_expand) + back_lift)
    back_act = back_act.astype(narrow)
    back_pre_grad = (back_slope * matmul_right(back_branches, back_shrink)).astype(narrow)
    back_norm_grad = sum_rows(matmul_right(back_pre_grad, back_expand), "x")
    middle_grad = norm_back(back_norm_grad * back_gain, back_xhat, back_inverse)
    front_branch = (gated + middle_grad).astype(narrow)
    front_branches = share_rows(front_branch, "y")
    front_pre_grad = (front_slope * matmul_right(front_branches, front_shrink)).astype(narrow)
    front_norm_grad = sum_rows(matmul_right(front_pre_grad, front_expand), "y")
    first_grad = norm_back(front_norm_grad * front_gain, front_xhat, front_inverse)
    back_out = sum_rows(matmul(back_act, back_shrink), "x") + back_offset
    branches = front_out + back_out
    logit_grad = jnp.sum(ct_rows * branches, -1, keepdims=True) * gate * (1.0 - gate)
    sent_grad = (logit_grad * centre + middle_grad + first_grad).astype(narrow)

    returned = (gate * branches).astype(narrow)
    result = (hidden + to_tokens(returned)).astype(narrow)
    hidden_grad = cotangent.astype(wide) + to_tokens(sent_grad)
    out_low = hidden_grad.astype(narrow)
    context_grad = matmul_right(out_low, outmat).astype(narrow)
    grads = exchange(jnp.transpose(context_grad.reshape(rows, experts, 128), (1, 0, 2)), GROUP)

    def scatter(normed_rows, pre_grad, act, branch_rows, axis):
        expand_grad = matmul_left(normed_rows, pre_grad).astype(narrow).reshape(width, 4, 256)
        expand_grad = lax.psum_scatter(
            jnp.transpose(expand_grad, (1, 0, 2)), axis, scatter_dimension=0, tiled=True
        )
        shrink_grad = lax.psum_scatter(
            matmul_left(act, branch_rows).astype(narrow), axis, scatter_dimension=0, tiled=True
        )
        return expand_grad.astype(wide), shrink_grad.astype(wide)[None]

    back_expand_grad, back_shrink_grad = scatter(
        back_rows, back_pre_grad, back_act, back_branches, "y"
    )
    front_expand_grad, front_shrink_grad = scatter(
        front_rows, front_pre_grad, front_act, front_branches, "x"
    )
    sums = jnp.stack(
        [
            jnp.sum(front_norm_grad * front_xhat, 0),
            jnp.sum(front_norm_grad, 0),
            jnp.sum(front_branch.astype(wide), 0),
            jnp.sum(back_norm_grad * back_xhat, 0),
            jnp.sum(back_norm_grad, 0),
            jnp.sum(back_branch.astype(wide), 0),
            jnp.sum(logit_grad * stream, 0),
        ]
    ).reshape(7, 16, 64)
    front_lift_sum = jnp.sum(front_pre_grad.astype(wide), 0).reshape(4, 1, 256)
    back_lift_sum = jnp.sum(back_pre_grad.astype(wide), 0).reshape(1, 4, 256)
    fours = jnp.arange(4)
    front_lift_sums = jnp.where(fours[None, :, None] == y_at, front_lift_sum, 0.0)
    back_lift_sums = jnp.where(fours[:, None, None] == x_at, back_lift_sum, 0.0)
    packed = jnp.concatenate(
        [
            jnp.transpose(sums, (1, 0, 2)).reshape(16, 448),
            front_lift_sums.reshape(16, 256),
            back_lift_sums.reshape(16, 256),
            jnp.zeros((16, 64), wide),
        ],
        1,
    )
    summed = jnp.sum(exchange(packed.reshape(16, 8, 128), DATA), 0).reshape(1, 1024)
    (
        front_gain_grad, front_shift_grad, front_offset_grad,
        back_gain_grad, back_shift_grad, back_offset_grad, centroid_grad,
    ) = (summed[:, i * 64 : i * 64 + 64] for i in range(7))
    front_lift_grad, back_lift_grad = summed[:, 448:704], summed[:, 704:960]

    dqkv = attend_back(low, qkv, grads, full, lse, segcol, segrow)
    own = jnp.transpose(exchange(dqkv, GROUP).reshape(experts, rows, 3, 128), (2, 1, 0, 3))
    dquery, dkey, dvalue = (own[i].reshape(rows, width) for i in range(3))
    attn_norm_grad = (
        matmul_right(dquery, querymat) + matmul_right(dkey, keymat) + matmul_right(dvalue, valuemat)
    )
    tokens_grad = hidden_grad + norm_back(attn_norm_grad * attn_gain, attn_xhat, attn_inverse)

    dqkv_rows = dqkv.reshape(experts * rows, 384)
    three = exchange(matmul_left(normed_all, dqkv_rows).astype(narrow).reshape(16, 64, 384), DATA)
    three = jnp.sum(three.astype(wide), 0).astype(narrow)
    out_part = matmul_left(context, out_low).astype(narrow).reshape(experts, 128, width)
    out_part = jnp.sum(exchange(out_part, GROUP).astype(wide), 0).astype(narrow)
    out_part = exchange(out_part.reshape(16, 8, width), DATA)
    out_part = jnp.sum(out_part.astype(wide), 0).astype(narrow)
    slices = jnp.concatenate([three.reshape(192, 128), out_part.reshape(64, 128)], 0)
    everything = lax.all_gather(slices, EVERY, axis=0).reshape(16, 8, 256, 128)
    mats = everything[:, :, :192].reshape(16, 8, 64, 3, 128)
    mats = jnp.transpose(mats, (3, 0, 2, 1, 4)).reshape(3, width, width).astype(wide)
    outmat_grad = jnp.transpose(everything[:, :, 192:].reshape(16, 8, 8, width), (1, 0, 2, 3))
    outmat_grad = outmat_grad.reshape(width, width).astype(wide)

    vectors = jnp.stack(
        [
            jnp.sum(out_low.astype(wide), 0),
            jnp.sum(attn_norm_grad * attn_xhat, 0),
            jnp.sum(attn_norm_grad, 0),
            jnp.sum(dquery.astype(wide), 0),
            jnp.sum(dvalue.astype(wide), 0),
        ]
    ).reshape(5, 8, 128)
    vectors = jnp.sum(exchange(jnp.transpose(vectors, (1, 0, 2)), GROUP), 0)
    vectors = jnp.transpose(vectors.reshape(5, 16, 8), (1, 0, 2)).reshape(16, 40)
    vectors = jnp.sum(exchange(vectors, DATA), 0)
    vectors = to_everyone(to_everyone(vectors, DATA, 16), GROUP, experts)
    vectors = jnp.transpose(vectors.reshape(8, 16, 5, 8), (2, 0, 1, 3)).reshape(5, width)
    outbias_grad, attngain_grad, attnshift_grad, querybias_grad, valuebias_grad = vectors
    return (
        result, tokens_grad, attngain_grad, attnshift_grad,
        mats[0], querybias_grad, mats[1], mats[2], valuebias_grad, outmat_grad, outbias_grad,
        front_gain_grad, front_shift_grad, front_expand_grad, front_lift_grad,
        front_shrink_grad, front_offset_grad,
        back_gain_grad, back_shift_grad, back_expand_grad, back_lift_grad,
        back_shrink_grad, back_offset_grad, centroid_grad,
    )


def solution(mesh):
    grid = Mesh(mesh.devices.reshape(4, 4, 4, 2), EVERY)
    rows, plan, full = P(EVERY, None), P(DATA, GROUP), P()
    vector, expand, shrink = P(GROUP, DATA), P(GROUP, None, DATA), P(GROUP, DATA, None)
    sublayer = (vector, vector, expand, vector, shrink, vector)
    return jax.shard_map(
        per_device,
        mesh=grid,
        in_specs=(rows, rows, plan, plan) + (full,) * 9 + sublayer * 2 + (vector,),
        out_specs=(rows, rows) + (full,) * 9 + sublayer * 2 + (vector,),
        check_vma=False,
    )
```

```python
import jax
import jax.numpy as jnp
from jax import lax
from jax.experimental import pallas as pl
from jax.experimental.pallas import tpu as pltpu
from jax.sharding import Mesh, PartitionSpec as P

HEADS = 16
HEAD_DIM = 64
EPSILON = 1e-05
MASKED = -1e30

GROUP = ("z", "c")
DATA = ("x", "y1", "y2")
COLUMN = ("y1", "y2")
EVERY = DATA + GROUP

wide = jnp.float32
narrow = jnp.bfloat16


def matmul(left, right):
    return jnp.dot(left, right, preferred_element_type=wide)


def matmul_left(left, right):
    return lax.dot_general(left, right, (((0,), (0,)), ((), ())), preferred_element_type=wide)


def matmul_right(left, right):
    return lax.dot_general(left, right, (((1,), (1,)), ((), ())), preferred_element_type=wide)


def norm_parts(stream):
    center = stream - jnp.mean(stream, -1, keepdims=True)
    inverse = lax.rsqrt(jnp.mean(center * center, -1, keepdims=True) + EPSILON)
    return center * inverse, inverse


def norm_back(scaled, xhat, inverse):
    return (
        scaled
        - jnp.mean(scaled, -1, keepdims=True)
        - xhat * jnp.mean(scaled * xhat, -1, keepdims=True)
    ) * inverse


def gelu_pair(value):
    cdf = 0.5 + 0.5 * lax.erf(value * (0.5**0.5))
    pdf = jnp.exp(-0.5 * value * value) * 0.3989422804014327
    return value * cdf, cdf + value * pdf


def swap(value, axis):
    return lax.ppermute(value, axis, [(0, 1), (1, 0)])


def shift_by(value, step):
    return lax.ppermute(value, "x", [(i, (i + step) % 4) for i in range(4)])


def share_two(rows):
    return jnp.concatenate([rows, swap(rows, "y2")], 0)


def share_four(rows):
    return jnp.concatenate([rows] + [shift_by(rows, step) for step in (1, 3, 2)], 0)


def return_four(partial):
    _, back, ahead, away = jnp.split(partial, 4, 0)
    return shift_by(back, 3), shift_by(ahead, 1), shift_by(away, 2)


def total(own, got):
    return own.astype(wide) + sum(part.astype(wide) for part in got)


def after(first, *later):
    later = lax.optimization_barrier((first,) + later)[1:]
    return later if len(later) > 1 else later[0]


def exchange(blocks, axes):
    return lax.all_to_all(blocks, axes, 0, 0, tiled=True)


def to_everyone(block, axes, count):
    return exchange(jnp.broadcast_to(block[None], (count,) + block.shape), axes)


def head_rows(matrix, head):
    rows = lax.broadcasted_iota(jnp.int32, matrix.shape, 0) // HEAD_DIM
    return jnp.where(rows == head, matrix, jnp.zeros_like(matrix))


def head_lanes(matrix, head):
    lanes = lax.broadcasted_iota(jnp.int32, matrix.shape, 1) // HEAD_DIM
    return jnp.where(lanes == head, matrix, jnp.zeros_like(matrix))


def turn(matrix):
    return jnp.transpose(matrix.astype(wide), (1, 0)).astype(matrix.dtype)


def mask_of(segcol_ref, segrow_ref, i, j, diagonal):
    same = segcol_ref[j] == segrow_ref[i]
    if diagonal:
        size = same.shape
        same = same & (
            lax.broadcasted_iota(jnp.int32, size, 0) <= lax.broadcasted_iota(jnp.int32, size, 1)
        )
    return same


def project_kernel(
    tokens_ref, gain_ref, shift_ref, query_ref, key_ref, value_ref, query_bias_ref, value_bias_ref,
    out_ref, xhat_ref, normed_ref,
):
    @pl.when(pl.program_id(0) == 0)
    def _():
        xhat, _ = norm_parts(tokens_ref[...].astype(wide))
        xhat_ref[...] = xhat.astype(narrow)
        normed = xhat * gain_ref[...].astype(wide) + shift_ref[...].astype(wide)
        normed_ref[...] = normed.astype(narrow)

    normed = normed_ref[...]
    query = matmul(normed, query_ref[...]) + query_bias_ref[...].astype(wide)
    value = matmul(normed, value_ref[...]) + value_bias_ref[...].astype(wide)
    out_ref[0, :, 0:128] = query.astype(narrow)
    out_ref[0, :, 128:256] = matmul(normed, key_ref[...]).astype(narrow)
    out_ref[0, :, 256:384] = value.astype(narrow)


def project(tokens, gain, shift, querymat, querybias, keymat, valuemat, valuebias):
    rows, width = tokens.shape
    all_rows = pl.BlockSpec((rows, width), lambda e: (0, 0))
    line = pl.BlockSpec((1, width), lambda e: (0, 0))
    mat, bias = pl.BlockSpec((width, 128), lambda e: (0, e)), pl.BlockSpec((1, 128), lambda e: (0, e))
    return pl.pallas_call(
        project_kernel,
        grid=(8,),
        out_shape=(
            jax.ShapeDtypeStruct((8, rows, 384), narrow),
            jax.ShapeDtypeStruct((rows, width), narrow),
        ),
        in_specs=[all_rows, line, line, mat, mat, mat, bias, bias],
        out_specs=(pl.BlockSpec((1, rows, 384), lambda e: (e, 0, 0)), all_rows),
        scratch_shapes=[pltpu.VMEM((rows, width), narrow)],
        compiler_params=pltpu.CompilerParams(vmem_limit_bytes=32 << 20),
        name="project",
    )(tokens, gain, shift, querymat, keymat, valuemat, querybias, valuebias)


def join_kernel(ctx_ref, outmat_ref, tokens_ref, bias_ref, sender_ref, hidden_ref, packed_ref, context_ref):
    @pl.when(pl.program_id(0) == 0)
    def _():
        for e in range(8):
            context_ref[:, e * 128 : e * 128 + 128] = ctx_ref[e]

    hidden = tokens_ref[...].astype(wide) + bias_ref[...].astype(wide)
    hidden = hidden + matmul(context_ref[...], outmat_ref[...])
    hidden_ref[...] = hidden
    packed_ref[...] = matmul(sender_ref[...], hidden.astype(narrow)).astype(narrow)


def join(ctx, outmat, tokens, outbias, sender):
    rows, width = tokens.shape
    slots = sender.shape[0]
    strip = lambda height: pl.BlockSpec((height, 256), lambda n: (0, n))
    return pl.pallas_call(
        join_kernel,
        grid=(4,),
        out_shape=(
            jax.ShapeDtypeStruct((rows, width), wide),
            jax.ShapeDtypeStruct((slots, width), narrow),
            jax.ShapeDtypeStruct((rows, width), narrow),
        ),
        in_specs=[
            pl.BlockSpec((8, rows, 128), lambda n: (0, 0, 0)),
            strip(width), strip(rows), strip(1),
            pl.BlockSpec((slots, rows), lambda n: (0, 0)),
        ],
        out_specs=(strip(rows), strip(slots), pl.BlockSpec((rows, width), lambda n: (0, 0))),
        compiler_params=pltpu.CompilerParams(vmem_limit_bytes=32 << 20),
        name="join",
    )(ctx, outmat, tokens, outbias, sender)


def hidden_back_kernel(blocks_ref, getter_ref, cotangent_ref, outmat_ref, hidden_ref, grads_ref, low_ref):
    @pl.when(pl.program_id(0) == 0)
    def _():
        hidden = cotangent_ref[...].astype(wide) + matmul(getter_ref[...], blocks_ref[...])
        hidden_ref[...] = hidden
        low_ref[...] = hidden.astype(narrow)

    grads = matmul_right(low_ref[...], outmat_ref[...]).astype(narrow)
    grads_ref[0] = grads[:, 0:128]
    grads_ref[1] = grads[:, 128:256]


def hidden_back(blocks, getter, cotangent, outmat):
    rows, width = cotangent.shape
    slots = getter.shape[1]
    all_rows = pl.BlockSpec((rows, width), lambda e: (0, 0))
    return pl.pallas_call(
        hidden_back_kernel,
        grid=(4,),
        out_shape=(
            jax.ShapeDtypeStruct((rows, width), wide),
            jax.ShapeDtypeStruct((8, rows, 128), narrow),
            jax.ShapeDtypeStruct((rows, width), narrow),
        ),
        in_specs=[
            pl.BlockSpec((slots, width), lambda e: (0, 0)),
            pl.BlockSpec((rows, slots), lambda e: (0, 0)),
            all_rows,
            pl.BlockSpec((256, width), lambda e: (e, 0)),
        ],
        out_specs=(all_rows, pl.BlockSpec((2, rows, 128), lambda e: (e, 0, 0)), all_rows),
        compiler_params=pltpu.CompilerParams(vmem_limit_bytes=32 << 20),
        name="hidden_back",
    )(blocks, getter, cotangent, outmat)


def attend_kernel(low_ref, qkv_ref, segcol_ref, segrow_ref, ctx_ref, full_ref, lse_ref, vals_ref):
    blocks, size, _ = qkv_ref.shape
    for j in range(blocks):
        turned = turn(qkv_ref[j, :, 256:384])
        for head in range(2):
            vals_ref[j, head, 0:64, :] = turned[head * 64 : head * 64 + 64]
            vals_ref[j, head, 64:80, :] = jnp.ones((16, size), narrow)
    for i in range(blocks):
        query = turn((qkv_ref[i, :, 0:128].astype(wide) * HEAD_DIM**-0.5).astype(narrow))
        queries = [head_rows(query, head) for head in range(2)]

        def step(j, carry, diagonal):
            keys = qkv_ref[j, :, 128:256]
            mask = mask_of(segcol_ref, segrow_ref, i, j, diagonal)
            out = []
            for head in range(2):
                scores = jnp.where(mask, matmul(keys, queries[head]), MASKED)
                top = jnp.max(scores, 0, keepdims=True)
                if carry is not None:
                    top = jnp.maximum(top, carry[2 * head])
                probs = jnp.exp(scores - top).astype(narrow)
                total = matmul(vals_ref[j, head], probs)
                if carry is not None:
                    total = total + carry[2 * head + 1] * jnp.exp(carry[2 * head] - top)
                out += [top, total]
            return tuple(out)

        carry = step(i, None, True)
        if i > 0:
            carry = lax.fori_loop(low_ref[i], i, lambda j, c: step(j, c, False), carry)
        parts = []
        for head in range(2):
            top, total = carry[2 * head], carry[2 * head + 1]
            parts.append(total[0:64] / total[64:65])
            lse_ref[i, head : head + 1, :] = top + jnp.log(total[64:65])
        full = jnp.concatenate(parts, 0)
        full_ref[i] = full
        ctx_ref[i] = jnp.transpose(full, (1, 0)).astype(narrow)


def attend(low, qkv, segcol, segrow):
    blocks, size, _ = qkv.shape
    vmem = pl.BlockSpec(memory_space=pltpu.VMEM)
    return pl.pallas_call(
        attend_kernel,
        out_shape=(
            jax.ShapeDtypeStruct((blocks, size, 128), narrow),
            jax.ShapeDtypeStruct((blocks, 128, size), wide),
            jax.ShapeDtypeStruct((blocks, 8, size), wide),
        ),
        in_specs=[pl.BlockSpec(memory_space=pltpu.SMEM), vmem, vmem, vmem],
        out_specs=(vmem, vmem, vmem),
        scratch_shapes=[pltpu.VMEM((blocks, 2, 80, size), narrow)],
        compiler_params=pltpu.CompilerParams(vmem_limit_bytes=40 << 20),
        name="attend",
    )(low, qkv, segcol, segrow)


def attend_back_kernel(
    low_ref, qkv_ref, grad_ref, full_ref, lse_ref, segcol_ref, segrow_ref, xhat_ref,
    out_ref, three_ref, sums_ref, keys_ref, dk_ref, dv_ref,
):
    blocks, size, _ = qkv_ref.shape
    for j in range(blocks):
        keys_ref[j] = turn(qkv_ref[j, :, 128:256])
    dk_ref[...] = jnp.zeros_like(dk_ref)
    dv_ref[...] = jnp.zeros_like(dv_ref)
    for i in range(blocks):
        query = (qkv_ref[i, :, 0:128].astype(wide) * HEAD_DIM**-0.5).astype(narrow)
        query_t = turn(query)
        grad = grad_ref[i]
        grad_t = turn(grad)
        inner = grad_t.astype(wide) * full_ref[i]
        queries_t = [head_rows(query_t, head) for head in range(2)]
        grads_t = [head_rows(grad_t, head) for head in range(2)]
        inners = [
            jnp.sum(inner[head * 64 : head * 64 + 64], 0, keepdims=True) for head in range(2)
        ]
        lses = [lse_ref[i, head : head + 1, :] for head in range(2)]
        query_pair = jnp.concatenate([head_lanes(query, head) for head in range(2)], 0)
        grad_pair = jnp.concatenate([head_lanes(grad, head) for head in range(2)], 0)

        def step(j, carry, diagonal):
            keys = qkv_ref[j, :, 128:256]
            vals = qkv_ref[j, :, 256:384]
            mask = mask_of(segcol_ref, segrow_ref, i, j, diagonal)
            lows, score_lows, out = [], [], []
            for head in range(2):
                scores = matmul(keys, queries_t[head])
                probs = jnp.where(mask, jnp.exp(scores - lses[head]), 0.0)
                prob_grad = matmul(vals, grads_t[head])
                score_low = (probs * (prob_grad - inners[head])).astype(narrow)
                lows.append(probs.astype(narrow))
                score_lows.append(score_low)
                part = matmul(keys_ref[j, head * 64 : head * 64 + 64, :], score_low)
                out.append(part if carry is None else carry[head] + part)
            dv_ref[j] += matmul(jnp.concatenate(lows, 1), grad_pair)
            dk_ref[j] += matmul(jnp.concatenate(score_lows, 1), query_pair)
            return tuple(out)

        carry = step(i, None, True)
        if i > 0:
            carry = lax.fori_loop(low_ref[i], i, lambda j, c: step(j, c, False), carry)
        dq = jnp.concatenate(carry, 0) * HEAD_DIM**-0.5
        out_ref[i, :, 0:128] = jnp.transpose(dq, (1, 0)).astype(narrow)
    for j in range(blocks):
        out_ref[j, :, 128:256] = dk_ref[j].astype(narrow)
        out_ref[j, :, 256:384] = dv_ref[j].astype(narrow)
    for part in range(4):
        height = slice(part * 256, part * 256 + 256)
        three = sum(matmul(xhat_ref[j, height, :], out_ref[j]) for j in range(blocks))
        for d in range(4):
            for i in range(3):
                three_ref[part * 4 + d, i * 64 : i * 64 + 64, :] = three[
                    d * 64 : d * 64 + 64, i * 128 : i * 128 + 128
                ].astype(narrow)
    sums_ref[...] = sum(jnp.sum(out_ref[j].astype(wide), 0, keepdims=True) for j in range(blocks))


def attend_back(low, qkv, grad, full, lse, segcol, segrow, xhat):
    blocks, size, _ = qkv.shape
    vmem = pl.BlockSpec(memory_space=pltpu.VMEM)
    return pl.pallas_call(
        attend_back_kernel,
        out_shape=(
            jax.ShapeDtypeStruct((blocks, size, 384), narrow),
            jax.ShapeDtypeStruct((16, 192, 128), narrow),
            jax.ShapeDtypeStruct((1, 384), wide),
        ),
        in_specs=[pl.BlockSpec(memory_space=pltpu.SMEM)] + [vmem] * 7,
        out_specs=(vmem, vmem, vmem),
        scratch_shapes=[
            pltpu.VMEM((blocks, 128, size), narrow),
            pltpu.VMEM((blocks, size, 128), wide),
            pltpu.VMEM((blocks, size, 128), wide),
        ],
        compiler_params=pltpu.CompilerParams(vmem_limit_bytes=40 << 20),
        name="attend_back",
    )(low, qkv, grad, full, lse, segcol, segrow, xhat)


def unpack_kernel(
    all_ref, bias_ref, gain_ref, shift_ref, query_ref, key_ref, value_ref,
    dquery_ref, dkey_ref, dvalue_ref, dout_ref, vector_ref,
):
    mats = ((query_ref, dquery_ref), (key_ref, dkey_ref), (value_ref, dvalue_ref))
    for d in range(all_ref.shape[0]):
        height = slice(d * 64, d * 64 + 64)
        gain, shift = gain_ref[d].astype(wide), shift_ref[d].astype(wide)
        gain_sum = shift_sum = jnp.zeros((64, 128), wide)
        for e in range(8):
            lanes = slice(e * 128, e * 128 + 128)
            for i, (mat_ref, grad_ref) in enumerate(mats):
                part = all_ref[d, e, i * 64 : i * 64 + 64, :].astype(wide)
                bias = bias_ref[i : i + 1, lanes]
                mat = mat_ref[height, lanes].astype(wide)
                grad_ref[height, lanes] = gain * part + shift * bias
                gain_sum = gain_sum + mat * part
                shift_sum = shift_sum + mat * bias
            for i in range(8):
                dout_ref[e, d, :, i * 128 : i * 128 + 128] = all_ref[
                    d, e, 192 + i * 8 : 200 + i * 8, :
                ].astype(wide)
        vector_ref[d, :, 0:1] = jnp.sum(gain_sum, 1, keepdims=True)
        vector_ref[d, :, 1:2] = jnp.sum(shift_sum, 1, keepdims=True)


def unpack(everything, biases, gain, shift, querymat, keymat, valuemat, step=2):
    width = querymat.shape[0]
    column = pl.BlockSpec((step, 64, 1), lambda d: (d, 0, 0))
    strip = pl.BlockSpec((step * 64, width), lambda d: (d, 0))
    square = jax.ShapeDtypeStruct((width, width), wide)
    return pl.pallas_call(
        unpack_kernel,
        grid=(16 // step,),
        out_shape=(
            square, square, square,
            jax.ShapeDtypeStruct((8, 16, 8, width), wide),
            jax.ShapeDtypeStruct((16, 64, 2), wide),
        ),
        in_specs=[
            pl.BlockSpec((step, 8, 264, 128), lambda d: (d, 0, 0, 0)),
            pl.BlockSpec((3, width), lambda d: (0, 0)),
            column, column, strip, strip, strip,
        ],
        out_specs=(
            strip, strip, strip,
            pl.BlockSpec((8, step, 8, width), lambda d: (0, d, 0, 0)),
            pl.BlockSpec((step, 64, 2), lambda d: (d, 0, 0)),
        ),
        compiler_params=pltpu.CompilerParams(vmem_limit_bytes=32 << 20),
        name="unpack",
    )(everything, biases, gain, shift, querymat, keymat, valuemat)


def per_device(
    tokens, cotangent, segments, routes,
    attngain, attnshift, querymat, querybias, keymat, valuemat, valuebias, outmat, outbias,
    frontgain, frontshift, frontexpand, frontlift, frontreduce, frontoffset,
    backgain, backshift, backexpand, backlift, backreduce, backoffset, centroid,
):
    rows, width = tokens.shape
    experts = 8
    capacity = rows // experts + rows // (2 * experts)
    slots = experts * capacity
    mine = lax.axis_index(GROUP)
    x_at, y1_at, y2_at = (lax.axis_index(axis) for axis in DATA)

    plans = to_everyone(jnp.concatenate([segments, routes], 0), GROUP, experts)
    small_own = jnp.concatenate(
        [
            frontgain[0], frontshift[0], frontoffset[0], backgain[0], backshift[0], backoffset[0],
            centroid[0], frontlift[0], backlift[0], jnp.zeros((64,), narrow),
        ]
    )
    small = small_own.reshape(8, 128)

    def reduced(matrix, axes):
        return lax.psum_scatter(matrix, axes, scatter_dimension=0, tiled=True)

    def gathered(matrix, axes):
        return lax.all_gather(matrix, axes, axis=0, tiled=True)

    front_expand, front_shrink = frontexpand[0].T, frontreduce[0]
    front_pair = swap(jnp.concatenate([front_expand, front_shrink], 0), "y1")
    front_expands, front_shrinks = [gathered(front_expand, "x")], [gathered(front_shrink, "x")]

    route = routes[0]
    picks = (route[:, None] == jnp.arange(experts)[None, :]).astype(narrow)
    lower = (jnp.arange(rows)[:, None] > jnp.arange(rows)[None, :]).astype(narrow)
    rank = jnp.sum(matmul(lower, picks) * picks.astype(wide), 1).astype(jnp.int32)
    send_index = route * capacity + rank
    sender = (jnp.arange(slots)[:, None] == send_index[None, :]).astype(narrow)
    def pack(row_data):
        return matmul(sender, row_data).astype(narrow).reshape(experts, capacity, width)

    def unpack_rows(blocks):
        return matmul(taker, blocks.reshape(slots, width)).astype(narrow)

    def pack_back(row_data):
        return matmul_left(taker, row_data).astype(narrow).reshape(experts, capacity, width)

    def unpack_back(blocks):
        return matmul_left(sender, blocks.reshape(slots, width))

    line = lambda vector: vector.reshape(1, width)
    split, xhat_low = project(
        tokens, line(attngain), line(attnshift),
        querymat, line(querybias), keymat, valuemat, line(valuebias),
    )
    split, plans = lax.optimization_barrier((split, plans))
    seg_all, route_all = plans[:, 0], plans[:, 1]
    qkv = exchange(split, GROUP)
    small = to_everyone(after(qkv, small), DATA, 16)
    counts = jnp.sum((route_all == mine).astype(jnp.int32), 1)
    ahead = jnp.arange(experts)[:, None] > jnp.arange(experts)[None, :]
    starts = jnp.sum(jnp.where(ahead, counts[None, :], 0), 1)
    place = jnp.arange(capacity)[None, :]
    spots = jnp.where(place < counts[:, None], starts[:, None] + place, -1).reshape(-1)
    taker = (jnp.arange(rows)[:, None] == spots[None, :]).astype(narrow)

    segcol, segrow = seg_all[:, :, None], seg_all[:, None, :]
    low = jnp.sum((seg_all[None, :, -1] < seg_all[:, None, 0]).astype(jnp.int32), 1)
    ctx, full, lse = attend(low, qkv, segcol, segrow)
    ctx, small = lax.optimization_barrier((ctx, small))
    front_pair, back_expand, back_shrink = after(ctx, front_pair, backexpand[0].T, backreduce[0])
    front_expands.append(gathered(front_pair[:256], "x"))
    front_shrinks.append(gathered(front_pair[256:], "x"))
    back_expand, back_shrink = gathered(back_expand, COLUMN), gathered(back_shrink, COLUMN)
    small = small.reshape(16, 1024).astype(wide)
    front_gain, front_shift, front_offset, back_gain, back_shift, back_offset, centre = (
        small[:, i * 64 : i * 64 + 64].reshape(1, width) for i in range(7)
    )
    lifts = small[:, 448:960].reshape(4, 2, 2, 512)
    front_lift = lax.dynamic_index_in_dim(lifts, y2_at, 2, False)[:, :, :256]
    front_lift = jnp.where(y1_at == 0, front_lift, front_lift[:, ::-1])
    front_lift = jnp.transpose(front_lift, (1, 0, 2)).reshape(2, 1, 1024)
    back_lift = lax.dynamic_index_in_dim(lifts, x_at, 0, False)[:, :, 256:].reshape(1, 1024)
    hidden, blocks, context = join(exchange(ctx, GROUP), outmat, tokens, line(outbias), sender)
    xhat_all = lax.all_gather(after(blocks, xhat_low).T, GROUP, axis=0)

    stream = unpack_rows(exchange(blocks.reshape(experts, capacity, width), GROUP)).astype(wide)
    front_xhat, front_inverse = norm_parts(stream)
    front_normed = share_two((front_xhat * front_gain + front_shift).astype(narrow))
    gate = jax.nn.sigmoid(jnp.sum(stream * centre, -1, keepdims=True))
    ct_blocks = exchange(pack(after(front_normed, cotangent)), GROUP)
    front_acts, front_slopes = [], []
    for expand, lift in zip(front_expands, front_lift):
        act, slope = gelu_pair(matmul_right(front_normed, expand) + lift)
        front_acts.append(act.astype(narrow))
        front_slopes.append(slope)
    front_part = sum(matmul(act, shrink) for act, shrink in zip(front_acts, front_shrinks))
    front_part, ct_blocks = lax.optimization_barrier((front_part, ct_blocks))
    ct_rows = unpack_rows(ct_blocks).astype(wide)
    gated = gate * ct_rows
    back_branch = gated.astype(narrow)
    front_got, back_branches = lax.optimization_barrier(
        (swap(front_part[rows:].astype(narrow), "y2"), share_four(back_branch))
    )
    front_out = front_part[:rows] + front_got.astype(wide) + front_offset
    middle = stream + front_out
    back_xhat, back_inverse = norm_parts(middle)
    back_normed = share_four((back_xhat * back_gain + back_shift).astype(narrow))
    back_act, back_slope = gelu_pair(matmul_right(back_normed, back_expand) + back_lift)
    back_act = back_act.astype(narrow)
    back_pre_grad = (back_slope * matmul_right(back_branches, back_shrink)).astype(narrow)
    back_part = matmul(back_pre_grad, back_expand).astype(narrow)
    act_late, normed_late, back_pre_late = after(back_part, back_act, back_normed, back_pre_grad)
    back_grads = [matmul_left(act_late, back_branches), matmul_left(back_pre_late, normed_late)]
    back_grads = [part.astype(narrow) for part in back_grads]
    *back_got, shrink_part, expand_part = lax.optimization_barrier(
        (*return_four(back_part), *back_grads)
    )
    back_grads = [reduced(part, COLUMN) for part in (shrink_part, expand_part)]
    back_norm_grad = total(back_part[:rows], back_got)
    middle_grad = norm_back(back_norm_grad * back_gain, back_xhat, back_inverse)
    front_branch = (gated + middle_grad).astype(narrow)
    out_part = matmul(after(front_branch, back_act), back_shrink).astype(narrow)
    branch_got, out_part = lax.optimization_barrier((swap(front_branch, "y2"), out_part))
    front_branches = jnp.concatenate([front_branch, branch_got], 0)
    front_pre_grads = [
        (slope * matmul_right(front_branches, shrink)).astype(narrow)
        for slope, shrink in zip(front_slopes, front_shrinks)
    ]
    front_part = sum(matmul(grad, expand) for grad, expand in zip(front_pre_grads, front_expands))
    front_low = front_part[rows:].astype(narrow)
    front_acts = after(front_low, *front_acts)
    front_shrink_part = [matmul_left(act, front_branches).astype(narrow) for act in front_acts]
    front_got, out_got, front_shrink_part = lax.optimization_barrier(
        (swap(front_low, "y2"), return_four(out_part), front_shrink_part)
    )
    front_shrink_part = [reduced(part, "x") for part in front_shrink_part]
    front_norm_grad = front_part[:rows] + front_got.astype(wide)
    first_grad = norm_back(front_norm_grad * front_gain, front_xhat, front_inverse)
    branches = front_out + total(out_part[:rows], out_got) + back_offset
    logit_grad = jnp.sum(ct_rows * branches, -1, keepdims=True) * gate * (1.0 - gate)
    sent_grad = (logit_grad * centre + middle_grad + first_grad).astype(narrow)

    sent_blocks = pack_back(sent_grad)
    normed_late, *front_pre_late = after(sent_blocks, front_normed, *front_pre_grads)
    front_expand_part = [matmul_left(grad, normed_late).astype(narrow) for grad in front_pre_late]
    sent_blocks, front_expand_part, back_grads = lax.optimization_barrier(
        (exchange(sent_blocks, GROUP), front_expand_part, back_grads)
    )
    front_expand_part = [reduced(part, "x") for part in front_expand_part]
    getter = (send_index[:, None] == jnp.arange(slots)[None, :]).astype(narrow)
    hidden_grad, context_grad, out_low = hidden_back(
        sent_blocks.reshape(slots, width), getter, cotangent, outmat
    )
    grads = exchange(context_grad, GROUP)
    context, out_late = after(context_grad, context, out_low)
    out_part = matmul_left(context, out_late).astype(narrow).reshape(experts, 128, width)
    grads, out_part = lax.optimization_barrier((grads, out_part))
    out_part = exchange(out_part, GROUP)
    grads, xhat_all, front_shrink_part = lax.optimization_barrier((grads, xhat_all, front_shrink_part))

    dqkv, three, sums = attend_back(low, qkv, grads, full, lse, segcol, segrow, xhat_all)

    out_part = jnp.sum(out_part.astype(wide), 0).astype(narrow).reshape(16, 8, 8, 128)
    biases = jnp.concatenate(
        [
            sums.reshape(16, 24),
            jnp.sum(out_low.astype(wide), 0).reshape(16, 64),
        ],
        1,
    ).astype(narrow)
    expert_sums = jnp.stack(
        [
            jnp.sum(front_norm_grad * front_xhat, 0),
            jnp.sum(front_norm_grad, 0),
            jnp.sum(front_branch.astype(wide), 0),
            jnp.sum(back_norm_grad * back_xhat, 0),
            jnp.sum(back_norm_grad, 0),
            jnp.sum(back_branch.astype(wide), 0),
            jnp.sum(logit_grad * stream, 0),
        ]
    ).reshape(7, 16, 64)
    front_lifts = jnp.stack([jnp.sum(grad.astype(wide), 0).reshape(4, 256) for grad in front_pre_late], 1)
    front_lifts = jnp.where(y1_at == 0, front_lifts, front_lifts[:, ::-1])
    front_lifts = jnp.where(jnp.arange(2)[:, None] == y2_at, front_lifts[:, :, None], 0.0)
    back_lifts = jnp.sum(back_pre_late.astype(wide), 0).reshape(1, 4, 256)
    back_lifts = jnp.where(jnp.arange(4)[:, None, None] == x_at, back_lifts, 0.0)
    packed = jnp.concatenate(
        [
            jnp.transpose(expert_sums, (1, 0, 2)).reshape(16, 448),
            front_lifts.reshape(16, 256),
            back_lifts.reshape(16, 256),
            jnp.zeros((16, 64), wide),
        ],
        1,
    )
    slices = jnp.concatenate(
        [
            three,
            jnp.transpose(out_part, (0, 2, 1, 3)).reshape(16, 64, 128),
            jnp.pad(biases[:, None], ((0, 0), (0, 7), (0, 40))),
            packed.reshape(16, 8, 128).astype(narrow),
        ],
        1,
    )
    front_swap = swap(front_shrink_part[1], "y1")
    slices, front_swap, front_expand_part = lax.optimization_barrier(
        (exchange(slices, DATA), front_swap, front_expand_part)
    )
    slices = jnp.sum(slices.astype(wide), 0)
    summed = slices[264:].reshape(1, 1024)
    slices = slices[:264].astype(narrow)
    everything = lax.all_gather(slices, EVERY, axis=0).reshape(16, 8, 264, 128)
    biases = everything[:, :, 256, :88].astype(wide)
    outbias_grad = jnp.sum(biases[:, :, 24:], 1).reshape(width)
    biases = jnp.transpose(biases[:, :, :24], (1, 0, 2)).reshape(8, 3, 128)
    biases = jnp.transpose(biases, (1, 0, 2)).reshape(3, width)
    query_grad, key_grad, value_grad, outmat_grad, vectors = unpack(
        everything, biases, attngain.reshape(16, 64, 1), attnshift.reshape(16, 64, 1),
        querymat, keymat, valuemat,
    )
    outmat_grad = outmat_grad.reshape(width, width)
    attngain_grad, attnshift_grad = vectors[:, :, 0].reshape(width), vectors[:, :, 1].reshape(width)
    querybias_grad, _, valuebias_grad = biases

    dqkv, returned, front_expand_own, other = after(
        slices, dqkv, pack_back((gate * branches).astype(narrow)), *front_expand_part
    )
    own, returned, other = lax.optimization_barrier(
        (exchange(dqkv, GROUP), exchange(returned, GROUP), swap(other, "y1"))
    )
    own = jnp.transpose(own.reshape(experts, rows, 3, 128), (2, 1, 0, 3))
    dquery, dkey, dvalue = (own[i].reshape(rows, width) for i in range(3))
    attn_norm_grad = (
        matmul_right(dquery, querymat) + matmul_right(dkey, keymat) + matmul_right(dvalue, valuemat)
    )
    attn_xhat, attn_inverse = norm_parts(tokens.astype(wide))
    tokens_grad = hidden_grad + norm_back(
        attn_norm_grad * attngain.astype(wide), attn_xhat, attn_inverse
    )
    result = (hidden + unpack_back(returned)).astype(narrow)
    back_shrink_grad, back_expand_grad = (grad.astype(wide) for grad in back_grads)
    front_shrink_grad = front_shrink_part[0].astype(wide) + front_swap.astype(wide)
    front_expand_grad = front_expand_own.astype(wide) + other.astype(wide)
    back_shrink_grad, front_shrink_grad = back_shrink_grad[None], front_shrink_grad[None]
    back_expand_grad, front_expand_grad = back_expand_grad.T[None], front_expand_grad.T[None]
    (
        front_gain_grad, front_shift_grad, front_offset_grad,
        back_gain_grad, back_shift_grad, back_offset_grad, centroid_grad,
    ) = (summed[:, i * 64 : i * 64 + 64] for i in range(7))
    front_lift_grad, back_lift_grad = summed[:, 448:704], summed[:, 704:960]

    return (
        result, tokens_grad, attngain_grad, attnshift_grad,
        query_grad, querybias_grad, key_grad, value_grad, valuebias_grad, outmat_grad, outbias_grad,
        front_gain_grad, front_shift_grad, front_expand_grad, front_lift_grad,
        front_shrink_grad, front_offset_grad,
        back_gain_grad, back_shift_grad, back_expand_grad, back_lift_grad,
        back_shrink_grad, back_offset_grad, centroid_grad,
    )


def solution(mesh):
    grid = Mesh(mesh.devices.reshape(4, 2, 2, 4, 2), EVERY)
    rows, plan, full = P(EVERY, None), P(DATA, GROUP), P()
    vector, expand, shrink = P(GROUP, DATA), P(GROUP, None, DATA), P(GROUP, DATA, None)
    sublayer = (vector, vector, expand, vector, shrink, vector)
    return jax.shard_map(
        per_device,
        mesh=grid,
        in_specs=(rows, rows, plan, plan) + (full,) * 9 + sublayer * 2 + (vector,),
        out_specs=(rows, rows) + (full,) * 9 + sublayer * 2 + (vector,),
        check_vma=False,
    )
```

```python
import jax
import jax.numpy as jnp
from jax import lax
from jax.experimental import pallas as pl
from jax.experimental.pallas import tpu as pltpu
from jax.sharding import Mesh, PartitionSpec as P

HEADS = 16
HEAD_DIM = 64
EPSILON = 1e-05
MASKED = -1e30

GROUP = ("z", "c")
DATA = ("x", "y1", "y2")
COLUMN = ("y1", "y2")
EVERY = DATA + GROUP

wide = jnp.float32
narrow = jnp.bfloat16


def matmul(left, right):
    return jnp.dot(left, right, preferred_element_type=wide)


def matmul_left(left, right):
    return lax.dot_general(left, right, (((0,), (0,)), ((), ())), preferred_element_type=wide)


def matmul_right(left, right):
    return lax.dot_general(left, right, (((1,), (1,)), ((), ())), preferred_element_type=wide)


def norm_parts(stream):
    center = stream - jnp.mean(stream, -1, keepdims=True)
    inverse = lax.rsqrt(jnp.mean(center * center, -1, keepdims=True) + EPSILON)
    return center * inverse, inverse


def norm_back(scaled, xhat, inverse):
    return (
        scaled
        - jnp.mean(scaled, -1, keepdims=True)
        - xhat * jnp.mean(scaled * xhat, -1, keepdims=True)
    ) * inverse


def gelu_pair(value):
    cdf = 0.5 + 0.5 * lax.erf(value * (0.5**0.5))
    pdf = jnp.exp(-0.5 * value * value) * 0.3989422804014327
    return value * cdf, cdf + value * pdf


def swap(value, axis):
    return lax.ppermute(value, axis, [(0, 1), (1, 0)])


def shift_by(value, step):
    return lax.ppermute(value, COLUMN, [(i, (i + step) % 4) for i in range(4)])


def share_four(rows):
    return [rows] + [shift_by(rows, step) for step in (1, 3, 2)]


def return_four(parts):
    return [shift_by(part, step) for part, step in zip(parts[1:], (3, 1, 2))]


def total(own, got):
    return own.astype(wide) + sum(part.astype(wide) for part in got)


def after(first, *later):
    later = lax.optimization_barrier((first,) + later)[1:]
    return later if len(later) > 1 else later[0]


def exchange(blocks, axes):
    return lax.all_to_all(blocks, axes, 0, 0, tiled=True)


def to_everyone(block, axes, count):
    return exchange(jnp.broadcast_to(block[None], (count,) + block.shape), axes)


def head_rows(matrix, head):
    rows = lax.broadcasted_iota(jnp.int32, matrix.shape, 0) // HEAD_DIM
    return jnp.where(rows == head, matrix, jnp.zeros_like(matrix))


def head_lanes(matrix, head):
    lanes = lax.broadcasted_iota(jnp.int32, matrix.shape, 1) // HEAD_DIM
    return jnp.where(lanes == head, matrix, jnp.zeros_like(matrix))


def turn(matrix):
    return jnp.transpose(matrix.astype(wide), (1, 0)).astype(matrix.dtype)


def mask_of(segcol_ref, segrow_ref, i, j, diagonal):
    same = segcol_ref[j] == segrow_ref[i]
    if diagonal:
        size = same.shape
        same = same & (
            lax.broadcasted_iota(jnp.int32, size, 0) <= lax.broadcasted_iota(jnp.int32, size, 1)
        )
    return same


EXPAND = pl.BlockSpec((1, 256, 1024), lambda k: (k, 0, 0))
SHRINK = pl.BlockSpec((1, 256, 1024), lambda k: (k, 1, 0))
COLUMNS = pl.BlockSpec((256, 256), lambda k: (0, k))
WHOLE = pl.BlockSpec((256, 1024), lambda k: (0, 0))
LINE = pl.BlockSpec((1, 1024), lambda k: (0, 0))
LIFT = pl.BlockSpec((1, 256), lambda k: (0, k))


def first_step(run):
    pl.when(pl.program_id(0) == 0)(run)


def add_up(acc_ref, part_ref, part):
    k = pl.program_id(0)

    @first_step
    def _():
        acc_ref[...] = part

    @pl.when(k > 0)
    def _():
        acc_ref[...] += part

    @pl.when(k == pl.num_programs(0) - 1)
    def _():
        part_ref[...] = acc_ref[...].astype(part_ref.dtype)


def expert_call(kernel, name, in_specs, out_specs, outs, kept, accs, *args):
    return pl.pallas_call(
        kernel,
        grid=(4,),
        out_shape=[
            pltpu.HBM((256, 1024), dtype) if i < kept else jax.ShapeDtypeStruct((256, 1024), dtype)
            for i, dtype in enumerate(outs)
        ],
        in_specs=in_specs,
        out_specs=out_specs,
        scratch_shapes=[pltpu.VMEM((256, 1024), wide)] * accs,
        compiler_params=pltpu.CompilerParams(vmem_limit_bytes=16 << 20),
        name=name,
    )(*args)


def front_forward_kernel(
    xhat_ref, gain_ref, shift_ref, lift_a_ref, lift_b_ref,
    expand_a_ref, shrink_a_ref, expand_b_ref, shrink_b_ref,
    act_a_ref, act_b_ref, slope_a_ref, slope_b_ref, rows_ref, part_ref, acc_ref,
):
    @first_step
    def _():
        rows = xhat_ref[...].astype(wide) * gain_ref[...] + shift_ref[...]
        rows_ref[...] = rows.astype(narrow)

    part = 0.0
    for lift_ref, expand_ref, shrink_ref, act_ref, slope_ref in (
        (lift_a_ref, expand_a_ref, shrink_a_ref, act_a_ref, slope_a_ref),
        (lift_b_ref, expand_b_ref, shrink_b_ref, act_b_ref, slope_b_ref),
    ):
        act, slope = gelu_pair(matmul_right(rows_ref[...], expand_ref[0]) + lift_ref[...])
        act = act.astype(narrow)
        act_ref[...] = act
        slope_ref[...] = slope
        part = part + matmul(act, shrink_ref[0])
    add_up(acc_ref, part_ref, part)


def front_forward(xhat, gain, shift, lifts, mats, last):
    return expert_call(
        front_forward_kernel, "front_forward",
        [WHOLE, LINE, LINE, LIFT, LIFT, EXPAND, SHRINK, EXPAND, SHRINK],
        [COLUMNS] * 4 + [WHOLE] * 2, [narrow, narrow, wide, wide, narrow, last], 5, 1,
        xhat, gain, shift, lifts[0], lifts[1], mats[0], mats[0], mats[1], mats[1],
    )


def front_backward_kernel(
    rows_ref, slope_a_ref, slope_b_ref, expand_a_ref, shrink_a_ref, expand_b_ref, shrink_b_ref,
    grad_a_ref, grad_b_ref, part_ref, acc_ref,
):
    part = 0.0
    for slope_ref, expand_ref, shrink_ref, grad_ref in (
        (slope_a_ref, expand_a_ref, shrink_a_ref, grad_a_ref),
        (slope_b_ref, expand_b_ref, shrink_b_ref, grad_b_ref),
    ):
        grad = (slope_ref[...] * matmul_right(rows_ref[...], shrink_ref[0])).astype(narrow)
        grad_ref[...] = grad
        part = part + matmul(grad, expand_ref[0])
    add_up(acc_ref, part_ref, part)


def front_backward(rows, slopes, mats, last):
    return expert_call(
        front_backward_kernel, "front_backward",
        [WHOLE, COLUMNS, COLUMNS, EXPAND, SHRINK, EXPAND, SHRINK],
        [COLUMNS] * 2 + [WHOLE], [narrow, narrow, last], 2, 1,
        rows, pinned(slopes[0]), pinned(slopes[1]), mats[0], mats[0], mats[1], mats[1],
    )


def back_kernel(
    rows_ref, branch_ref, lift_ref, expand_ref, shrink_ref,
    act_ref, grad_ref, part_ref, out_ref, part_acc_ref, out_acc_ref,
):
    act, slope = gelu_pair(matmul_right(rows_ref[...], expand_ref[0]) + lift_ref[...])
    act = act.astype(narrow)
    act_ref[...] = act
    grad = (slope * matmul_right(branch_ref[...], shrink_ref[0])).astype(narrow)
    grad_ref[...] = grad
    add_up(part_acc_ref, part_ref, matmul(grad, expand_ref[0]))
    add_up(out_acc_ref, out_ref, matmul(act, shrink_ref[0]))


def back_both(rows, branch, lift, mats, last):
    return expert_call(
        back_kernel, "back_both", [WHOLE, WHOLE, LIFT, EXPAND, SHRINK],
        [COLUMNS] * 2 + [WHOLE] * 2, [narrow, narrow, last, last], 2, 2,
        rows, branch, lift, mats, mats,
    )


def mat_grads_kernel(count, sides, *refs):
    lefts, rights, out_ref = refs[: count * sides], refs[count * sides : -2], refs[-2]
    for side in range(sides):
        side_lefts = [lefts[side * count + i][...] for i in range(count)]
        part = sum(matmul_left(left, right[...]) for left, right in zip(side_lefts, rights))
        out_ref[0, side] = part.astype(narrow)
        line = sum(jnp.sum(left.astype(wide), 0, keepdims=True) for left in side_lefts)
        refs[-1][0, side] = jnp.broadcast_to(line, (8, 256))


def mat_grads(lefts, rights):
    count, sides = len(rights), len(lefts)
    return pl.pallas_call(
        lambda *refs: mat_grads_kernel(count, sides, *refs),
        grid=(4,),
        out_shape=(
            pltpu.HBM((4, sides, 256, 1024), narrow),
            jax.ShapeDtypeStruct((4, sides, 8, 256), wide),
        ),
        in_specs=[COLUMNS] * (count * sides) + [WHOLE] * count,
        out_specs=(
            pl.BlockSpec((1, sides, 256, 1024), lambda k: (k, 0, 0, 0)),
            pl.BlockSpec((1, sides, 8, 256), lambda k: (k, 0, 0, 0)),
        ),
        compiler_params=pltpu.CompilerParams(vmem_limit_bytes=14 << 20),
        name="mat_grads",
    )(*(pinned(part) for side in lefts for part in side), *rights)


def sums_kernel(
    front_grad_ref, front_xhat_ref, front_branch_ref, back_grad_ref, back_xhat_ref, back_branch_ref,
    logit_grad_ref, stream_ref, out_ref,
):
    front_grad, back_grad = front_grad_ref[...], back_grad_ref[...]
    lines = (
        front_grad * front_xhat_ref[...], front_grad, front_branch_ref[...].astype(wide),
        back_grad * back_xhat_ref[...], back_grad, back_branch_ref[...].astype(wide),
        logit_grad_ref[...] * stream_ref[...],
    )
    for i, line in enumerate(lines):
        out_ref[i : i + 1, :] = jnp.sum(line, 0, keepdims=True)
    out_ref[7:8, :] = jnp.zeros_like(out_ref[7:8, :])


def row_sums(*args):
    return pl.pallas_call(
        sums_kernel,
        out_shape=jax.ShapeDtypeStruct((8, 1024), wide),
        compiler_params=pltpu.CompilerParams(vmem_limit_bytes=12 << 20),
        name="row_sums",
    )(*args)


def turn_kernel(in_ref, out_ref):
    out_ref[...] = turn(in_ref[...])


def turned(matrix):
    return pl.pallas_call(
        turn_kernel, out_shape=jax.ShapeDtypeStruct(matrix.shape[::-1], matrix.dtype), name="turned"
    )(matrix)


def pinned(value):
    return pltpu.with_memory_space_constraint(value, pltpu.HBM)


def project_kernel(
    tokens_ref, gain_ref, shift_ref, query_ref, key_ref, value_ref, query_bias_ref, value_bias_ref,
    out_ref, xhat_ref, normed_ref,
):
    @pl.when(pl.program_id(0) == 0)
    def _():
        xhat, _ = norm_parts(tokens_ref[...].astype(wide))
        xhat_ref[...] = xhat.astype(narrow)
        normed = xhat * gain_ref[...].astype(wide) + shift_ref[...].astype(wide)
        normed_ref[...] = normed.astype(narrow)

    normed = normed_ref[...]
    query = matmul(normed, query_ref[...]) + query_bias_ref[...].astype(wide)
    value = matmul(normed, value_ref[...]) + value_bias_ref[...].astype(wide)
    out_ref[0, :, 0:128] = query.astype(narrow)
    out_ref[0, :, 128:256] = matmul(normed, key_ref[...]).astype(narrow)
    out_ref[0, :, 256:384] = value.astype(narrow)


def project(tokens, gain, shift, querymat, querybias, keymat, valuemat, valuebias):
    rows, width = tokens.shape
    all_rows = pl.BlockSpec((rows, width), lambda e: (0, 0))
    line = pl.BlockSpec((1, width), lambda e: (0, 0))
    mat, bias = pl.BlockSpec((width, 128), lambda e: (0, e)), pl.BlockSpec((1, 128), lambda e: (0, e))
    return pl.pallas_call(
        project_kernel,
        grid=(8,),
        out_shape=(
            jax.ShapeDtypeStruct((8, rows, 384), narrow),
            jax.ShapeDtypeStruct((rows, width), narrow),
        ),
        in_specs=[all_rows, line, line, mat, mat, mat, bias, bias],
        out_specs=(pl.BlockSpec((1, rows, 384), lambda e: (e, 0, 0)), all_rows),
        scratch_shapes=[pltpu.VMEM((rows, width), narrow)],
        compiler_params=pltpu.CompilerParams(vmem_limit_bytes=8 << 20),
        name="project",
    )(tokens, gain, shift, pinned(querymat), pinned(keymat), pinned(valuemat), querybias, valuebias)


def join_kernel(ctx_ref, outmat_ref, tokens_ref, bias_ref, sender_ref, hidden_ref, packed_ref, context_ref):
    @pl.when(pl.program_id(0) == 0)
    def _():
        for e in range(8):
            context_ref[:, e * 128 : e * 128 + 128] = ctx_ref[e]

    hidden = tokens_ref[...].astype(wide) + bias_ref[...].astype(wide)
    hidden = hidden + matmul(context_ref[...], outmat_ref[...])
    hidden_ref[...] = hidden
    packed_ref[...] = matmul(sender_ref[...], hidden.astype(narrow)).astype(narrow)


def join(ctx, outmat, tokens, outbias, sender):
    rows, width = tokens.shape
    slots = sender.shape[0]
    strip = lambda height: pl.BlockSpec((height, 256), lambda n: (0, n))
    return pl.pallas_call(
        join_kernel,
        grid=(4,),
        out_shape=(
            jax.ShapeDtypeStruct((rows, width), wide),
            jax.ShapeDtypeStruct((slots, width), narrow),
            jax.ShapeDtypeStruct((rows, width), narrow),
        ),
        in_specs=[
            pl.BlockSpec((8, rows, 128), lambda n: (0, 0, 0)),
            strip(width), strip(rows), strip(1),
            pl.BlockSpec((slots, rows), lambda n: (0, 0)),
        ],
        out_specs=(strip(rows), strip(slots), pl.BlockSpec((rows, width), lambda n: (0, 0))),
        compiler_params=pltpu.CompilerParams(vmem_limit_bytes=10 << 20),
        name="join",
    )(ctx, outmat, tokens, outbias, sender)


def hidden_back_kernel(blocks_ref, getter_ref, cotangent_ref, outmat_ref, hidden_ref, grads_ref, low_ref):
    @pl.when(pl.program_id(0) == 0)
    def _():
        hidden = cotangent_ref[...].astype(wide) + matmul(getter_ref[...], blocks_ref[...])
        hidden_ref[...] = hidden
        low_ref[...] = hidden.astype(narrow)

    grads = matmul_right(low_ref[...], outmat_ref[...]).astype(narrow)
    grads_ref[0] = grads[:, 0:128]
    grads_ref[1] = grads[:, 128:256]


def hidden_back(blocks, getter, cotangent, outmat):
    rows, width = cotangent.shape
    slots = getter.shape[1]
    all_rows = pl.BlockSpec((rows, width), lambda e: (0, 0))
    return pl.pallas_call(
        hidden_back_kernel,
        grid=(4,),
        out_shape=(
            jax.ShapeDtypeStruct((rows, width), wide),
            jax.ShapeDtypeStruct((8, rows, 128), narrow),
            jax.ShapeDtypeStruct((rows, width), narrow),
        ),
        in_specs=[
            pl.BlockSpec((slots, width), lambda e: (0, 0)),
            pl.BlockSpec((rows, slots), lambda e: (0, 0)),
            all_rows,
            pl.BlockSpec((256, width), lambda e: (e, 0)),
        ],
        out_specs=(all_rows, pl.BlockSpec((2, rows, 128), lambda e: (e, 0, 0)), all_rows),
        compiler_params=pltpu.CompilerParams(vmem_limit_bytes=12 << 20),
        name="hidden_back",
    )(blocks, getter, cotangent, outmat)


def attend_kernel(low_ref, qkv_ref, segcol_ref, segrow_ref, ctx_ref, full_ref, lse_ref, vals_ref):
    blocks, size, _ = qkv_ref.shape
    for j in range(blocks):
        turned = turn(qkv_ref[j, :, 256:384])
        for head in range(2):
            vals_ref[j, head, 0:64, :] = turned[head * 64 : head * 64 + 64]
            vals_ref[j, head, 64:80, :] = jnp.ones((16, size), narrow)
    for i in range(blocks):
        query = turn((qkv_ref[i, :, 0:128].astype(wide) * HEAD_DIM**-0.5).astype(narrow))
        queries = [head_rows(query, head) for head in range(2)]

        def step(j, carry, diagonal):
            keys = qkv_ref[j, :, 128:256]
            mask = mask_of(segcol_ref, segrow_ref, i, j, diagonal)
            out = []
            for head in range(2):
                scores = jnp.where(mask, matmul(keys, queries[head]), MASKED)
                top = jnp.max(scores, 0, keepdims=True)
                if carry is not None:
                    top = jnp.maximum(top, carry[2 * head])
                probs = jnp.exp(scores - top).astype(narrow)
                total = matmul(vals_ref[j, head], probs)
                if carry is not None:
                    total = total + carry[2 * head + 1] * jnp.exp(carry[2 * head] - top)
                out += [top, total]
            return tuple(out)

        carry = step(i, None, True)
        if i > 0:
            carry = lax.fori_loop(low_ref[i], i, lambda j, c: step(j, c, False), carry)
        parts = []
        for head in range(2):
            top, total = carry[2 * head], carry[2 * head + 1]
            parts.append(total[0:64] / total[64:65])
            lse_ref[i, head : head + 1, :] = top + jnp.log(total[64:65])
        full = jnp.concatenate(parts, 0)
        full_ref[i] = full
        ctx_ref[i] = jnp.transpose(full, (1, 0)).astype(narrow)


def attend(low, qkv, segcol, segrow):
    blocks, size, _ = qkv.shape
    vmem = pl.BlockSpec(memory_space=pltpu.VMEM)
    return pl.pallas_call(
        attend_kernel,
        out_shape=(
            jax.ShapeDtypeStruct((blocks, size, 128), narrow),
            jax.ShapeDtypeStruct((blocks, 128, size), wide),
            jax.ShapeDtypeStruct((blocks, 8, size), wide),
        ),
        in_specs=[pl.BlockSpec(memory_space=pltpu.SMEM), vmem, vmem, vmem],
        out_specs=(vmem, vmem, vmem),
        scratch_shapes=[pltpu.VMEM((blocks, 2, 80, size), narrow)],
        compiler_params=pltpu.CompilerParams(vmem_limit_bytes=12 << 20),
        name="attend",
    )(low, qkv, segcol, segrow)


def attend_back_kernel(
    low_ref, qkv_ref, grad_ref, full_ref, lse_ref, segcol_ref, segrow_ref, xhat_ref,
    out_ref, three_ref, sums_ref, keys_ref, dk_ref, dv_ref, held_ref, sem_ref,
):
    fetch = pltpu.make_async_copy(xhat_ref, held_ref, sem_ref)
    fetch.start()
    blocks, size, _ = qkv_ref.shape
    for j in range(blocks):
        keys_ref[j] = turn(qkv_ref[j, :, 128:256])
    dk_ref[...] = jnp.zeros_like(dk_ref)
    dv_ref[...] = jnp.zeros_like(dv_ref)
    for i in range(blocks):
        query = (qkv_ref[i, :, 0:128].astype(wide) * HEAD_DIM**-0.5).astype(narrow)
        query_t = turn(query)
        grad = grad_ref[i]
        grad_t = turn(grad)
        inner = grad_t.astype(wide) * full_ref[i]
        queries_t = [head_rows(query_t, head) for head in range(2)]
        grads_t = [head_rows(grad_t, head) for head in range(2)]
        inners = [
            jnp.sum(inner[head * 64 : head * 64 + 64], 0, keepdims=True) for head in range(2)
        ]
        lses = [lse_ref[i, head : head + 1, :] for head in range(2)]
        query_pair = jnp.concatenate([head_lanes(query, head) for head in range(2)], 0)
        grad_pair = jnp.concatenate([head_lanes(grad, head) for head in range(2)], 0)

        def step(j, carry, diagonal):
            keys = qkv_ref[j, :, 128:256]
            vals = qkv_ref[j, :, 256:384]
            mask = mask_of(segcol_ref, segrow_ref, i, j, diagonal)
            lows, score_lows, out = [], [], []
            for head in range(2):
                scores = matmul(keys, queries_t[head])
                probs = jnp.where(mask, jnp.exp(scores - lses[head]), 0.0)
                prob_grad = matmul(vals, grads_t[head])
                score_low = (probs * (prob_grad - inners[head])).astype(narrow)
                lows.append(probs.astype(narrow))
                score_lows.append(score_low)
                part = matmul(keys_ref[j, head * 64 : head * 64 + 64, :], score_low)
                out.append(part if carry is None else carry[head] + part)
            dv_ref[j] += matmul(jnp.concatenate(lows, 1), grad_pair)
            dk_ref[j] += matmul(jnp.concatenate(score_lows, 1), query_pair)
            return tuple(out)

        carry = step(i, None, True)
        if i > 0:
            carry = lax.fori_loop(low_ref[i], i, lambda j, c: step(j, c, False), carry)
        dq = jnp.concatenate(carry, 0) * HEAD_DIM**-0.5
        out_ref[i, :, 0:128] = jnp.transpose(dq, (1, 0)).astype(narrow)
    for j in range(blocks):
        out_ref[j, :, 128:256] = dk_ref[j].astype(narrow)
        out_ref[j, :, 256:384] = dv_ref[j].astype(narrow)
    fetch.wait()
    for part in range(4):
        height = slice(part * 256, part * 256 + 256)
        three = sum(matmul(held_ref[j, height, :], out_ref[j]) for j in range(blocks))
        for d in range(4):
            for i in range(3):
                three_ref[part * 4 + d, i * 64 : i * 64 + 64, :] = three[
                    d * 64 : d * 64 + 64, i * 128 : i * 128 + 128
                ].astype(narrow)
    sums_ref[...] = sum(jnp.sum(out_ref[j].astype(wide), 0, keepdims=True) for j in range(blocks))


def attend_back(low, qkv, grad, full, lse, segcol, segrow, xhat):
    blocks, size, _ = qkv.shape
    vmem = pl.BlockSpec(memory_space=pltpu.VMEM)
    return pl.pallas_call(
        attend_back_kernel,
        out_shape=(
            jax.ShapeDtypeStruct((blocks, size, 384), narrow),
            jax.ShapeDtypeStruct((16, 192, 128), narrow),
            jax.ShapeDtypeStruct((1, 384), wide),
        ),
        in_specs=[pl.BlockSpec(memory_space=pltpu.SMEM)]
        + [vmem] * 6
        + [pl.BlockSpec(memory_space=pltpu.HBM)],
        out_specs=(vmem, vmem, vmem),
        scratch_shapes=[
            pltpu.VMEM((blocks, 128, size), narrow),
            pltpu.VMEM((blocks, size, 128), wide),
            pltpu.VMEM((blocks, size, 128), wide),
            pltpu.VMEM(xhat.shape, narrow),
            pltpu.SemaphoreType.DMA,
        ],
        compiler_params=pltpu.CompilerParams(vmem_limit_bytes=20 << 20),
        name="attend_back",
    )(low, qkv, grad, full, lse, segcol, segrow, xhat)


def unpack_kernel(
    all_ref, bias_ref, gain_ref, shift_ref, query_ref, key_ref, value_ref,
    dquery_ref, dkey_ref, dvalue_ref, dout_ref, vector_ref,
):
    mats = ((query_ref, dquery_ref), (key_ref, dkey_ref), (value_ref, dvalue_ref))
    for d in range(all_ref.shape[0]):
        height = slice(d * 64, d * 64 + 64)
        gain, shift = gain_ref[d].astype(wide), shift_ref[d].astype(wide)
        gain_sum = shift_sum = jnp.zeros((64, 128), wide)
        for e in range(8):
            lanes = slice(e * 128, e * 128 + 128)
            for i, (mat_ref, grad_ref) in enumerate(mats):
                part = all_ref[d, e, i * 64 : i * 64 + 64, :].astype(wide)
                bias = bias_ref[i : i + 1, lanes]
                mat = mat_ref[height, lanes].astype(wide)
                grad_ref[height, lanes] = gain * part + shift * bias
                gain_sum = gain_sum + mat * part
                shift_sum = shift_sum + mat * bias
            for i in range(8):
                dout_ref[e, d, :, i * 128 : i * 128 + 128] = all_ref[
                    d, e, 192 + i * 8 : 200 + i * 8, :
                ].astype(wide)
        vector_ref[d, :, 0:1] = jnp.sum(gain_sum, 1, keepdims=True)
        vector_ref[d, :, 1:2] = jnp.sum(shift_sum, 1, keepdims=True)


def unpack(everything, biases, gain, shift, querymat, keymat, valuemat, step=2):
    width = querymat.shape[0]
    column = pl.BlockSpec((step, 64, 1), lambda d: (d, 0, 0))
    strip = pl.BlockSpec((step * 64, width), lambda d: (d, 0))
    square = jax.ShapeDtypeStruct((width, width), wide)
    return pl.pallas_call(
        unpack_kernel,
        grid=(16 // step,),
        out_shape=(
            square, square, square,
            jax.ShapeDtypeStruct((8, 16, 8, width), wide),
            jax.ShapeDtypeStruct((16, 64, 2), wide),
        ),
        in_specs=[
            pl.BlockSpec((step, 8, 264, 128), lambda d: (d, 0, 0, 0)),
            pl.BlockSpec((3, width), lambda d: (0, 0)),
            column, column, strip, strip, strip,
        ],
        out_specs=(
            strip, strip, strip,
            pl.BlockSpec((8, step, 8, width), lambda d: (0, d, 0, 0)),
            pl.BlockSpec((step, 64, 2), lambda d: (d, 0, 0)),
        ),
        compiler_params=pltpu.CompilerParams(vmem_limit_bytes=14 << 20),
        name="unpack",
    )(everything, biases, gain, shift, querymat, keymat, valuemat)


def per_device(
    tokens, cotangent, segments, routes,
    attngain, attnshift, querymat, querybias, keymat, valuemat, valuebias, outmat, outbias,
    frontgain, frontshift, frontexpand, frontlift, frontreduce, frontoffset,
    backgain, backshift, backexpand, backlift, backreduce, backoffset, centroid,
):
    rows, width = tokens.shape
    experts = 8
    capacity = rows // experts + rows // (2 * experts)
    slots = experts * capacity
    mine = lax.axis_index(GROUP)
    y1_at, y2_at, y_at = (lax.axis_index(axis) for axis in ("y1", "y2", COLUMN))

    plans = to_everyone(jnp.concatenate([segments, routes], 0), GROUP, experts)
    small_own = jnp.concatenate(
        [
            frontgain[0], frontshift[0], frontoffset[0], backgain[0], backshift[0], backoffset[0],
            centroid[0], frontlift[0], backlift[0], jnp.zeros((64,), narrow),
        ]
    )
    small = small_own.reshape(8, 128)

    def reduced(matrix, axes):
        return lax.psum_scatter(matrix, axes, scatter_dimension=0, tiled=True)

    def gathered(matrix, axes):
        return lax.all_gather(matrix, axes, axis=0)

    front_own = jnp.concatenate([frontexpand[0].T, frontreduce[0]], 0)
    front_other = swap(front_own, "y1")
    front_mats = [gathered(front_own, "x")]

    route = routes[0]
    picks = (route[:, None] == jnp.arange(experts)[None, :]).astype(narrow)
    lower = (jnp.arange(rows)[:, None] > jnp.arange(rows)[None, :]).astype(narrow)
    rank = jnp.sum(matmul(lower, picks) * picks.astype(wide), 1).astype(jnp.int32)
    send_index = route * capacity + rank
    sender = (jnp.arange(slots)[:, None] == send_index[None, :]).astype(narrow)
    def pack(row_data):
        return matmul(sender, row_data).astype(narrow).reshape(experts, capacity, width)

    def unpack_rows(blocks):
        return matmul(taker, blocks.reshape(slots, width)).astype(narrow)

    def pack_back(row_data):
        return matmul_left(taker, row_data).astype(narrow).reshape(experts, capacity, width)

    def unpack_back(blocks):
        return matmul_left(sender, blocks.reshape(slots, width))

    line = lambda vector: vector.reshape(1, width)
    split, xhat_low = project(
        tokens, line(attngain), line(attnshift),
        querymat, line(querybias), keymat, valuemat, line(valuebias),
    )
    split, plans = lax.optimization_barrier((split, plans))
    seg_all, route_all = plans[:, 0], plans[:, 1]
    qkv = exchange(split, GROUP)
    xhat_turned = turned(xhat_low)
    qkv, xhat_turned = lax.optimization_barrier((qkv, xhat_turned))
    small = to_everyone(after(qkv, small), DATA, 16)
    front_other, back_own = after(qkv, front_other, jnp.concatenate([backexpand[0].T, backreduce[0]], 0))
    front_mats.append(gathered(front_other, "x"))
    back_mats = gathered(back_own, "x")
    counts = jnp.sum((route_all == mine).astype(jnp.int32), 1)
    ahead = jnp.arange(experts)[:, None] > jnp.arange(experts)[None, :]
    starts = jnp.sum(jnp.where(ahead, counts[None, :], 0), 1)
    place = jnp.arange(capacity)[None, :]
    spots = jnp.where(place < counts[:, None], starts[:, None] + place, -1).reshape(-1)
    taker = (jnp.arange(rows)[:, None] == spots[None, :]).astype(narrow)

    segcol, segrow = seg_all[:, :, None], seg_all[:, None, :]
    low = jnp.sum((seg_all[None, :, -1] < seg_all[:, None, 0]).astype(jnp.int32), 1)
    ctx, full, lse = attend(low, qkv, segcol, segrow)
    ctx, small, front_mats[0] = lax.optimization_barrier((ctx, small, front_mats[0]))
    small = small.reshape(16, 1024).astype(wide)
    front_gain, front_shift, front_offset, back_gain, back_shift, back_offset, centre = (
        small[:, i * 64 : i * 64 + 64].reshape(1, width) for i in range(7)
    )
    lifts = small[:, 448:960].reshape(4, 2, 2, 512)
    front_lift = lax.dynamic_index_in_dim(lifts, y2_at, 2, False)[:, :, :256]
    front_lift = jnp.where(y1_at == 0, front_lift, front_lift[:, ::-1])
    front_lift = jnp.transpose(front_lift, (1, 0, 2)).reshape(2, 1, 1024)
    back_lift = lax.dynamic_index_in_dim(lifts.reshape(4, 4, 512), y_at, 1, False)[:, 256:]
    back_lift = back_lift.reshape(1, 1024)
    hidden, blocks, context = join(exchange(ctx, GROUP), outmat, tokens, line(outbias), sender)

    blocks = exchange(blocks.reshape(experts, capacity, width), GROUP)
    stream = unpack_rows(blocks).astype(wide)
    front_xhat, front_inverse = norm_parts(stream)
    xhat_own = front_xhat.astype(narrow)
    ct_blocks = exchange(pack(after(xhat_own, cotangent)), GROUP)
    front_side = front_gain, front_shift, front_lift, [pinned(mats) for mats in front_mats]
    *own_acts, own_slope_a, own_slope_b, front_normed, own_part = front_forward(
        xhat_own, *front_side, wide
    )
    ct_blocks, own_part = lax.optimization_barrier((ct_blocks, own_part))
    gate = jax.nn.sigmoid(jnp.sum(stream * centre, -1, keepdims=True))
    ct_rows = unpack_rows(ct_blocks).astype(wide)
    gated = gate * ct_rows
    back_branch = gated.astype(narrow)
    xhat_got, back_branch, own_part = lax.optimization_barrier(
        (swap(xhat_own, "y2"), back_branch, own_part)
    )
    back_branches = share_four(back_branch)
    *got_acts, got_slope_a, got_slope_b, normed_got, got_part = front_forward(
        xhat_got, *front_side, narrow
    )
    got_part, *back_branches = lax.optimization_barrier((got_part, *back_branches))
    front_got = swap(got_part, "y2")
    front_out = own_part + front_got.astype(wide) + front_offset
    xhat_all = lax.all_gather(after(got_part, xhat_turned), GROUP, axis=0)
    middle = stream + front_out
    back_xhat, back_inverse = norm_parts(middle)
    back_normed = share_four((back_xhat * back_gain + back_shift).astype(narrow))
    back_results = [
        back_both(normed, branch, back_lift, back_mats, last)
        for normed, branch, last in zip(back_normed, back_branches, (wide, narrow, narrow, narrow))
    ]
    back_acts, back_pre_grads, back_parts, out_parts = map(list, zip(*back_results))
    back_late = after(back_parts[-1], *back_pre_grads)
    expand_part, back_lifts = mat_grads([back_late], back_normed)
    *back_got, expand_part, xhat_all = lax.optimization_barrier(
        (*return_four(back_parts), expand_part, xhat_all)
    )
    expand_grad = reduced(expand_part, "x")
    back_norm_grad = total(back_parts[0], back_got)
    middle_grad = norm_back(back_norm_grad * back_gain, back_xhat, back_inverse)
    front_branch = (gated + middle_grad).astype(narrow)
    back_acts = after(front_branch, *back_acts)
    shrink_part, _ = mat_grads([back_acts], back_branches)
    branch_got, shrink_part, *out_got = lax.optimization_barrier(
        (swap(front_branch, "y2"), shrink_part, *return_four(out_parts))
    )
    back_grads = [reduced(shrink_part, "x"), expand_grad]
    *got_pre_grads, got_part = front_backward(
        branch_got, (got_slope_a, got_slope_b), front_side[-1], narrow
    )
    *own_pre_grads, own_part = front_backward(
        front_branch, (own_slope_a, own_slope_b), front_side[-1], wide
    )
    late = after(got_part, *own_acts, *got_acts)
    front_shrink_part, _ = mat_grads(list(zip(late[:2], late[2:])), (front_branch, branch_got))
    front_got, front_shrink_part = lax.optimization_barrier((swap(got_part, "y2"), front_shrink_part))
    front_shrink_part = reduced(front_shrink_part, "x")
    front_norm_grad = own_part + front_got.astype(wide)
    first_grad = norm_back(front_norm_grad * front_gain, front_xhat, front_inverse)
    branches = front_out + total(out_parts[0], out_got) + back_offset
    logit_grad = jnp.sum(ct_rows * branches, -1, keepdims=True) * gate * (1.0 - gate)
    sent_grad = (logit_grad * centre + middle_grad + first_grad).astype(narrow)

    sent_blocks = pack_back(sent_grad)
    pre_late = after(sent_blocks, *own_pre_grads, *got_pre_grads)
    front_expand_part, front_lifts = mat_grads(
        list(zip(pre_late[:2], pre_late[2:])), (front_normed, normed_got)
    )
    sent_blocks, front_expand_part, back_grads = lax.optimization_barrier(
        (exchange(sent_blocks, GROUP), front_expand_part, back_grads)
    )
    front_expand_part = reduced(front_expand_part, "x")
    getter = (send_index[:, None] == jnp.arange(slots)[None, :]).astype(narrow)
    hidden_grad, context_grad, out_low = hidden_back(
        sent_blocks.reshape(slots, width), getter, cotangent, outmat
    )
    grads = exchange(context_grad, GROUP)
    expert_sums = row_sums(
        *after(
            context_grad, front_norm_grad, front_xhat, front_branch, back_norm_grad, back_xhat,
            back_branches[0], logit_grad, stream,
        )
    )[:7].reshape(7, 16, 64)
    context, out_late = after(context_grad, context, out_low)
    out_part = matmul_left(context, out_late).astype(narrow).reshape(experts, 128, width)
    grads, out_part, expert_sums = lax.optimization_barrier((grads, out_part, expert_sums))
    out_part = exchange(out_part, GROUP)
    grads, front_shrink_part = lax.optimization_barrier((grads, front_shrink_part))

    dqkv, three, sums = attend_back(low, qkv, grads, full, lse, segcol, segrow, xhat_all)

    out_part = jnp.sum(after(sums, out_part).astype(wide), 0).astype(narrow).reshape(16, 8, 8, 128)
    biases = jnp.concatenate(
        [
            sums.reshape(16, 24),
            jnp.sum(out_low.astype(wide), 0).reshape(16, 64),
        ],
        1,
    ).astype(narrow)
    front_lifts, back_lifts = front_lifts[:, :, 0], back_lifts[:, 0, 0]
    front_lifts = jnp.where(y1_at == 0, front_lifts, front_lifts[:, ::-1])
    front_lifts = jnp.where(jnp.arange(2)[:, None] == y2_at, front_lifts[:, :, None], 0.0)
    back_lifts = jnp.where(jnp.arange(4)[:, None] == y_at, back_lifts[:, None], 0.0)
    packed = jnp.concatenate(
        [
            jnp.transpose(expert_sums, (1, 0, 2)).reshape(16, 448),
            front_lifts.reshape(16, 256),
            back_lifts.reshape(16, 256),
            jnp.zeros((16, 64), wide),
        ],
        1,
    )
    slices = jnp.concatenate(
        [
            three,
            jnp.transpose(out_part, (0, 2, 1, 3)).reshape(16, 64, 128),
            jnp.pad(biases[:, None], ((0, 0), (0, 7), (0, 40))),
            packed.reshape(16, 8, 128).astype(narrow),
        ],
        1,
    )
    front_swap = swap(front_shrink_part[0, 1], "y1")
    slices, front_swap, front_expand_part = lax.optimization_barrier(
        (exchange(slices, DATA), front_swap, front_expand_part)
    )
    slices = jnp.sum(slices.astype(wide), 0)
    summed = slices[264:].reshape(1, 1024)
    slices = slices[:264].astype(narrow)
    everything = lax.all_gather(slices, EVERY, axis=0).reshape(16, 8, 264, 128)
    biases = everything[:, :, 256, :88].astype(wide)
    outbias_grad = jnp.sum(biases[:, :, 24:], 1).reshape(width)
    biases = jnp.transpose(biases[:, :, :24], (1, 0, 2)).reshape(8, 3, 128)
    biases = jnp.transpose(biases, (1, 0, 2)).reshape(3, width)
    query_grad, key_grad, value_grad, outmat_grad, vectors = unpack(
        everything, biases, attngain.reshape(16, 64, 1), attnshift.reshape(16, 64, 1),
        querymat, keymat, valuemat,
    )
    outmat_grad = outmat_grad.reshape(width, width)
    attngain_grad, attnshift_grad = vectors[:, :, 0].reshape(width), vectors[:, :, 1].reshape(width)
    querybias_grad, _, valuebias_grad = biases

    dqkv, returned, front_expand_own, other = after(
        slices, dqkv, pack_back((gate * branches).astype(narrow)), *front_expand_part[0]
    )
    own, returned, other = lax.optimization_barrier(
        (exchange(dqkv, GROUP), exchange(returned, GROUP), swap(other, "y1"))
    )
    own = jnp.transpose(own.reshape(experts, rows, 3, 128), (2, 1, 0, 3))
    dquery, dkey, dvalue = (own[i].reshape(rows, width) for i in range(3))
    attn_norm_grad = (
        matmul_right(dquery, querymat) + matmul_right(dkey, keymat) + matmul_right(dvalue, valuemat)
    )
    attn_xhat, attn_inverse = norm_parts(tokens.astype(wide))
    tokens_grad = hidden_grad + norm_back(
        attn_norm_grad * attngain.astype(wide), attn_xhat, attn_inverse
    )
    result = (hidden + unpack_back(returned)).astype(narrow)
    back_shrink_grad, back_expand_grad = (grad[0, 0].astype(wide) for grad in back_grads)
    front_shrink_grad = front_shrink_part[0, 0].astype(wide) + front_swap.astype(wide)
    front_expand_grad = front_expand_own.astype(wide) + other.astype(wide)
    back_shrink_grad, front_shrink_grad = back_shrink_grad[None], front_shrink_grad[None]
    back_expand_grad, front_expand_grad = back_expand_grad.T[None], front_expand_grad.T[None]
    (
        front_gain_grad, front_shift_grad, front_offset_grad,
        back_gain_grad, back_shift_grad, back_offset_grad, centroid_grad,
    ) = (summed[:, i * 64 : i * 64 + 64] for i in range(7))
    front_lift_grad, back_lift_grad = summed[:, 448:704], summed[:, 704:960]

    return (
        result, tokens_grad, attngain_grad, attnshift_grad,
        query_grad, querybias_grad, key_grad, value_grad, valuebias_grad, outmat_grad, outbias_grad,
        front_gain_grad, front_shift_grad, front_expand_grad, front_lift_grad,
        front_shrink_grad, front_offset_grad,
        back_gain_grad, back_shift_grad, back_expand_grad, back_lift_grad,
        back_shrink_grad, back_offset_grad, centroid_grad,
    )


def solution(mesh):
    grid = Mesh(mesh.devices.reshape(4, 2, 2, 4, 2), EVERY)
    rows, plan, full = P(EVERY, None), P(DATA, GROUP), P()
    vector, expand, shrink = P(GROUP, DATA), P(GROUP, None, DATA), P(GROUP, DATA, None)
    sublayer = (vector, vector, expand, vector, shrink, vector)
    return jax.shard_map(
        per_device,
        mesh=grid,
        in_specs=(rows, rows, plan, plan) + (full,) * 9 + sublayer * 2 + (vector,),
        out_specs=(rows, rows) + (full,) * 9 + sublayer * 2 + (vector,),
        check_vma=False,
    )
```

```python
import jax
import jax.numpy as jnp
from jax import lax
from jax.experimental import pallas as pl
from jax.experimental.pallas import tpu as pltpu
from jax.sharding import Mesh, PartitionSpec as P

HEADS = 16
HEAD_DIM = 64
EPSILON = 1e-05
MASKED = -1e30

GROUP = ("z", "c")
DATA = ("x", "y1", "y2")
COLUMN = ("y1", "y2")
EVERY = DATA + GROUP

wide = jnp.float32
narrow = jnp.bfloat16


def matmul(left, right):
    return jnp.dot(left, right, preferred_element_type=wide)


def matmul_left(left, right):
    return lax.dot_general(left, right, (((0,), (0,)), ((), ())), preferred_element_type=wide)


def matmul_right(left, right):
    return lax.dot_general(left, right, (((1,), (1,)), ((), ())), preferred_element_type=wide)


def norm_parts(stream):
    center = stream - jnp.mean(stream, -1, keepdims=True)
    inverse = lax.rsqrt(jnp.mean(center * center, -1, keepdims=True) + EPSILON)
    return center * inverse, inverse


def norm_back(scaled, xhat, inverse):
    return (
        scaled
        - jnp.mean(scaled, -1, keepdims=True)
        - xhat * jnp.mean(scaled * xhat, -1, keepdims=True)
    ) * inverse


def gelu_pair(value):
    cdf = 0.5 + 0.5 * lax.erf(value * (0.5**0.5))
    pdf = jnp.exp(-0.5 * value * value) * 0.3989422804014327
    return value * cdf, cdf + value * pdf


def swap(value, axis):
    return lax.ppermute(value, axis, [(0, 1), (1, 0)])


def shift_by(value, step):
    return lax.ppermute(value, COLUMN, [(i, (i + step) % 4) for i in range(4)])


def share_four(rows):
    return [rows] + [shift_by(rows, step) for step in (1, 3, 2)]


def return_four(parts):
    return [shift_by(part, step) for part, step in zip(parts[1:], (3, 1, 2))]


def total(own, got):
    return own.astype(wide) + sum(part.astype(wide) for part in got)


def after(first, *later):
    later = lax.optimization_barrier((first,) + later)[1:]
    return later if len(later) > 1 else later[0]


def exchange(blocks, axes):
    return lax.all_to_all(blocks, axes, 0, 0, tiled=True)


def to_everyone(block, axes, count):
    return exchange(jnp.broadcast_to(block[None], (count,) + block.shape), axes)


def head_rows(matrix, head):
    rows = lax.broadcasted_iota(jnp.int32, matrix.shape, 0) // HEAD_DIM
    return jnp.where(rows == head, matrix, jnp.zeros_like(matrix))


def head_lanes(matrix, head):
    lanes = lax.broadcasted_iota(jnp.int32, matrix.shape, 1) // HEAD_DIM
    return jnp.where(lanes == head, matrix, jnp.zeros_like(matrix))


def turn(matrix):
    return jnp.transpose(matrix.astype(wide), (1, 0)).astype(matrix.dtype)


def mask_of(segcol_ref, segrow_ref, i, j, diagonal):
    same = segcol_ref[j] == segrow_ref[i]
    if diagonal:
        size = same.shape
        same = same & (
            lax.broadcasted_iota(jnp.int32, size, 0) <= lax.broadcasted_iota(jnp.int32, size, 1)
        )
    return same


EXPAND = pl.BlockSpec((1, 256, 1024), lambda k: (k, 0, 0))
SHRINK = pl.BlockSpec((1, 256, 1024), lambda k: (k, 1, 0))
COLUMNS = pl.BlockSpec((256, 256), lambda k: (0, k))
WHOLE = pl.BlockSpec((256, 1024), lambda k: (0, 0))
LANES = pl.BlockSpec((256, 128), lambda k: (0, 0))
LINE = pl.BlockSpec((1, 1024), lambda k: (0, 0))
LIFT = pl.BlockSpec((1, 256), lambda k: (0, k))


def first_step(run):
    pl.when(pl.program_id(0) == 0)(run)


def add_up(acc_ref, part_ref, part):
    k = pl.program_id(0)

    @first_step
    def _():
        acc_ref[...] = part

    @pl.when(k > 0)
    def _():
        acc_ref[...] += part

    @pl.when(k == pl.num_programs(0) - 1)
    def _():
        part_ref[...] = acc_ref[...].astype(part_ref.dtype)


def expert_call(kernel, name, in_specs, out_specs, outs, kept, accs, *args):
    return pl.pallas_call(
        kernel,
        grid=(4,),
        out_shape=[
            pltpu.HBM((256, 1024), dtype)
            if i < kept
            else jax.ShapeDtypeStruct((256, 128 if spec is LANES else 1024), dtype)
            for i, (dtype, spec) in enumerate(zip(outs, out_specs))
        ],
        in_specs=in_specs,
        out_specs=out_specs,
        scratch_shapes=[pltpu.VMEM((256, 1024), wide)] * accs,
        compiler_params=pltpu.CompilerParams(vmem_limit_bytes=16 << 20),
        name=name,
    )(*args)


def front_forward_kernel(
    xhat_ref, gain_ref, shift_ref, lift_a_ref, lift_b_ref,
    expand_a_ref, shrink_a_ref, expand_b_ref, shrink_b_ref,
    act_a_ref, act_b_ref, slope_a_ref, slope_b_ref, rows_ref, part_ref, acc_ref,
):
    @first_step
    def _():
        rows = xhat_ref[...].astype(wide) * gain_ref[...] + shift_ref[...]
        rows_ref[...] = rows.astype(narrow)

    part = 0.0
    for lift_ref, expand_ref, shrink_ref, act_ref, slope_ref in (
        (lift_a_ref, expand_a_ref, shrink_a_ref, act_a_ref, slope_a_ref),
        (lift_b_ref, expand_b_ref, shrink_b_ref, act_b_ref, slope_b_ref),
    ):
        act, slope = gelu_pair(matmul_right(rows_ref[...], expand_ref[0]) + lift_ref[...])
        act = act.astype(narrow)
        act_ref[...] = act
        slope_ref[...] = slope
        part = part + matmul(act, shrink_ref[0])
    add_up(acc_ref, part_ref, part)


def front_forward(xhat, gain, shift, lifts, mats, last):
    return expert_call(
        front_forward_kernel, "front_forward",
        [WHOLE, LINE, LINE, LIFT, LIFT, EXPAND, SHRINK, EXPAND, SHRINK],
        [COLUMNS] * 4 + [WHOLE] * 2, [narrow, narrow, wide, wide, narrow, last], 5, 1,
        xhat, gain, shift, lifts[0], lifts[1], mats[0], mats[0], mats[1], mats[1],
    )


def front_backward_kernel(
    rows_ref, slope_a_ref, slope_b_ref, expand_a_ref, shrink_a_ref, expand_b_ref, shrink_b_ref,
    grad_a_ref, grad_b_ref, part_ref, acc_ref,
):
    part = 0.0
    for slope_ref, expand_ref, shrink_ref, grad_ref in (
        (slope_a_ref, expand_a_ref, shrink_a_ref, grad_a_ref),
        (slope_b_ref, expand_b_ref, shrink_b_ref, grad_b_ref),
    ):
        grad = (slope_ref[...] * matmul_right(rows_ref[...], shrink_ref[0])).astype(narrow)
        grad_ref[...] = grad
        part = part + matmul(grad, expand_ref[0])
    add_up(acc_ref, part_ref, part)


def front_backward(rows, slopes, mats, last):
    return expert_call(
        front_backward_kernel, "front_backward",
        [WHOLE, COLUMNS, COLUMNS, EXPAND, SHRINK, EXPAND, SHRINK],
        [COLUMNS] * 2 + [WHOLE], [narrow, narrow, last], 2, 1,
        rows, pinned(slopes[0]), pinned(slopes[1]), mats[0], mats[0], mats[1], mats[1],
    )


def back_kernel(
    rows_ref, branch_ref, lift_ref, expand_ref, shrink_ref,
    act_ref, grad_ref, part_ref, out_ref, dot_ref, part_acc_ref, out_acc_ref,
):
    act, slope = gelu_pair(matmul_right(rows_ref[...], expand_ref[0]) + lift_ref[...])
    act = act.astype(narrow)
    act_ref[...] = act
    grad = (slope * matmul_right(branch_ref[...], shrink_ref[0])).astype(narrow)
    grad_ref[...] = grad
    add_up(part_acc_ref, part_ref, matmul(grad, expand_ref[0]))
    add_up(out_acc_ref, out_ref, matmul(act, shrink_ref[0]))

    @pl.when(pl.program_id(0) == 3)
    def _():
        dot = jnp.sum(branch_ref[...].astype(wide) * out_acc_ref[...], 1, keepdims=True)
        dot_ref[...] = jnp.broadcast_to(dot, dot_ref.shape)


def back_both(rows, branch, lift, mats, last):
    return expert_call(
        back_kernel, "back_both", [WHOLE, WHOLE, LIFT, EXPAND, SHRINK],
        [COLUMNS] * 2 + [WHOLE] * 2 + [LANES], [narrow, narrow, last, last, wide], 2, 2,
        rows, branch, lift, mats, mats,
    )


def mat_grads_kernel(count, sides, *refs):
    lefts, rights = refs[: count * sides], refs[count * sides : -2]
    for side in range(sides):
        start = side * count if len(rights) > count else 0
        side_lefts = [left[...] for left in lefts[side * count : side * count + count]]
        side_rights = rights[start : start + count]
        part = sum(matmul_left(left, right[...]) for left, right in zip(side_lefts, side_rights))
        refs[-2][0, side] = part.astype(narrow)
        line = sum(jnp.sum(left.astype(wide), 0, keepdims=True) for left in side_lefts)
        refs[-1][0, side] = jnp.broadcast_to(line, (8, 256))


def mat_grads(lefts, *rights):
    count, sides = len(rights[0]), len(lefts)
    rights = [part for side in rights for part in side]
    return pl.pallas_call(
        lambda *refs: mat_grads_kernel(count, sides, *refs),
        grid=(4,),
        out_shape=(
            pltpu.HBM((4, sides, 256, 1024), narrow),
            jax.ShapeDtypeStruct((4, sides, 8, 256), wide),
        ),
        in_specs=[COLUMNS] * (count * sides) + [WHOLE] * len(rights),
        out_specs=(
            pl.BlockSpec((1, sides, 256, 1024), lambda k: (k, 0, 0, 0)),
            pl.BlockSpec((1, sides, 8, 256), lambda k: (k, 0, 0, 0)),
        ),
        compiler_params=pltpu.CompilerParams(vmem_limit_bytes=20 << 20),
        name="mat_grads",
    )(*(pinned(part) for side in lefts for part in side), *rights)


def sums_kernel(
    front_grad_ref, front_xhat_ref, front_branch_ref, back_grad_ref, back_xhat_ref, back_branch_ref,
    logit_grad_ref, stream_ref, out_ref,
):
    front_grad, back_grad = front_grad_ref[...], back_grad_ref[...]
    lines = (
        front_grad * front_xhat_ref[...], front_grad, front_branch_ref[...].astype(wide),
        back_grad * back_xhat_ref[...], back_grad, back_branch_ref[...].astype(wide),
        logit_grad_ref[...] * stream_ref[...],
    )
    for i, line in enumerate(lines):
        out_ref[i : i + 1, :] = jnp.sum(line, 0, keepdims=True)
    out_ref[7:8, :] = jnp.zeros_like(out_ref[7:8, :])


def row_sums(*args):
    return pl.pallas_call(
        sums_kernel,
        out_shape=jax.ShapeDtypeStruct((8, 1024), wide),
        compiler_params=pltpu.CompilerParams(vmem_limit_bytes=12 << 20),
        name="row_sums",
    )(*args)


def turn_kernel(in_ref, out_ref):
    out_ref[...] = turn(in_ref[...])


def turned(matrix):
    return pl.pallas_call(
        turn_kernel, out_shape=jax.ShapeDtypeStruct(matrix.shape[::-1], matrix.dtype), name="turned"
    )(matrix)


def pinned(value):
    return pltpu.with_memory_space_constraint(value, pltpu.HBM)


def project_kernel(
    tokens_ref, gain_ref, shift_ref, query_ref, key_ref, value_ref, query_bias_ref, value_bias_ref,
    out_ref, xhat_ref, normed_ref,
):
    @pl.when(pl.program_id(0) == 0)
    def _():
        xhat, _ = norm_parts(tokens_ref[...].astype(wide))
        xhat_ref[...] = xhat.astype(narrow)
        normed = xhat * gain_ref[...].astype(wide) + shift_ref[...].astype(wide)
        normed_ref[...] = normed.astype(narrow)

    normed = normed_ref[...]
    query = matmul(normed, query_ref[...]) + query_bias_ref[...].astype(wide)
    value = matmul(normed, value_ref[...]) + value_bias_ref[...].astype(wide)
    out_ref[0, :, 0:128] = query.astype(narrow)
    out_ref[0, :, 128:256] = matmul(normed, key_ref[...]).astype(narrow)
    out_ref[0, :, 256:384] = value.astype(narrow)


def project(tokens, gain, shift, querymat, querybias, keymat, valuemat, valuebias):
    rows, width = tokens.shape
    all_rows = pl.BlockSpec((rows, width), lambda e: (0, 0))
    line = pl.BlockSpec((1, width), lambda e: (0, 0))
    mat, bias = pl.BlockSpec((width, 128), lambda e: (0, e)), pl.BlockSpec((1, 128), lambda e: (0, e))
    return pl.pallas_call(
        project_kernel,
        grid=(8,),
        out_shape=(
            jax.ShapeDtypeStruct((8, rows, 384), narrow),
            jax.ShapeDtypeStruct((rows, width), narrow),
        ),
        in_specs=[all_rows, line, line, mat, mat, mat, bias, bias],
        out_specs=(pl.BlockSpec((1, rows, 384), lambda e: (e, 0, 0)), all_rows),
        scratch_shapes=[pltpu.VMEM((rows, width), narrow)],
        compiler_params=pltpu.CompilerParams(vmem_limit_bytes=8 << 20),
        name="project",
    )(tokens, gain, shift, pinned(querymat), pinned(keymat), pinned(valuemat), querybias, valuebias)


def join_kernel(ctx_ref, outmat_ref, tokens_ref, bias_ref, sender_ref, hidden_ref, packed_ref, context_ref):
    @pl.when(pl.program_id(0) == 0)
    def _():
        for e in range(8):
            context_ref[:, e * 128 : e * 128 + 128] = ctx_ref[e]

    hidden = tokens_ref[...].astype(wide) + bias_ref[...].astype(wide)
    hidden = hidden + matmul(context_ref[...], outmat_ref[...])
    hidden_ref[...] = hidden
    packed_ref[...] = matmul(sender_ref[...], hidden.astype(narrow)).astype(narrow)


def join(ctx, outmat, tokens, outbias, sender):
    rows, width = tokens.shape
    slots = sender.shape[0]
    strip = lambda height: pl.BlockSpec((height, 256), lambda n: (0, n))
    return pl.pallas_call(
        join_kernel,
        grid=(4,),
        out_shape=(
            jax.ShapeDtypeStruct((rows, width), wide),
            jax.ShapeDtypeStruct((slots, width), narrow),
            jax.ShapeDtypeStruct((rows, width), narrow),
        ),
        in_specs=[
            pl.BlockSpec((8, rows, 128), lambda n: (0, 0, 0)),
            strip(width), strip(rows), strip(1),
            pl.BlockSpec((slots, rows), lambda n: (0, 0)),
        ],
        out_specs=(strip(rows), strip(slots), pl.BlockSpec((rows, width), lambda n: (0, 0))),
        compiler_params=pltpu.CompilerParams(vmem_limit_bytes=10 << 20),
        name="join",
    )(ctx, outmat, tokens, outbias, sender)


def hidden_back_kernel(blocks_ref, getter_ref, cotangent_ref, outmat_ref, hidden_ref, grads_ref, low_ref):
    @pl.when(pl.program_id(0) == 0)
    def _():
        hidden = cotangent_ref[...].astype(wide) + matmul(getter_ref[...], blocks_ref[...])
        hidden_ref[...] = hidden
        low_ref[...] = hidden.astype(narrow)

    grads = matmul_right(low_ref[...], outmat_ref[...]).astype(narrow)
    grads_ref[0] = grads[:, 0:128]
    grads_ref[1] = grads[:, 128:256]


def hidden_back(blocks, getter, cotangent, outmat):
    rows, width = cotangent.shape
    slots = getter.shape[1]
    all_rows = pl.BlockSpec((rows, width), lambda e: (0, 0))
    return pl.pallas_call(
        hidden_back_kernel,
        grid=(4,),
        out_shape=(
            jax.ShapeDtypeStruct((rows, width), wide),
            jax.ShapeDtypeStruct((8, rows, 128), narrow),
            jax.ShapeDtypeStruct((rows, width), narrow),
        ),
        in_specs=[
            pl.BlockSpec((slots, width), lambda e: (0, 0)),
            pl.BlockSpec((rows, slots), lambda e: (0, 0)),
            all_rows,
            pl.BlockSpec((256, width), lambda e: (e, 0)),
        ],
        out_specs=(all_rows, pl.BlockSpec((2, rows, 128), lambda e: (e, 0, 0)), all_rows),
        compiler_params=pltpu.CompilerParams(vmem_limit_bytes=12 << 20),
        name="hidden_back",
    )(blocks, getter, cotangent, outmat)


def attend_kernel(low_ref, qkv_ref, segcol_ref, segrow_ref, ctx_ref, full_ref, lse_ref, vals_ref):
    blocks, size, _ = qkv_ref.shape
    for j in range(blocks):
        turned = turn(qkv_ref[j, :, 256:384])
        for head in range(2):
            vals_ref[j, head, 0:64, :] = turned[head * 64 : head * 64 + 64]
            vals_ref[j, head, 64:80, :] = jnp.ones((16, size), narrow)
    for i in range(blocks):
        query = turn((qkv_ref[i, :, 0:128].astype(wide) * HEAD_DIM**-0.5).astype(narrow))
        queries = [head_rows(query, head) for head in range(2)]

        def step(j, carry, diagonal):
            keys = qkv_ref[j, :, 128:256]
            mask = mask_of(segcol_ref, segrow_ref, i, j, diagonal)
            out = []
            for head in range(2):
                scores = jnp.where(mask, matmul(keys, queries[head]), MASKED)
                top = jnp.max(scores, 0, keepdims=True)
                if carry is not None:
                    top = jnp.maximum(top, carry[2 * head])
                probs = jnp.exp(scores - top).astype(narrow)
                total = matmul(vals_ref[j, head], probs)
                if carry is not None:
                    total = total + carry[2 * head + 1] * jnp.exp(carry[2 * head] - top)
                out += [top, total]
            return tuple(out)

        carry = step(i, None, True)
        if i > 0:
            carry = lax.fori_loop(low_ref[i], i, lambda j, c: step(j, c, False), carry)
        parts = []
        for head in range(2):
            top, total = carry[2 * head], carry[2 * head + 1]
            parts.append(total[0:64] / total[64:65])
            lse_ref[i, head : head + 1, :] = top + jnp.log(total[64:65])
        full = jnp.concatenate(parts, 0)
        full_ref[i] = full
        ctx_ref[i] = jnp.transpose(full, (1, 0)).astype(narrow)


def attend(low, qkv, segcol, segrow):
    blocks, size, _ = qkv.shape
    vmem = pl.BlockSpec(memory_space=pltpu.VMEM)
    return pl.pallas_call(
        attend_kernel,
        out_shape=(
            jax.ShapeDtypeStruct((blocks, size, 128), narrow),
            jax.ShapeDtypeStruct((blocks, 128, size), wide),
            jax.ShapeDtypeStruct((blocks, 8, size), wide),
        ),
        in_specs=[pl.BlockSpec(memory_space=pltpu.SMEM), vmem, vmem, vmem],
        out_specs=(vmem, vmem, vmem),
        scratch_shapes=[pltpu.VMEM((blocks, 2, 80, size), narrow)],
        compiler_params=pltpu.CompilerParams(vmem_limit_bytes=12 << 20),
        name="attend",
    )(low, qkv, segcol, segrow)


def attend_back_kernel(
    low_ref, qkv_ref, grad_ref, full_ref, lse_ref, segcol_ref, segrow_ref, xhat_ref,
    out_ref, three_ref, sums_ref, keys_ref, dk_ref, dv_ref, held_ref, sem_ref,
):
    fetch = pltpu.make_async_copy(xhat_ref, held_ref, sem_ref)
    fetch.start()
    blocks, size, _ = qkv_ref.shape
    for j in range(blocks):
        keys_ref[j] = turn(qkv_ref[j, :, 128:256])
    dk_ref[...] = jnp.zeros_like(dk_ref)
    dv_ref[...] = jnp.zeros_like(dv_ref)
    for i in range(blocks):
        query = (qkv_ref[i, :, 0:128].astype(wide) * HEAD_DIM**-0.5).astype(narrow)
        query_t = turn(query)
        grad = grad_ref[i]
        grad_t = turn(grad)
        inner = grad_t.astype(wide) * full_ref[i]
        queries_t = [head_rows(query_t, head) for head in range(2)]
        grads_t = [head_rows(grad_t, head) for head in range(2)]
        inners = [
            jnp.sum(inner[head * 64 : head * 64 + 64], 0, keepdims=True) for head in range(2)
        ]
        lses = [lse_ref[i, head : head + 1, :] for head in range(2)]
        query_pair = jnp.concatenate([head_lanes(query, head) for head in range(2)], 0)
        grad_pair = jnp.concatenate([head_lanes(grad, head) for head in range(2)], 0)

        def step(j, carry, diagonal):
            keys = qkv_ref[j, :, 128:256]
            vals = qkv_ref[j, :, 256:384]
            mask = mask_of(segcol_ref, segrow_ref, i, j, diagonal)
            lows, score_lows, out = [], [], []
            for head in range(2):
                scores = matmul(keys, queries_t[head])
                probs = jnp.where(mask, jnp.exp(scores - lses[head]), 0.0)
                prob_grad = matmul(vals, grads_t[head])
                score_low = (probs * (prob_grad - inners[head])).astype(narrow)
                lows.append(probs.astype(narrow))
                score_lows.append(score_low)
                part = matmul(keys_ref[j, head * 64 : head * 64 + 64, :], score_low)
                out.append(part if carry is None else carry[head] + part)
            dv_ref[j] += matmul(jnp.concatenate(lows, 1), grad_pair)
            dk_ref[j] += matmul(jnp.concatenate(score_lows, 1), query_pair)
            return tuple(out)

        carry = step(i, None, True)
        if i > 0:
            carry = lax.fori_loop(low_ref[i], i, lambda j, c: step(j, c, False), carry)
        dq = jnp.concatenate(carry, 0) * HEAD_DIM**-0.5
        out_ref[i, :, 0:128] = jnp.transpose(dq, (1, 0)).astype(narrow)
    for j in range(blocks):
        out_ref[j, :, 128:256] = dk_ref[j].astype(narrow)
        out_ref[j, :, 256:384] = dv_ref[j].astype(narrow)
    fetch.wait()
    for part in range(4):
        height = slice(part * 256, part * 256 + 256)
        three = sum(matmul(held_ref[j, height, :], out_ref[j]) for j in range(blocks))
        for d in range(4):
            for i in range(3):
                three_ref[part * 4 + d, i * 64 : i * 64 + 64, :] = three[
                    d * 64 : d * 64 + 64, i * 128 : i * 128 + 128
                ].astype(narrow)
    sums_ref[...] = sum(jnp.sum(out_ref[j].astype(wide), 0, keepdims=True) for j in range(blocks))


def attend_back(low, qkv, grad, full, lse, segcol, segrow, xhat):
    blocks, size, _ = qkv.shape
    vmem = pl.BlockSpec(memory_space=pltpu.VMEM)
    return pl.pallas_call(
        attend_back_kernel,
        out_shape=(
            jax.ShapeDtypeStruct((blocks, size, 384), narrow),
            jax.ShapeDtypeStruct((16, 192, 128), narrow),
            jax.ShapeDtypeStruct((1, 384), wide),
        ),
        in_specs=[pl.BlockSpec(memory_space=pltpu.SMEM)]
        + [vmem] * 6
        + [pl.BlockSpec(memory_space=pltpu.HBM)],
        out_specs=(vmem, vmem, vmem),
        scratch_shapes=[
            pltpu.VMEM((blocks, 128, size), narrow),
            pltpu.VMEM((blocks, size, 128), wide),
            pltpu.VMEM((blocks, size, 128), wide),
            pltpu.VMEM(xhat.shape, narrow),
            pltpu.SemaphoreType.DMA,
        ],
        compiler_params=pltpu.CompilerParams(vmem_limit_bytes=20 << 20),
        name="attend_back",
    )(low, qkv, grad, full, lse, segcol, segrow, xhat)


def unpack_kernel(
    all_ref, bias_ref, gain_ref, shift_ref, query_ref, key_ref, value_ref,
    dquery_ref, dkey_ref, dvalue_ref, dout_ref, vector_ref,
):
    mats = ((query_ref, dquery_ref), (key_ref, dkey_ref), (value_ref, dvalue_ref))
    for d in range(all_ref.shape[0]):
        height = slice(d * 64, d * 64 + 64)
        gain, shift = gain_ref[d].astype(wide), shift_ref[d].astype(wide)
        gain_sum = shift_sum = jnp.zeros((64, 128), wide)
        for e in range(8):
            lanes = slice(e * 128, e * 128 + 128)
            for i, (mat_ref, grad_ref) in enumerate(mats):
                part = all_ref[d, e, i * 64 : i * 64 + 64, :].astype(wide)
                bias = bias_ref[i : i + 1, lanes]
                mat = mat_ref[height, lanes].astype(wide)
                grad_ref[height, lanes] = gain * part + shift * bias
                gain_sum = gain_sum + mat * part
                shift_sum = shift_sum + mat * bias
            for i in range(8):
                dout_ref[e, d, :, i * 128 : i * 128 + 128] = all_ref[
                    d, e, 192 + i * 8 : 200 + i * 8, :
                ].astype(wide)
        vector_ref[d, :, 0:1] = jnp.sum(gain_sum, 1, keepdims=True)
        vector_ref[d, :, 1:2] = jnp.sum(shift_sum, 1, keepdims=True)


def unpack(everything, biases, gain, shift, querymat, keymat, valuemat, step=2):
    width = querymat.shape[0]
    column = pl.BlockSpec((step, 64, 1), lambda d: (d, 0, 0))
    strip = pl.BlockSpec((step * 64, width), lambda d: (d, 0))
    square = jax.ShapeDtypeStruct((width, width), wide)
    return pl.pallas_call(
        unpack_kernel,
        grid=(16 // step,),
        out_shape=(
            square, square, square,
            jax.ShapeDtypeStruct((8, 16, 8, width), wide),
            jax.ShapeDtypeStruct((16, 64, 2), wide),
        ),
        in_specs=[
            pl.BlockSpec((step, 8, 264, 128), lambda d: (d, 0, 0, 0)),
            pl.BlockSpec((3, width), lambda d: (0, 0)),
            column, column, strip, strip, strip,
        ],
        out_specs=(
            strip, strip, strip,
            pl.BlockSpec((8, step, 8, width), lambda d: (0, d, 0, 0)),
            pl.BlockSpec((step, 64, 2), lambda d: (d, 0, 0)),
        ),
        compiler_params=pltpu.CompilerParams(vmem_limit_bytes=14 << 20),
        name="unpack",
    )(everything, biases, gain, shift, querymat, keymat, valuemat)


def per_device(
    tokens, cotangent, segments, routes,
    attngain, attnshift, querymat, querybias, keymat, valuemat, valuebias, outmat, outbias,
    frontgain, frontshift, frontexpand, frontlift, frontreduce, frontoffset,
    backgain, backshift, backexpand, backlift, backreduce, backoffset, centroid,
):
    rows, width = tokens.shape
    experts = 8
    capacity = rows // experts + rows // (2 * experts)
    slots = experts * capacity
    mine = lax.axis_index(GROUP)
    y1_at, y2_at, y_at = (lax.axis_index(axis) for axis in ("y1", "y2", COLUMN))

    plans = to_everyone(jnp.concatenate([segments, routes], 0), GROUP, experts)
    small_own = jnp.concatenate(
        [
            frontgain[0], frontshift[0], frontoffset[0], backgain[0], backshift[0], backoffset[0],
            centroid[0], frontlift[0], backlift[0], jnp.zeros((64,), narrow),
        ]
    )
    small = small_own.reshape(8, 128)

    def reduced(matrix, axes):
        return lax.psum_scatter(matrix, axes, scatter_dimension=0, tiled=True)

    def gathered(matrix, axes):
        return lax.all_gather(matrix, axes, axis=0)

    front_own = jnp.concatenate([frontexpand[0].T, frontreduce[0]], 0)
    front_other = swap(front_own, "y1")
    front_mats = [gathered(front_own, "x")]

    route = routes[0]
    picks = (route[:, None] == jnp.arange(experts)[None, :]).astype(narrow)
    lower = (jnp.arange(rows)[:, None] > jnp.arange(rows)[None, :]).astype(narrow)
    rank = jnp.sum(matmul(lower, picks) * picks.astype(wide), 1).astype(jnp.int32)
    send_index = route * capacity + rank
    sender = (jnp.arange(slots)[:, None] == send_index[None, :]).astype(narrow)
    def pack(row_data):
        return matmul(sender, row_data).astype(narrow).reshape(experts, capacity, width)

    def unpack_rows(blocks):
        return matmul(taker, blocks.reshape(slots, width)).astype(narrow)

    def pack_back(row_data):
        return matmul_left(taker, row_data).astype(narrow).reshape(experts, capacity, width)

    def unpack_back(blocks):
        return matmul_left(sender, blocks.reshape(slots, width))

    line = lambda vector: vector.reshape(1, width)
    split, xhat_low = project(
        tokens, line(attngain), line(attnshift),
        querymat, line(querybias), keymat, valuemat, line(valuebias),
    )
    split, plans = lax.optimization_barrier((split, plans))
    seg_all, route_all = plans[:, 0], plans[:, 1]
    qkv = exchange(split, GROUP)
    xhat_turned = turned(xhat_low)
    qkv, xhat_turned = lax.optimization_barrier((qkv, xhat_turned))
    small = to_everyone(after(qkv, small), DATA, 16)
    counts = jnp.sum((route_all == mine).astype(jnp.int32), 1)
    ahead = jnp.arange(experts)[:, None] > jnp.arange(experts)[None, :]
    starts = jnp.sum(jnp.where(ahead, counts[None, :], 0), 1)
    place = jnp.arange(capacity)[None, :]
    spots = jnp.where(place < counts[:, None], starts[:, None] + place, -1).reshape(-1)
    taker = (jnp.arange(rows)[:, None] == spots[None, :]).astype(narrow)

    segcol, segrow = seg_all[:, :, None], seg_all[:, None, :]
    low = jnp.sum((seg_all[None, :, -1] < seg_all[:, None, 0]).astype(jnp.int32), 1)
    ctx, full, lse = attend(low, qkv, segcol, segrow)
    ctx, small, front_mats[0] = lax.optimization_barrier((ctx, small, front_mats[0]))
    front_other, back_own = after(ctx, front_other, jnp.concatenate([backexpand[0].T, backreduce[0]], 0))
    front_mats.append(gathered(front_other, "x"))
    back_mats = gathered(back_own, "x")
    small = small.reshape(16, 1024).astype(wide)
    front_gain, front_shift, front_offset, back_gain, back_shift, back_offset, centre = (
        small[:, i * 64 : i * 64 + 64].reshape(1, width) for i in range(7)
    )
    lifts = small[:, 448:960].reshape(4, 2, 2, 512)
    front_lift = lax.dynamic_index_in_dim(lifts, y2_at, 2, False)[:, :, :256]
    front_lift = jnp.where(y1_at == 0, front_lift, front_lift[:, ::-1])
    front_lift = jnp.transpose(front_lift, (1, 0, 2)).reshape(2, 1, 1024)
    back_lift = lax.dynamic_index_in_dim(lifts.reshape(4, 4, 512), y_at, 1, False)[:, 256:]
    back_lift = back_lift.reshape(1, 1024)
    hidden, blocks, context = join(exchange(ctx, GROUP), outmat, tokens, line(outbias), sender)

    blocks = exchange(blocks.reshape(experts, capacity, width), GROUP)
    stream = unpack_rows(blocks).astype(wide)
    front_xhat, front_inverse = norm_parts(stream)
    xhat_own = front_xhat.astype(narrow)
    ct_blocks = exchange(pack(after(xhat_own, cotangent)), GROUP)
    front_side = front_gain, front_shift, front_lift, [pinned(mats) for mats in front_mats]
    *own_acts, own_slope_a, own_slope_b, front_normed, own_part = front_forward(
        xhat_own, *front_side, wide
    )
    ct_blocks, own_part = lax.optimization_barrier((ct_blocks, own_part))
    gate = jax.nn.sigmoid(jnp.sum(stream * centre, -1, keepdims=True))
    ct_rows = unpack_rows(ct_blocks).astype(wide)
    gated = gate * ct_rows
    back_branch = gated.astype(narrow)
    xhat_got, back_branch, own_part = lax.optimization_barrier(
        (swap(xhat_own, "y2"), back_branch, own_part)
    )
    back_branches = share_four(back_branch)
    *got_acts, got_slope_a, got_slope_b, normed_got, got_part = front_forward(
        xhat_got, *front_side, narrow
    )
    got_part, *back_branches[1:3] = lax.optimization_barrier((got_part, *back_branches[1:3]))
    front_got, back_branches[3] = lax.optimization_barrier((swap(got_part, "y2"), back_branches[3]))
    front_out = own_part + front_got.astype(wide) + front_offset
    xhat_all = lax.all_gather(after(got_part, xhat_turned), GROUP, axis=0)
    middle = stream + front_out
    back_xhat, back_inverse = norm_parts(middle)
    back_normed = share_four((back_xhat * back_gain + back_shift).astype(narrow))
    own_results = list(back_both(back_normed[0], back_branches[0], back_lift, back_mats, wide))
    own_results[2], *back_normed[1:] = lax.optimization_barrier((own_results[2], *back_normed[1:]))
    back_results = [own_results] + [
        back_both(normed, branch, back_lift, back_mats, narrow)
        for normed, branch in zip(back_normed[1:], back_branches[1:])
    ]
    back_acts, back_pre_grads, back_parts, out_parts, dots = map(list, zip(*back_results))
    back_late = after(back_parts[-1], *back_acts, *back_pre_grads)
    back_mat_part, back_lifts = mat_grads([back_late[:4], back_late[4:]], back_branches, back_normed)
    *back_got, back_mat_part, xhat_all = lax.optimization_barrier(
        (*return_four(back_parts), back_mat_part, xhat_all)
    )
    back_grads = reduced(back_mat_part, "x")
    back_norm_grad = total(back_parts[0], back_got)
    middle_grad = norm_back(back_norm_grad * back_gain, back_xhat, back_inverse)
    front_branch = (gated + middle_grad).astype(narrow)
    *own_pre_grads, own_part = front_backward(
        front_branch, (own_slope_a, own_slope_b), front_side[-1], wide
    )
    branch_got, own_part, *dots_got = lax.optimization_barrier(
        (swap(front_branch, "y2"), own_part, *return_four(dots))
    )
    *got_pre_grads, got_part = front_backward(
        branch_got, (got_slope_a, got_slope_b), front_side[-1], narrow
    )
    late = after(got_part, *own_acts, *got_acts)
    front_shrink_part, _ = mat_grads(list(zip(late[:2], late[2:])), (front_branch, branch_got))
    front_got, front_shrink_part = lax.optimization_barrier((swap(got_part, "y2"), front_shrink_part))
    front_shrink_part = reduced(front_shrink_part, "x")
    front_norm_grad = own_part + front_got.astype(wide)
    first_grad = norm_back(front_norm_grad * front_gain, front_xhat, front_inverse)
    gated_dot = jnp.sum(gated * (front_out + back_offset), -1, keepdims=True)
    logit_grad = (gated_dot + total(dots[0], dots_got)[:, :1]) * (1.0 - gate)
    sent_grad = (logit_grad * centre + middle_grad + first_grad).astype(narrow)

    sent_blocks = pack_back(sent_grad)
    pre_late = after(sent_blocks, *own_pre_grads, *got_pre_grads)
    front_expand_part, front_lifts = mat_grads(
        list(zip(pre_late[:2], pre_late[2:])), (front_normed, normed_got)
    )
    sent_blocks, front_expand_part, back_grads = lax.optimization_barrier(
        (exchange(sent_blocks, GROUP), front_expand_part, back_grads)
    )
    front_expand_part = reduced(front_expand_part, "x")
    getter = (send_index[:, None] == jnp.arange(slots)[None, :]).astype(narrow)
    hidden_grad, context_grad, out_low = hidden_back(
        sent_blocks.reshape(slots, width), getter, cotangent, outmat
    )
    grads = exchange(context_grad, GROUP)
    expert_sums = row_sums(
        *after(
            context_grad, front_norm_grad, front_xhat, front_branch, back_norm_grad, back_xhat,
            back_branches[0], logit_grad, stream,
        )
    )[:7].reshape(7, 16, 64)
    context, out_late = after(context_grad, context, out_low)
    out_part = matmul_left(context, out_late).astype(narrow).reshape(experts, 128, width)
    grads, out_part, expert_sums, *out_got = lax.optimization_barrier(
        (grads, out_part, expert_sums, *return_four(after(sent_blocks, *out_parts)))
    )
    branches = front_out + total(out_parts[0], out_got) + back_offset
    out_part = exchange(out_part, GROUP)

    dqkv, three, sums = attend_back(low, qkv, grads, full, lse, segcol, segrow, xhat_all)

    out_part = jnp.sum(after(sums, out_part).astype(wide), 0).astype(narrow).reshape(16, 8, 8, 128)
    biases = jnp.concatenate(
        [
            sums.reshape(16, 24),
            jnp.sum(out_low.astype(wide), 0).reshape(16, 64),
        ],
        1,
    ).astype(narrow)
    front_lifts, back_lifts = front_lifts[:, :, 0], back_lifts[:, 1, 0]
    front_lifts = jnp.where(y1_at == 0, front_lifts, front_lifts[:, ::-1])
    front_lifts = jnp.where(jnp.arange(2)[:, None] == y2_at, front_lifts[:, :, None], 0.0)
    back_lifts = jnp.where(jnp.arange(4)[:, None] == y_at, back_lifts[:, None], 0.0)
    packed = jnp.concatenate(
        [
            jnp.transpose(expert_sums, (1, 0, 2)).reshape(16, 448),
            front_lifts.reshape(16, 256),
            back_lifts.reshape(16, 256),
            jnp.zeros((16, 64), wide),
        ],
        1,
    )
    slices = jnp.concatenate(
        [
            three,
            jnp.transpose(out_part, (0, 2, 1, 3)).reshape(16, 64, 128),
            jnp.pad(biases[:, None], ((0, 0), (0, 7), (0, 40))),
            packed.reshape(16, 8, 128).astype(narrow),
        ],
        1,
    )
    slices, front_shrink_part, front_expand_part = lax.optimization_barrier(
        (exchange(slices, DATA), front_shrink_part, front_expand_part)
    )
    slices = jnp.sum(slices.astype(wide), 0)
    summed = slices[264:].reshape(1, 1024)
    slices = slices[:264].astype(narrow)
    everything = lax.all_gather(slices, EVERY, axis=0).reshape(16, 8, 264, 128)
    biases = everything[:, :, 256, :88].astype(wide)
    outbias_grad = jnp.sum(biases[:, :, 24:], 1).reshape(width)
    biases = jnp.transpose(biases[:, :, :24], (1, 0, 2)).reshape(8, 3, 128)
    biases = jnp.transpose(biases, (1, 0, 2)).reshape(3, width)
    query_grad, key_grad, value_grad, outmat_grad, vectors = unpack(
        everything, biases, attngain.reshape(16, 64, 1), attnshift.reshape(16, 64, 1),
        querymat, keymat, valuemat,
    )
    outmat_grad = outmat_grad.reshape(width, width)
    attngain_grad, attnshift_grad = vectors[:, :, 0].reshape(width), vectors[:, :, 1].reshape(width)
    querybias_grad, _, valuebias_grad = biases

    dqkv, returned, front_shrink_part, front_expand_part = after(
        slices, dqkv, pack_back((gate * branches).astype(narrow)), front_shrink_part, front_expand_part
    )
    own, returned, front_swap, other = lax.optimization_barrier(
        (
            exchange(dqkv, GROUP),
            exchange(returned, GROUP),
            swap(front_shrink_part[0, 1], "y1"),
            swap(front_expand_part[0, 1], "y1"),
        )
    )
    own = jnp.transpose(own.reshape(experts, rows, 3, 128), (2, 1, 0, 3))
    dquery, dkey, dvalue = (own[i].reshape(rows, width) for i in range(3))
    attn_norm_grad = (
        matmul_right(dquery, querymat) + matmul_right(dkey, keymat) + matmul_right(dvalue, valuemat)
    )
    attn_xhat, attn_inverse = norm_parts(tokens.astype(wide))
    tokens_grad = hidden_grad + norm_back(
        attn_norm_grad * attngain.astype(wide), attn_xhat, attn_inverse
    )
    result = (hidden + unpack_back(returned)).astype(narrow)
    back_shrink_grad, back_expand_grad = (grad.astype(wide) for grad in back_grads[0])
    front_shrink_grad = front_shrink_part[0, 0].astype(wide) + front_swap.astype(wide)
    front_expand_grad = front_expand_part[0, 0].astype(wide) + other.astype(wide)
    back_shrink_grad, front_shrink_grad = back_shrink_grad[None], front_shrink_grad[None]
    back_expand_grad, front_expand_grad = back_expand_grad.T[None], front_expand_grad.T[None]
    (
        front_gain_grad, front_shift_grad, front_offset_grad,
        back_gain_grad, back_shift_grad, back_offset_grad, centroid_grad,
    ) = (summed[:, i * 64 : i * 64 + 64] for i in range(7))
    front_lift_grad, back_lift_grad = summed[:, 448:704], summed[:, 704:960]

    return (
        result, tokens_grad, attngain_grad, attnshift_grad,
        query_grad, querybias_grad, key_grad, value_grad, valuebias_grad, outmat_grad, outbias_grad,
        front_gain_grad, front_shift_grad, front_expand_grad, front_lift_grad,
        front_shrink_grad, front_offset_grad,
        back_gain_grad, back_shift_grad, back_expand_grad, back_lift_grad,
        back_shrink_grad, back_offset_grad, centroid_grad,
    )


def solution(mesh):
    grid = Mesh(mesh.devices.reshape(4, 2, 2, 4, 2), EVERY)
    rows, plan, full = P(EVERY, None), P(DATA, GROUP), P()
    vector, expand, shrink = P(GROUP, DATA), P(GROUP, None, DATA), P(GROUP, DATA, None)
    sublayer = (vector, vector, expand, vector, shrink, vector)
    return jax.shard_map(
        per_device,
        mesh=grid,
        in_specs=(rows, rows, plan, plan) + (full,) * 9 + sublayer * 2 + (vector,),
        out_specs=(rows, rows) + (full,) * 9 + sublayer * 2 + (vector,),
        check_vma=False,
    )
```

```python
import jax
import jax.numpy as jnp
from jax import lax
from jax.experimental import pallas as pl
from jax.experimental.pallas import tpu as pltpu
from jax.sharding import Mesh, PartitionSpec as P

HEADS = 16
HEAD_DIM = 64
EPSILON = 1e-05
MASKED = -1e30

GROUP = ("z", "c")
DATA = ("x", "y1", "y2")
COLUMN = ("y1", "y2")
EVERY = DATA + GROUP

wide = jnp.float32
narrow = jnp.bfloat16


def matmul(left, right):
    return jnp.dot(left, right, preferred_element_type=wide)


def matmul_left(left, right):
    return lax.dot_general(left, right, (((0,), (0,)), ((), ())), preferred_element_type=wide)


def matmul_right(left, right):
    return lax.dot_general(left, right, (((1,), (1,)), ((), ())), preferred_element_type=wide)


def norm_parts(stream):
    center = stream - jnp.mean(stream, -1, keepdims=True)
    inverse = lax.rsqrt(jnp.mean(center * center, -1, keepdims=True) + EPSILON)
    return center * inverse, inverse


def norm_back(scaled, xhat, inverse):
    return (
        scaled
        - jnp.mean(scaled, -1, keepdims=True)
        - xhat * jnp.mean(scaled * xhat, -1, keepdims=True)
    ) * inverse


def gelu_pair(value):
    cdf = 0.5 + 0.5 * lax.erf(value * (0.5**0.5))
    pdf = jnp.exp(-0.5 * value * value) * 0.3989422804014327
    return value * cdf, cdf + value * pdf


def swap(value, axis):
    return lax.ppermute(value, axis, [(0, 1), (1, 0)])


def shift_by(value, step):
    return lax.ppermute(value, COLUMN, [(i, (i + step) % 4) for i in range(4)])


def share_four(rows):
    return [rows] + [shift_by(rows, step) for step in (1, 3, 2)]


def return_four(parts):
    return [shift_by(part, step) for part, step in zip(parts[1:], (3, 1, 2))]


def total(own, got):
    return own.astype(wide) + sum(part.astype(wide) for part in got)


def after(first, *later):
    later = lax.optimization_barrier((first,) + later)[1:]
    return later if len(later) > 1 else later[0]


def exchange(blocks, axes):
    return lax.all_to_all(blocks, axes, 0, 0, tiled=True)


def to_everyone(block, axes, count):
    return exchange(jnp.broadcast_to(block[None], (count,) + block.shape), axes)


def head_rows(matrix, head):
    rows = lax.broadcasted_iota(jnp.int32, matrix.shape, 0) // HEAD_DIM
    return jnp.where(rows == head, matrix, jnp.zeros_like(matrix))


def head_lanes(matrix, head):
    lanes = lax.broadcasted_iota(jnp.int32, matrix.shape, 1) // HEAD_DIM
    return jnp.where(lanes == head, matrix, jnp.zeros_like(matrix))


def turn(matrix):
    return jnp.transpose(matrix.astype(wide), (1, 0)).astype(matrix.dtype)


def mask_of(segcol_ref, segrow_ref, i, j, diagonal):
    same = segcol_ref[j] == segrow_ref[i]
    if diagonal:
        size = same.shape
        same = same & (
            lax.broadcasted_iota(jnp.int32, size, 0) <= lax.broadcasted_iota(jnp.int32, size, 1)
        )
    return same


EXPAND = pl.BlockSpec((1, 256, 1024), lambda k: (k, 0, 0))
SHRINK = pl.BlockSpec((1, 256, 1024), lambda k: (k, 1, 0))
COLUMNS = pl.BlockSpec((256, 256), lambda k: (0, k))
WHOLE = pl.BlockSpec((256, 1024), lambda k: (0, 0))
LANES = pl.BlockSpec((256, 128), lambda k: (0, 0))
LINE = pl.BlockSpec((1, 1024), lambda k: (0, 0))
LIFT = pl.BlockSpec((1, 256), lambda k: (0, k))


def first_step(run):
    pl.when(pl.program_id(0) == 0)(run)


def add_up(acc_ref, part_ref, part):
    k = pl.program_id(0)

    @first_step
    def _():
        acc_ref[...] = part

    @pl.when(k > 0)
    def _():
        acc_ref[...] += part

    @pl.when(k == pl.num_programs(0) - 1)
    def _():
        part_ref[...] = acc_ref[...].astype(part_ref.dtype)


def expert_call(kernel, name, in_specs, out_specs, outs, kept, accs, *args):
    return pl.pallas_call(
        kernel,
        grid=(4,),
        out_shape=[
            pltpu.HBM((256, 1024), dtype)
            if i < kept
            else jax.ShapeDtypeStruct((256, 128 if spec is LANES else 1024), dtype)
            for i, (dtype, spec) in enumerate(zip(outs, out_specs))
        ],
        in_specs=in_specs,
        out_specs=out_specs,
        scratch_shapes=[pltpu.VMEM((256, 1024), wide)] * accs,
        compiler_params=pltpu.CompilerParams(vmem_limit_bytes=16 << 20),
        name=name,
    )(*args)


def front_forward_kernel(
    xhat_ref, gain_ref, shift_ref, lift_a_ref, lift_b_ref,
    expand_a_ref, shrink_a_ref, expand_b_ref, shrink_b_ref,
    act_a_ref, act_b_ref, slope_a_ref, slope_b_ref, rows_ref, part_ref, acc_ref,
):
    @first_step
    def _():
        rows = xhat_ref[...].astype(wide) * gain_ref[...] + shift_ref[...]
        rows_ref[...] = rows.astype(narrow)

    part = 0.0
    for lift_ref, expand_ref, shrink_ref, act_ref, slope_ref in (
        (lift_a_ref, expand_a_ref, shrink_a_ref, act_a_ref, slope_a_ref),
        (lift_b_ref, expand_b_ref, shrink_b_ref, act_b_ref, slope_b_ref),
    ):
        act, slope = gelu_pair(matmul_right(rows_ref[...], expand_ref[0]) + lift_ref[...])
        act = act.astype(narrow)
        act_ref[...] = act
        slope_ref[...] = slope
        part = part + matmul(act, shrink_ref[0])
    add_up(acc_ref, part_ref, part)


def front_forward(xhat, gain, shift, lifts, mats, last):
    return expert_call(
        front_forward_kernel, "front_forward",
        [WHOLE, LINE, LINE, LIFT, LIFT, EXPAND, SHRINK, EXPAND, SHRINK],
        [COLUMNS] * 4 + [WHOLE] * 2, [narrow, narrow, wide, wide, narrow, last], 5, 1,
        xhat, gain, shift, lifts[0], lifts[1], mats[0], mats[0], mats[1], mats[1],
    )


def front_backward_kernel(
    rows_ref, slope_a_ref, slope_b_ref, expand_a_ref, shrink_a_ref, expand_b_ref, shrink_b_ref,
    grad_a_ref, grad_b_ref, part_ref, acc_ref,
):
    part = 0.0
    for slope_ref, expand_ref, shrink_ref, grad_ref in (
        (slope_a_ref, expand_a_ref, shrink_a_ref, grad_a_ref),
        (slope_b_ref, expand_b_ref, shrink_b_ref, grad_b_ref),
    ):
        grad = (slope_ref[...] * matmul_right(rows_ref[...], shrink_ref[0])).astype(narrow)
        grad_ref[...] = grad
        part = part + matmul(grad, expand_ref[0])
    add_up(acc_ref, part_ref, part)


def front_backward(rows, slopes, mats, last):
    return expert_call(
        front_backward_kernel, "front_backward",
        [WHOLE, COLUMNS, COLUMNS, EXPAND, SHRINK, EXPAND, SHRINK],
        [COLUMNS] * 2 + [WHOLE], [narrow, narrow, last], 2, 1,
        rows, pinned(slopes[0]), pinned(slopes[1]), mats[0], mats[0], mats[1], mats[1],
    )


def back_kernel(
    rows_ref, branch_ref, lift_ref, expand_ref, shrink_ref,
    act_ref, grad_ref, part_ref, out_ref, dot_ref, part_acc_ref, out_acc_ref,
):
    act, slope = gelu_pair(matmul_right(rows_ref[...], expand_ref[0]) + lift_ref[...])
    act = act.astype(narrow)
    act_ref[...] = act
    grad = (slope * matmul_right(branch_ref[...], shrink_ref[0])).astype(narrow)
    grad_ref[...] = grad
    add_up(part_acc_ref, part_ref, matmul(grad, expand_ref[0]))
    add_up(out_acc_ref, out_ref, matmul(act, shrink_ref[0]))

    @pl.when(pl.program_id(0) == 3)
    def _():
        dot = jnp.sum(branch_ref[...].astype(wide) * out_acc_ref[...], 1, keepdims=True)
        dot_ref[...] = jnp.broadcast_to(dot, dot_ref.shape)


def back_both(rows, branch, lift, mats, last):
    return expert_call(
        back_kernel, "back_both", [WHOLE, WHOLE, LIFT, EXPAND, SHRINK],
        [COLUMNS] * 2 + [WHOLE] * 2 + [LANES], [narrow, narrow, last, last, wide], 2, 2,
        rows, branch, lift, mats, mats,
    )


def mat_grads_kernel(count, sides, *refs):
    lefts, rights = refs[: count * sides], refs[count * sides : -2]
    for side in range(sides):
        start = side * count if len(rights) > count else 0
        side_lefts = [left[...] for left in lefts[side * count : side * count + count]]
        side_rights = rights[start : start + count]
        part = sum(matmul_left(left, right[...]) for left, right in zip(side_lefts, side_rights))
        refs[-2][0, side] = part.astype(narrow)
        line = sum(jnp.sum(left.astype(wide), 0, keepdims=True) for left in side_lefts)
        refs[-1][0, side] = jnp.broadcast_to(line, (8, 256))


def mat_grads(lefts, *rights):
    count, sides = len(rights[0]), len(lefts)
    rights = [part for side in rights for part in side]
    return pl.pallas_call(
        lambda *refs: mat_grads_kernel(count, sides, *refs),
        grid=(4,),
        out_shape=(
            pltpu.HBM((4, sides, 256, 1024), narrow),
            jax.ShapeDtypeStruct((4, sides, 8, 256), wide),
        ),
        in_specs=[COLUMNS] * (count * sides) + [WHOLE] * len(rights),
        out_specs=(
            pl.BlockSpec((1, sides, 256, 1024), lambda k: (k, 0, 0, 0)),
            pl.BlockSpec((1, sides, 8, 256), lambda k: (k, 0, 0, 0)),
        ),
        compiler_params=pltpu.CompilerParams(vmem_limit_bytes=20 << 20),
        name="mat_grads",
    )(*(pinned(part) for side in lefts for part in side), *rights)


def sums_kernel(
    front_grad_ref, front_xhat_ref, front_branch_ref, back_grad_ref, back_xhat_ref, back_branch_ref,
    logit_grad_ref, stream_ref, out_ref,
):
    front_grad, back_grad = front_grad_ref[...], back_grad_ref[...]
    lines = (
        front_grad * front_xhat_ref[...], front_grad, front_branch_ref[...].astype(wide),
        back_grad * back_xhat_ref[...], back_grad, back_branch_ref[...].astype(wide),
        logit_grad_ref[...] * stream_ref[...],
    )
    for i, line in enumerate(lines):
        out_ref[i : i + 1, :] = jnp.sum(line, 0, keepdims=True)
    out_ref[7:8, :] = jnp.zeros_like(out_ref[7:8, :])


def row_sums(*args):
    return pl.pallas_call(
        sums_kernel,
        out_shape=jax.ShapeDtypeStruct((8, 1024), wide),
        compiler_params=pltpu.CompilerParams(vmem_limit_bytes=12 << 20),
        name="row_sums",
    )(*args)


def turn_kernel(in_ref, out_ref):
    out_ref[...] = turn(in_ref[...])


def turned(matrix):
    return pl.pallas_call(
        turn_kernel, out_shape=jax.ShapeDtypeStruct(matrix.shape[::-1], matrix.dtype), name="turned"
    )(matrix)


def pinned(value):
    return pltpu.with_memory_space_constraint(value, pltpu.HBM)


def project_kernel(
    tokens_ref, gain_ref, shift_ref, query_ref, key_ref, value_ref, query_bias_ref, value_bias_ref,
    out_ref, xhat_ref, normed_ref,
):
    @pl.when(pl.program_id(0) == 0)
    def _():
        xhat, _ = norm_parts(tokens_ref[...].astype(wide))
        xhat_ref[...] = xhat.astype(narrow)
        normed = xhat * gain_ref[...].astype(wide) + shift_ref[...].astype(wide)
        normed_ref[...] = normed.astype(narrow)

    normed = normed_ref[...]
    query = matmul(normed, query_ref[...]) + query_bias_ref[...].astype(wide)
    value = matmul(normed, value_ref[...]) + value_bias_ref[...].astype(wide)
    out_ref[0, :, 0:128] = query.astype(narrow)
    out_ref[0, :, 128:256] = matmul(normed, key_ref[...]).astype(narrow)
    out_ref[0, :, 256:384] = value.astype(narrow)


def project(tokens, gain, shift, querymat, querybias, keymat, valuemat, valuebias):
    rows, width = tokens.shape
    all_rows = pl.BlockSpec((rows, width), lambda e: (0, 0))
    line = pl.BlockSpec((1, width), lambda e: (0, 0))
    mat, bias = pl.BlockSpec((width, 128), lambda e: (0, e)), pl.BlockSpec((1, 128), lambda e: (0, e))
    return pl.pallas_call(
        project_kernel,
        grid=(8,),
        out_shape=(
            jax.ShapeDtypeStruct((8, rows, 384), narrow),
            jax.ShapeDtypeStruct((rows, width), narrow),
        ),
        in_specs=[all_rows, line, line, mat, mat, mat, bias, bias],
        out_specs=(pl.BlockSpec((1, rows, 384), lambda e: (e, 0, 0)), all_rows),
        scratch_shapes=[pltpu.VMEM((rows, width), narrow)],
        compiler_params=pltpu.CompilerParams(vmem_limit_bytes=8 << 20),
        name="project",
    )(tokens, gain, shift, pinned(querymat), pinned(keymat), pinned(valuemat), querybias, valuebias)


def join_kernel(ctx_ref, outmat_ref, tokens_ref, bias_ref, sender_ref, hidden_ref, packed_ref, context_ref):
    @pl.when(pl.program_id(0) == 0)
    def _():
        for e in range(8):
            context_ref[:, e * 128 : e * 128 + 128] = ctx_ref[e]

    hidden = tokens_ref[...].astype(wide) + bias_ref[...].astype(wide)
    hidden = hidden + matmul(context_ref[...], outmat_ref[...])
    hidden_ref[...] = hidden
    packed_ref[...] = matmul(sender_ref[...], hidden.astype(narrow)).astype(narrow)


def join(ctx, outmat, tokens, outbias, sender):
    rows, width = tokens.shape
    slots = sender.shape[0]
    strip = lambda height: pl.BlockSpec((height, 256), lambda n: (0, n))
    return pl.pallas_call(
        join_kernel,
        grid=(4,),
        out_shape=(
            jax.ShapeDtypeStruct((rows, width), wide),
            jax.ShapeDtypeStruct((slots, width), narrow),
            jax.ShapeDtypeStruct((rows, width), narrow),
        ),
        in_specs=[
            pl.BlockSpec((8, rows, 128), lambda n: (0, 0, 0)),
            strip(width), strip(rows), strip(1),
            pl.BlockSpec((slots, rows), lambda n: (0, 0)),
        ],
        out_specs=(strip(rows), strip(slots), pl.BlockSpec((rows, width), lambda n: (0, 0))),
        compiler_params=pltpu.CompilerParams(vmem_limit_bytes=10 << 20),
        name="join",
    )(ctx, outmat, tokens, outbias, sender)


def hidden_back_kernel(blocks_ref, getter_ref, cotangent_ref, outmat_ref, hidden_ref, grads_ref, low_ref):
    @pl.when(pl.program_id(0) == 0)
    def _():
        hidden = cotangent_ref[...].astype(wide) + matmul(getter_ref[...], blocks_ref[...])
        hidden_ref[...] = hidden
        low_ref[...] = hidden.astype(narrow)

    grads = matmul_right(low_ref[...], outmat_ref[...]).astype(narrow)
    grads_ref[0] = grads[:, 0:128]
    grads_ref[1] = grads[:, 128:256]


def hidden_back(blocks, getter, cotangent, outmat):
    rows, width = cotangent.shape
    slots = getter.shape[1]
    all_rows = pl.BlockSpec((rows, width), lambda e: (0, 0))
    return pl.pallas_call(
        hidden_back_kernel,
        grid=(4,),
        out_shape=(
            jax.ShapeDtypeStruct((rows, width), wide),
            jax.ShapeDtypeStruct((8, rows, 128), narrow),
            jax.ShapeDtypeStruct((rows, width), narrow),
        ),
        in_specs=[
            pl.BlockSpec((slots, width), lambda e: (0, 0)),
            pl.BlockSpec((rows, slots), lambda e: (0, 0)),
            all_rows,
            pl.BlockSpec((256, width), lambda e: (e, 0)),
        ],
        out_specs=(all_rows, pl.BlockSpec((2, rows, 128), lambda e: (e, 0, 0)), all_rows),
        compiler_params=pltpu.CompilerParams(vmem_limit_bytes=12 << 20),
        name="hidden_back",
    )(blocks, getter, cotangent, outmat)


def attend_kernel(low_ref, qkv_ref, segcol_ref, segrow_ref, ctx_ref, full_ref, lse_ref, vals_ref):
    blocks, size, _ = qkv_ref.shape
    for j in range(blocks):
        turned = turn(qkv_ref[j, :, 256:384])
        for head in range(2):
            vals_ref[j, head, 0:64, :] = turned[head * 64 : head * 64 + 64]
            vals_ref[j, head, 64:80, :] = jnp.ones((16, size), narrow)
    for i in range(blocks):
        query = turn((qkv_ref[i, :, 0:128].astype(wide) * HEAD_DIM**-0.5).astype(narrow))
        queries = [head_rows(query, head) for head in range(2)]

        def step(j, carry, diagonal):
            keys = qkv_ref[j, :, 128:256]
            mask = mask_of(segcol_ref, segrow_ref, i, j, diagonal)
            out = []
            for head in range(2):
                scores = jnp.where(mask, matmul(keys, queries[head]), MASKED)
                top = jnp.max(scores, 0, keepdims=True)
                if carry is not None:
                    top = jnp.maximum(top, carry[2 * head])
                probs = jnp.exp(scores - top).astype(narrow)
                total = matmul(vals_ref[j, head], probs)
                if carry is not None:
                    total = total + carry[2 * head + 1] * jnp.exp(carry[2 * head] - top)
                out += [top, total]
            return tuple(out)

        carry = step(i, None, True)
        if i > 0:
            carry = lax.fori_loop(low_ref[i], i, lambda j, c: step(j, c, False), carry)
        parts = []
        for head in range(2):
            top, total = carry[2 * head], carry[2 * head + 1]
            parts.append(total[0:64] / total[64:65])
            lse_ref[i, head : head + 1, :] = top + jnp.log(total[64:65])
        full = jnp.concatenate(parts, 0)
        full_ref[i] = full
        ctx_ref[i] = jnp.transpose(full, (1, 0)).astype(narrow)


def attend(low, qkv, segcol, segrow):
    blocks, size, _ = qkv.shape
    vmem = pl.BlockSpec(memory_space=pltpu.VMEM)
    return pl.pallas_call(
        attend_kernel,
        out_shape=(
            jax.ShapeDtypeStruct((blocks, size, 128), narrow),
            jax.ShapeDtypeStruct((blocks, 128, size), wide),
            jax.ShapeDtypeStruct((blocks, 8, size), wide),
        ),
        in_specs=[pl.BlockSpec(memory_space=pltpu.SMEM), vmem, vmem, vmem],
        out_specs=(vmem, vmem, vmem),
        scratch_shapes=[pltpu.VMEM((blocks, 2, 80, size), narrow)],
        compiler_params=pltpu.CompilerParams(vmem_limit_bytes=12 << 20),
        name="attend",
    )(low, qkv, segcol, segrow)


def attend_back_kernel(
    low_ref, qkv_ref, grad_ref, full_ref, lse_ref, segcol_ref, segrow_ref, xhat_ref,
    out_ref, three_ref, sums_ref, keys_ref, dk_ref, dv_ref, held_ref, sem_ref,
):
    fetch = pltpu.make_async_copy(xhat_ref, held_ref, sem_ref)
    fetch.start()
    blocks, size, _ = qkv_ref.shape
    for j in range(blocks):
        keys_ref[j] = turn(qkv_ref[j, :, 128:256])
    dk_ref[...] = jnp.zeros_like(dk_ref)
    dv_ref[...] = jnp.zeros_like(dv_ref)
    for i in range(blocks):
        query = (qkv_ref[i, :, 0:128].astype(wide) * HEAD_DIM**-0.5).astype(narrow)
        query_t = turn(query)
        grad = grad_ref[i]
        grad_t = turn(grad)
        inner = grad_t.astype(wide) * full_ref[i]
        queries_t = [head_rows(query_t, head) for head in range(2)]
        grads_t = [head_rows(grad_t, head) for head in range(2)]
        inners = [
            jnp.sum(inner[head * 64 : head * 64 + 64], 0, keepdims=True) for head in range(2)
        ]
        lses = [lse_ref[i, head : head + 1, :] for head in range(2)]
        query_pair = jnp.concatenate([head_lanes(query, head) for head in range(2)], 0)
        grad_pair = jnp.concatenate([head_lanes(grad, head) for head in range(2)], 0)

        def step(j, carry, diagonal):
            keys = qkv_ref[j, :, 128:256]
            vals = qkv_ref[j, :, 256:384]
            mask = mask_of(segcol_ref, segrow_ref, i, j, diagonal)
            lows, score_lows, out = [], [], []
            for head in range(2):
                scores = matmul(keys, queries_t[head])
                probs = jnp.where(mask, jnp.exp(scores - lses[head]), 0.0)
                prob_grad = matmul(vals, grads_t[head])
                score_low = (probs * (prob_grad - inners[head])).astype(narrow)
                lows.append(probs.astype(narrow))
                score_lows.append(score_low)
                part = matmul(keys_ref[j, head * 64 : head * 64 + 64, :], score_low)
                out.append(part if carry is None else carry[head] + part)
            dv_ref[j] += matmul(jnp.concatenate(lows, 1), grad_pair)
            dk_ref[j] += matmul(jnp.concatenate(score_lows, 1), query_pair)
            return tuple(out)

        carry = step(i, None, True)
        if i > 0:
            carry = lax.fori_loop(low_ref[i], i, lambda j, c: step(j, c, False), carry)
        dq = jnp.concatenate(carry, 0) * HEAD_DIM**-0.5
        out_ref[i, :, 0:128] = jnp.transpose(dq, (1, 0)).astype(narrow)
    for j in range(blocks):
        out_ref[j, :, 128:256] = dk_ref[j].astype(narrow)
        out_ref[j, :, 256:384] = dv_ref[j].astype(narrow)
    fetch.wait()
    for part in range(4):
        height = slice(part * 256, part * 256 + 256)
        three = sum(matmul(held_ref[j, height, :], out_ref[j]) for j in range(blocks))
        for d in range(4):
            for i in range(3):
                three_ref[part * 4 + d, i * 64 : i * 64 + 64, :] = three[
                    d * 64 : d * 64 + 64, i * 128 : i * 128 + 128
                ].astype(narrow)
    sums_ref[...] = sum(jnp.sum(out_ref[j].astype(wide), 0, keepdims=True) for j in range(blocks))


def attend_back(low, qkv, grad, full, lse, segcol, segrow, xhat):
    blocks, size, _ = qkv.shape
    vmem = pl.BlockSpec(memory_space=pltpu.VMEM)
    return pl.pallas_call(
        attend_back_kernel,
        out_shape=(
            jax.ShapeDtypeStruct((blocks, size, 384), narrow),
            jax.ShapeDtypeStruct((16, 192, 128), narrow),
            jax.ShapeDtypeStruct((1, 384), wide),
        ),
        in_specs=[pl.BlockSpec(memory_space=pltpu.SMEM)]
        + [vmem] * 6
        + [pl.BlockSpec(memory_space=pltpu.HBM)],
        out_specs=(vmem, vmem, vmem),
        scratch_shapes=[
            pltpu.VMEM((blocks, 128, size), narrow),
            pltpu.VMEM((blocks, size, 128), wide),
            pltpu.VMEM((blocks, size, 128), wide),
            pltpu.VMEM(xhat.shape, narrow),
            pltpu.SemaphoreType.DMA,
        ],
        compiler_params=pltpu.CompilerParams(vmem_limit_bytes=20 << 20),
        name="attend_back",
    )(low, qkv, grad, full, lse, segcol, segrow, xhat)


def unpack_kernel(
    all_ref, bias_ref, gain_ref, shift_ref, query_ref, key_ref, value_ref,
    dquery_ref, dkey_ref, dvalue_ref, dout_ref, vector_ref,
):
    mats = ((query_ref, dquery_ref), (key_ref, dkey_ref), (value_ref, dvalue_ref))
    for d in range(all_ref.shape[0]):
        height = slice(d * 64, d * 64 + 64)
        gain, shift = gain_ref[d].astype(wide), shift_ref[d].astype(wide)
        gain_sum = shift_sum = jnp.zeros((64, 128), wide)
        for e in range(8):
            lanes = slice(e * 128, e * 128 + 128)
            for i, (mat_ref, grad_ref) in enumerate(mats):
                part = all_ref[d, e, i * 64 : i * 64 + 64, :].astype(wide)
                bias = bias_ref[i : i + 1, lanes]
                mat = mat_ref[height, lanes].astype(wide)
                grad_ref[height, lanes] = gain * part + shift * bias
                gain_sum = gain_sum + mat * part
                shift_sum = shift_sum + mat * bias
            for i in range(8):
                dout_ref[e, d, :, i * 128 : i * 128 + 128] = all_ref[
                    d, e, 192 + i * 8 : 200 + i * 8, :
                ].astype(wide)
        vector_ref[d, :, 0:1] = jnp.sum(gain_sum, 1, keepdims=True)
        vector_ref[d, :, 1:2] = jnp.sum(shift_sum, 1, keepdims=True)


def unpack(everything, biases, gain, shift, querymat, keymat, valuemat, step=2):
    width = querymat.shape[0]
    column = pl.BlockSpec((step, 64, 1), lambda d: (d, 0, 0))
    strip = pl.BlockSpec((step * 64, width), lambda d: (d, 0))
    square = jax.ShapeDtypeStruct((width, width), wide)
    return pl.pallas_call(
        unpack_kernel,
        grid=(16 // step,),
        out_shape=(
            square, square, square,
            jax.ShapeDtypeStruct((8, 16, 8, width), wide),
            jax.ShapeDtypeStruct((16, 64, 2), wide),
        ),
        in_specs=[
            pl.BlockSpec((step, 8, 264, 128), lambda d: (d, 0, 0, 0)),
            pl.BlockSpec((3, width), lambda d: (0, 0)),
            column, column, strip, strip, strip,
        ],
        out_specs=(
            strip, strip, strip,
            pl.BlockSpec((8, step, 8, width), lambda d: (0, d, 0, 0)),
            pl.BlockSpec((step, 64, 2), lambda d: (d, 0, 0)),
        ),
        compiler_params=pltpu.CompilerParams(vmem_limit_bytes=14 << 20),
        name="unpack",
    )(everything, biases, gain, shift, querymat, keymat, valuemat)


def per_device(
    tokens, cotangent, segments, routes,
    attngain, attnshift, querymat, querybias, keymat, valuemat, valuebias, outmat, outbias,
    frontgain, frontshift, frontexpand, frontlift, frontreduce, frontoffset,
    backgain, backshift, backexpand, backlift, backreduce, backoffset, centroid,
):
    rows, width = tokens.shape
    experts = 8
    capacity = rows // experts + rows // (2 * experts)
    slots = experts * capacity
    mine = lax.axis_index(GROUP)
    y1_at, y2_at, y_at = (lax.axis_index(axis) for axis in ("y1", "y2", COLUMN))

    plans = to_everyone(jnp.concatenate([segments, routes], 0), GROUP, experts)
    small_own = jnp.concatenate(
        [
            frontgain[0], frontshift[0], frontoffset[0], backgain[0], backshift[0], backoffset[0],
            centroid[0], frontlift[0], backlift[0], jnp.zeros((64,), narrow),
        ]
    )
    small = small_own.reshape(8, 128)

    def reduced(matrix, axes):
        return lax.psum_scatter(matrix, axes, scatter_dimension=0, tiled=True)

    def gathered(matrix, axes):
        return lax.all_gather(matrix, axes, axis=0)

    front_own = jnp.concatenate([frontexpand[0].T, frontreduce[0]], 0)
    front_other = swap(front_own, "y1")
    front_mats = [gathered(front_own, "x")]

    route = routes[0]
    picks = (route[:, None] == jnp.arange(experts)[None, :]).astype(narrow)
    lower = (jnp.arange(rows)[:, None] > jnp.arange(rows)[None, :]).astype(narrow)
    rank = jnp.sum(matmul(lower, picks) * picks.astype(wide), 1).astype(jnp.int32)
    send_index = route * capacity + rank
    sender = (jnp.arange(slots)[:, None] == send_index[None, :]).astype(narrow)
    def pack(row_data):
        return matmul(sender, row_data).astype(narrow).reshape(experts, capacity, width)

    def unpack_rows(blocks):
        return matmul(taker, blocks.reshape(slots, width)).astype(narrow)

    def pack_back(row_data):
        return matmul_left(taker, row_data).astype(narrow).reshape(experts, capacity, width)

    def unpack_back(blocks):
        return matmul_left(sender, blocks.reshape(slots, width))

    line = lambda vector: vector.reshape(1, width)
    split, xhat_low = project(
        tokens, line(attngain), line(attnshift),
        querymat, line(querybias), keymat, valuemat, line(valuebias),
    )
    split, plans = lax.optimization_barrier((split, plans))
    seg_all, route_all = plans[:, 0], plans[:, 1]
    qkv = exchange(split, GROUP)
    xhat_turned = turned(xhat_low)
    qkv, xhat_turned = lax.optimization_barrier((qkv, xhat_turned))
    small = to_everyone(after(qkv, small), DATA, 16)
    counts = jnp.sum((route_all == mine).astype(jnp.int32), 1)
    ahead = jnp.arange(experts)[:, None] > jnp.arange(experts)[None, :]
    starts = jnp.sum(jnp.where(ahead, counts[None, :], 0), 1)
    place = jnp.arange(capacity)[None, :]
    spots = jnp.where(place < counts[:, None], starts[:, None] + place, -1).reshape(-1)
    taker = (jnp.arange(rows)[:, None] == spots[None, :]).astype(narrow)

    segcol, segrow = seg_all[:, :, None], seg_all[:, None, :]
    low = jnp.sum((seg_all[None, :, -1] < seg_all[:, None, 0]).astype(jnp.int32), 1)
    ctx, full, lse = attend(low, qkv, segcol, segrow)
    ctx, small, front_mats[0] = lax.optimization_barrier((ctx, small, front_mats[0]))
    front_other, back_own = after(ctx, front_other, jnp.concatenate([backexpand[0].T, backreduce[0]], 0))
    front_mats.append(gathered(front_other, "x"))
    back_mats = gathered(back_own, "x")
    small = small.reshape(16, 1024).astype(wide)
    front_gain, front_shift, front_offset, back_gain, back_shift, back_offset, centre = (
        small[:, i * 64 : i * 64 + 64].reshape(1, width) for i in range(7)
    )
    lifts = small[:, 448:960].reshape(4, 2, 2, 512)
    front_lift = lax.dynamic_index_in_dim(lifts, y2_at, 2, False)[:, :, :256]
    front_lift = jnp.where(y1_at == 0, front_lift, front_lift[:, ::-1])
    front_lift = jnp.transpose(front_lift, (1, 0, 2)).reshape(2, 1, 1024)
    back_lift = lax.dynamic_index_in_dim(lifts.reshape(4, 4, 512), y_at, 1, False)[:, 256:]
    back_lift = back_lift.reshape(1, 1024)
    hidden, blocks, context = join(exchange(ctx, GROUP), outmat, tokens, line(outbias), sender)

    blocks = exchange(blocks.reshape(experts, capacity, width), GROUP)
    stream = unpack_rows(blocks).astype(wide)
    front_xhat, front_inverse = norm_parts(stream)
    xhat_own = front_xhat.astype(narrow)
    ct_blocks = exchange(pack(after(xhat_own, cotangent)), GROUP)
    front_side = front_gain, front_shift, front_lift, [pinned(mats) for mats in front_mats]
    *own_acts, own_slope_a, own_slope_b, front_normed, own_part = front_forward(
        xhat_own, *front_side, wide
    )
    ct_blocks, own_part = lax.optimization_barrier((ct_blocks, own_part))
    gate = jax.nn.sigmoid(jnp.sum(stream * centre, -1, keepdims=True))
    ct_rows = unpack_rows(ct_blocks).astype(wide)
    gated = gate * ct_rows
    back_branch = gated.astype(narrow)
    xhat_got, back_branch, own_part = lax.optimization_barrier(
        (swap(xhat_own, "y2"), back_branch, own_part)
    )
    back_branches = share_four(back_branch)
    *got_acts, got_slope_a, got_slope_b, normed_got, got_part = front_forward(
        xhat_got, *front_side, narrow
    )
    got_part, back_branches[1], back_branches[3] = lax.optimization_barrier(
        (got_part, back_branches[1], back_branches[3])
    )
    front_got, back_branches[2] = lax.optimization_barrier((swap(got_part, "y2"), back_branches[2]))
    front_out = own_part + front_got.astype(wide) + front_offset
    xhat_all = lax.all_gather(after(got_part, xhat_turned), GROUP, axis=0)
    middle = stream + front_out
    back_xhat, back_inverse = norm_parts(middle)
    back_normed = share_four((back_xhat * back_gain + back_shift).astype(narrow))
    own_results = list(back_both(back_normed[0], back_branches[0], back_lift, back_mats, wide))
    own_results[2], *back_normed[1:] = lax.optimization_barrier((own_results[2], *back_normed[1:]))
    back_results = [own_results] + [
        back_both(normed, branch, back_lift, back_mats, narrow)
        for normed, branch in zip(back_normed[1:], back_branches[1:])
    ]
    back_acts, back_pre_grads, back_parts, out_parts, dots = map(list, zip(*back_results))
    back_late = after(back_parts[-1], *back_acts, *back_pre_grads)
    back_mat_part, back_lifts = mat_grads([back_late[:4], back_late[4:]], back_branches, back_normed)
    *back_got, back_mat_part, xhat_all = lax.optimization_barrier(
        (*return_four(back_parts), back_mat_part, xhat_all)
    )
    back_grads = reduced(back_mat_part, "x")
    back_norm_grad = total(back_parts[0], back_got)
    middle_grad = norm_back(back_norm_grad * back_gain, back_xhat, back_inverse)
    front_branch = (gated + middle_grad).astype(narrow)
    *own_pre_grads, own_part = front_backward(
        front_branch, (own_slope_a, own_slope_b), front_side[-1], wide
    )
    branch_got, own_part, *dots_got = lax.optimization_barrier(
        (swap(front_branch, "y2"), own_part, *return_four(dots))
    )
    *got_pre_grads, got_part = front_backward(
        branch_got, (got_slope_a, got_slope_b), front_side[-1], narrow
    )
    late = after(got_part, *own_acts, *got_acts)
    front_shrink_part, _ = mat_grads(list(zip(late[:2], late[2:])), (front_branch, branch_got))
    front_got, front_shrink_part = lax.optimization_barrier((swap(got_part, "y2"), front_shrink_part))
    front_shrink_part = reduced(front_shrink_part, "x")
    front_norm_grad = own_part + front_got.astype(wide)
    first_grad = norm_back(front_norm_grad * front_gain, front_xhat, front_inverse)
    gated_dot = jnp.sum(gated * (front_out + back_offset), -1, keepdims=True)
    logit_grad = (gated_dot + total(dots[0], dots_got)[:, :1]) * (1.0 - gate)
    sent_grad = (logit_grad * centre + middle_grad + first_grad).astype(narrow)

    sent_blocks = pack_back(sent_grad)
    pre_late = after(sent_blocks, *own_pre_grads, *got_pre_grads)
    front_expand_part, front_lifts = mat_grads(
        list(zip(pre_late[:2], pre_late[2:])), (front_normed, normed_got)
    )
    sent_blocks, front_expand_part, back_grads = lax.optimization_barrier(
        (exchange(sent_blocks, GROUP), front_expand_part, back_grads)
    )
    front_expand_part = reduced(front_expand_part, "x")
    getter = (send_index[:, None] == jnp.arange(slots)[None, :]).astype(narrow)
    hidden_grad, context_grad, out_low = hidden_back(
        sent_blocks.reshape(slots, width), getter, cotangent, outmat
    )
    grads = exchange(context_grad, GROUP)
    expert_sums = row_sums(
        *after(
            context_grad, front_norm_grad, front_xhat, front_branch, back_norm_grad, back_xhat,
            back_branches[0], logit_grad, stream,
        )
    )[:7].reshape(7, 16, 64)
    context, out_late = after(context_grad, context, out_low)
    out_part = matmul_left(context, out_late).astype(narrow).reshape(experts, 128, width)
    grads, out_part, expert_sums, *out_got = lax.optimization_barrier(
        (grads, out_part, expert_sums, *return_four(after(sent_blocks, *out_parts)))
    )
    branches = front_out + total(out_parts[0], out_got) + back_offset
    out_part = exchange(out_part, GROUP)

    dqkv, three, sums = attend_back(low, qkv, grads, full, lse, segcol, segrow, xhat_all)

    out_part = jnp.sum(after(sums, out_part).astype(wide), 0).astype(narrow).reshape(16, 8, 8, 128)
    biases = jnp.concatenate(
        [
            sums.reshape(16, 24),
            jnp.sum(out_low.astype(wide), 0).reshape(16, 64),
        ],
        1,
    ).astype(narrow)
    front_lifts, back_lifts = front_lifts[:, :, 0], back_lifts[:, 1, 0]
    front_lifts = jnp.where(y1_at == 0, front_lifts, front_lifts[:, ::-1])
    front_lifts = jnp.where(jnp.arange(2)[:, None] == y2_at, front_lifts[:, :, None], 0.0)
    back_lifts = jnp.where(jnp.arange(4)[:, None] == y_at, back_lifts[:, None], 0.0)
    packed = jnp.concatenate(
        [
            jnp.transpose(expert_sums, (1, 0, 2)).reshape(16, 448),
            front_lifts.reshape(16, 256),
            back_lifts.reshape(16, 256),
            jnp.zeros((16, 64), wide),
        ],
        1,
    )
    slices = jnp.concatenate(
        [
            three,
            jnp.transpose(out_part, (0, 2, 1, 3)).reshape(16, 64, 128),
            jnp.pad(biases[:, None], ((0, 0), (0, 7), (0, 40))),
            packed.reshape(16, 8, 128).astype(narrow),
        ],
        1,
    )
    slices, front_shrink_part, front_expand_part = lax.optimization_barrier(
        (exchange(slices, DATA), front_shrink_part, front_expand_part)
    )
    slices = jnp.sum(slices.astype(wide), 0)
    summed = slices[264:].reshape(1, 1024)
    slices = slices[:264].astype(narrow)
    everything = lax.all_gather(slices, EVERY, axis=0).reshape(16, 8, 264, 128)
    biases = everything[:, :, 256, :88].astype(wide)
    outbias_grad = jnp.sum(biases[:, :, 24:], 1).reshape(width)
    biases = jnp.transpose(biases[:, :, :24], (1, 0, 2)).reshape(8, 3, 128)
    biases = jnp.transpose(biases, (1, 0, 2)).reshape(3, width)
    query_grad, key_grad, value_grad, outmat_grad, vectors = unpack(
        everything, biases, attngain.reshape(16, 64, 1), attnshift.reshape(16, 64, 1),
        querymat, keymat, valuemat,
    )
    outmat_grad = outmat_grad.reshape(width, width)
    attngain_grad, attnshift_grad = vectors[:, :, 0].reshape(width), vectors[:, :, 1].reshape(width)
    querybias_grad, _, valuebias_grad = biases

    dqkv, returned, front_shrink_part, front_expand_part = after(
        slices, dqkv, pack_back((gate * branches).astype(narrow)), front_shrink_part, front_expand_part
    )
    own, returned, front_swap, other = lax.optimization_barrier(
        (
            exchange(dqkv, GROUP),
            exchange(returned, GROUP),
            swap(front_shrink_part[0, 1], "y1"),
            swap(front_expand_part[0, 1], "y1"),
        )
    )
    own = jnp.transpose(own.reshape(experts, rows, 3, 128), (2, 1, 0, 3))
    dquery, dkey, dvalue = (own[i].reshape(rows, width) for i in range(3))
    attn_norm_grad = (
        matmul_right(dquery, querymat) + matmul_right(dkey, keymat) + matmul_right(dvalue, valuemat)
    )
    attn_xhat, attn_inverse = norm_parts(tokens.astype(wide))
    tokens_grad = hidden_grad + norm_back(
        attn_norm_grad * attngain.astype(wide), attn_xhat, attn_inverse
    )
    result = (hidden + unpack_back(returned)).astype(narrow)
    back_shrink_grad, back_expand_grad = (grad.astype(wide) for grad in back_grads[0])
    front_shrink_grad = front_shrink_part[0, 0].astype(wide) + front_swap.astype(wide)
    front_expand_grad = front_expand_part[0, 0].astype(wide) + other.astype(wide)
    back_shrink_grad, front_shrink_grad = back_shrink_grad[None], front_shrink_grad[None]
    back_expand_grad, front_expand_grad = back_expand_grad.T[None], front_expand_grad.T[None]
    (
        front_gain_grad, front_shift_grad, front_offset_grad,
        back_gain_grad, back_shift_grad, back_offset_grad, centroid_grad,
    ) = (summed[:, i * 64 : i * 64 + 64] for i in range(7))
    front_lift_grad, back_lift_grad = summed[:, 448:704], summed[:, 704:960]

    return (
        result, tokens_grad, attngain_grad, attnshift_grad,
        query_grad, querybias_grad, key_grad, value_grad, valuebias_grad, outmat_grad, outbias_grad,
        front_gain_grad, front_shift_grad, front_expand_grad, front_lift_grad,
        front_shrink_grad, front_offset_grad,
        back_gain_grad, back_shift_grad, back_expand_grad, back_lift_grad,
        back_shrink_grad, back_offset_grad, centroid_grad,
    )


def solution(mesh):
    grid = Mesh(mesh.devices.reshape(4, 2, 2, 4, 2), EVERY)
    rows, plan, full = P(EVERY, None), P(DATA, GROUP), P()
    vector, expand, shrink = P(GROUP, DATA), P(GROUP, None, DATA), P(GROUP, DATA, None)
    sublayer = (vector, vector, expand, vector, shrink, vector)
    return jax.shard_map(
        per_device,
        mesh=grid,
        in_specs=(rows, rows, plan, plan) + (full,) * 9 + sublayer * 2 + (vector,),
        out_specs=(rows, rows) + (full,) * 9 + sublayer * 2 + (vector,),
        check_vma=False,
    )
```
